128 devices in a mesh: gx: 8 (over y, core), gy: 16 (over z, x).
Axes of the slice: x: 4, y: 4, z: 4, core: 2. Of those that a mesh axis runs over, the one named last changes fastest.
Arguments:
- model_state: float32 [3, 8, 3072, 2048], P(None, None, 'gx', 'gy'), may hold values from -6 to 6
- obs_val: float32 [16384, 384], P(('gx', 'gy')), may hold values from -6 to 6
- obs_owner: int32 [16384, 1], P(('gx', 'gy')), may hold values from 0 to 15; in each aligned block of 128 rows (0 to 127, 128 to 255, ...) at most 16 rows name the same one
- obs_x: int32 [16384], P(('gx', 'gy')), may hold values from 0 to 3071
- obs_y: int32 [16384], P(('gx', 'gy')), may hold values from 0 to 127
- cressman: float32 [3072, 3072], P(None, 'gx'), as said below
- vertical: float32 [3, 8, 128], replicated, may hold values from -2 to 2
Outputs:
- new_state: float32 [3, 8, 3072, 2048], P(None, None, 'gx', 'gy')
The draws below stay inside these ranges and needn't reach their ends.
Inputs may be any that keep to these rules, and one draw needn't show every extreme that they name: `obs_owner`: among the rows of one device, at most 16 name one column; in every draw some device's rows name some column exactly 16 times. `cressman`: entries are positive.
All inputs are finite; a program needn't handle non-finite values.
Results may differ from the reference program's by a relative error of at most 0.0001.
Values sent between devices are 32-bit elements; how exact they have to be, the bound alone decides.
A program may use at most 128 MiB of HBM per device.

```python
import math
import jax
import jax.numpy as jnp
import numpy as np
from jax import lax

CX = 384
CY = 128
NZ = 8
OBS_LEV = 128
REC_DEV = 128
CAPY = 16
NX = 3072
NY = 2048
RECS = 16384
N_GY = 16


def draw_cressman(key, part):
    rows = jnp.arange(NX, dtype=jnp.float32)[:, None]
    cols = jnp.arange(NX, dtype=jnp.float32)[None, :]
    base = jnp.exp(-jnp.abs(rows - cols) / (2.0 * CX))
    rough = jax.random.uniform(key, (NX, NX), jnp.float32, 0.5, 1.5)
    return (base * rough).astype(jnp.float32)


def with_ends(result, key, least, top_value):
    longest = result.shape.index(max(result.shape))
    spots = []
    for shift in (0, 1):
        where = [jax.random.randint(jax.random.fold_in(key, axis), (), 0, length) for axis, length in enumerate(result.shape)]
        where[longest] = (where[longest] + shift) % result.shape[longest]
        spots.append(tuple(where))
    return result.at[spots[0]].set(least).at[spots[1]].set(top_value)


def level_of(stream_key, dims, shards, least, largest):
    factor_of, own = 1.0, jax.random.fold_in(stream_key, 6)
    for dim, shards_of in shards:
        steps = jnp.exp(jax.random.uniform(jax.random.fold_in(own, dim), (shards_of,), jnp.float32, least / len(shards), largest / len(shards)))
        factor_of = factor_of * jnp.repeat(steps, dims[dim] // shards_of).reshape([-1 if axis == dim else 1 for axis in range(len(dims))])
    return factor_of


def shared_out(key, own, number, rows, count, top, reach, lean):
    sequence = jax.random.permutation(key, count)
    crowded, ordinary = load_shares(count, rows * top, reach, lean, True), load_shares(count, rows * top, reach, lean, False)
    places = jnp.arange(count)

    def named(lengths, offset_by):
        used = int((lengths > 0).sum())
        fixed = max(1, used // 4)
        shifted = fixed + (places - fixed + offset_by * (used - fixed)) % max(1, count - fixed)
        return jnp.zeros((count,), jnp.int32).at[sequence[jnp.where(places < fixed, places, shifted)]].set(jnp.asarray(lengths, jnp.int32))

    lengths = jnp.where(number % 4 == 0, named(crowded, number // 4), named(ordinary, number - number // 4 - 1))
    mixed = jax.random.permutation(jax.random.fold_in(own, 3), count)
    source_of, sink = mixed[0:count // 2 * 2:2], mixed[1:count // 2 * 2:2]
    room = jnp.minimum(lengths[source_of] - 1, reach - lengths[sink]) // 2
    room = jnp.where((source_of == sequence[0]) | (sink == sequence[0]) | (lengths[sink] == 0), 0, jnp.maximum(room, 0))
    shifted = jax.random.randint(jax.random.fold_in(own, 4), (count // 2,), 0, 1 << 20) % (room + 1)
    lengths = lengths.at[source_of].add(-shifted).at[sink].add(shifted)
    members = jnp.searchsorted(jnp.cumsum(lengths), jnp.arange(rows * top), side="right").astype(jnp.int32)
    listing = members.reshape(top, rows).T
    listing = listing[jax.random.permutation(jax.random.fold_in(own, 1), rows)]
    offset_by = jax.random.randint(jax.random.fold_in(own, 2), (rows, 1), 0, top)
    return jnp.take_along_axis(listing, (jnp.arange(top)[None, :] + offset_by) % top, axis=1)


def load_shares(amount, total, most, slope, full):
    weights = [(1 << 20) // math.isqrt(rank ** slope) + 1 for rank in range(1, amount + 1)]
    largest = most if full else min(most, max(-(-total // amount), total * weights[0] // sum(weights)))
    least = 1 if total - largest >= amount - 1 else 0
    given, surplus = [largest] + [least] * (amount - 1), total - largest - least * (amount - 1)
    while surplus > 0:
        movable = [i for i in range(1, amount) if given[i] < largest] or [i for i in range(1, amount) if given[i] < most]
        mass, left = sum([weights[i] for i in movable]), surplus
        for i in movable:
            addition = min(most - given[i], max(1, left * weights[i] // mass), surplus)
            given[i] = given[i] + addition
            surplus = surplus - addition
    return np.array(given)


def noise(rng, shape, scale, limit, shards=(), kind=jnp.bfloat16):
    drawn = jax.random.normal(rng, shape, jnp.float32) * scale
    if len(shards) > 0:
        drawn = level_of(rng, shape, shards, -0.22, 0.18) * drawn
    return jnp.clip(drawn, min=-limit, max=limit).astype(kind)


def setup_inputs(seed: int = 0) -> dict:
    key_list = jax.random.split(jax.random.key(seed), 8)
    model_state = noise(key_list[0], (3, NZ, NX, NY), 1.0, 6.0, ((2, 8), (3, 16)), jnp.float32)
    obs_val = noise(key_list[1], (RECS, 3 * OBS_LEV), 1.0, 6.0, ((0, 128),), jnp.float32)
    obs_owner_keys = jax.random.split(jax.random.fold_in(key_list[2], 1), RECS // REC_DEV)
    obs_owner_turns = jax.random.permutation(jax.random.fold_in(key_list[2], 3), RECS // REC_DEV)
    obs_owner = jax.vmap(lambda own, number: shared_out(jax.random.fold_in(key_list[2], 2), own, number, REC_DEV, N_GY, 1, CAPY, 2))(obs_owner_keys, obs_owner_turns).reshape((RECS, 1))
    obs_x = with_ends(jax.random.randint(key_list[3], (RECS,), 0, NX), jax.random.fold_in(key_list[3], 1), 0, NX - 1).astype(jnp.int32)
    obs_y = with_ends(jax.random.randint(key_list[4], (RECS,), 0, CY), jax.random.fold_in(key_list[4], 1), 0, CY - 1).astype(jnp.int32)
    cressman = draw_cressman(jax.random.fold_in(key_list[7], 71), 0)
    vertical = noise(key_list[6], (3, NZ, OBS_LEV), NZ ** -0.5, 2.0, (), jnp.float32)
    return dict(model_state=model_state, obs_val=obs_val, obs_owner=obs_owner, obs_x=obs_x, obs_y=obs_y, cressman=cressman, vertical=vertical)


advect_coef = 0.5
diffuse_h = 0.2
diffuse_z = 0.1
time_step = 0.5
nudge_gain = 1.0
spread_gain = 0.125


def tendency(padded):
    center = padded[:, :, 1:-1, 1:-1]
    to_east = padded[:, :, 2:, 1:-1]
    to_west = padded[:, :, :-2, 1:-1]
    to_north = padded[:, :, 1:-1, 2:]
    to_south = padded[:, :, 1:-1, :-2]
    wind_u = center[0][None]
    wind_v = center[1][None]
    advection = -0.5 * advect_coef * (wind_u * (to_east - to_west) + wind_v * (to_north - to_south))
    laplace = to_east + to_west + to_north + to_south - 4.0 * center
    upper_cells = jnp.concatenate([center[:, 1:], center[:, -1:]], axis=1)
    lower_cells = jnp.concatenate([center[:, :1], center[:, :-1]], axis=1)
    return advection + diffuse_h * laplace + diffuse_z * (upper_cells + lower_cells - 2.0 * center)


def reference(model_state, obs_val, obs_owner, obs_x, obs_y, cressman, vertical):
    fields, levels, width_x, width_y = model_state.shape
    obs_levels = vertical.shape[2]
    records = obs_val.shape[0]
    block = math.gcd(records, 512)
    blocks = records // block
    columns = (obs_owner[:, 0] * CY + obs_y).astype(jnp.int32)
    highest = lax.Precision.HIGHEST

    def per_block(running, piece):
        numer, weights_sum = running
        x_cells, y_cells, values = piece
        weight = jnp.take(cressman, x_cells, axis=0)
        picked = jnp.take(model_state, y_cells, axis=3)
        colsum = jnp.einsum('vzxb,bx->bvz', picked, weight, precision=highest)
        total = jnp.sum(weight, axis=1)
        model_eq = jnp.einsum('bvz,vzl->bvl', colsum / total[:, None, None], vertical, precision=highest)
        innovation = values - model_eq
        spread = jnp.einsum('bvl,vzl->bvz', innovation, vertical, precision=highest) * spread_gain
        weighted = spread[:, :, :, None] * weight[:, None, None, :]
        numer = numer.at[y_cells].add(weighted)
        weights_sum = weights_sum.at[y_cells].add(weight)
        return (numer, weights_sum), None

    start = (jnp.zeros((width_y, fields, levels, width_x), jnp.float32), jnp.zeros((width_y, width_x), jnp.float32))
    pieces = (obs_x.reshape(blocks, block), columns.reshape(blocks, block), obs_val.reshape(blocks, block, fields, obs_levels))
    (numer, weights_sum), _ = lax.scan(per_block, start, pieces)
    nudge = jnp.transpose(numer, (1, 2, 3, 0)) / jnp.maximum(jnp.transpose(weights_sum), 1.0)[None, None]
    padded = jnp.pad(model_state, ((0, 0), (0, 0), (1, 1), (1, 1)))
    return model_state + time_step * (tendency(padded) + nudge_gain * nudge)
```

```python
import functools

import jax
import jax.numpy as jnp
from jax import lax
from jax.experimental import pallas as pl
from jax.experimental.pallas import tpu as pltpu
from jax.sharding import PartitionSpec as P

F32 = jnp.float32
BF16 = jnp.bfloat16
I32 = jnp.int32
HIGHEST = lax.Precision.HIGHEST
MESH = pl.DeviceIdType.MESH

advect_coef = 0.5
diffuse_h = 0.2
diffuse_z = 0.1
time_step = 0.5
nudge_gain = 1.0
spread_gain = 0.125

FEATURES = 32
GROUPS = 8
BLOCK = 128


def iota(shape, dim):
    return lax.broadcasted_iota(I32, shape, dim)


def dot(a, b, precision=None):
    return lax.dot_general(
        a, b, (((1,), (0,)), ((), ())), precision=precision, preferred_element_type=F32
    )


def dot_t(a, b, precision=None):
    return lax.dot_general(
        a, b, (((1,), (1,)), ((), ())), precision=precision, preferred_element_type=F32
    )


def split(value):
    high = value.astype(BF16)
    return high, (value - high.astype(F32)).astype(BF16)


def regroup(parts):
    lane_block = iota(parts[0].shape, 1) // 16
    for bit in (1, 2, 4):
        upper = (lane_block & bit) != 0
        out = list(parts)
        for a in range(8):
            if a & bit:
                continue
            low, high = parts[a], parts[a | bit]
            out[a] = jnp.where(upper, pltpu.roll(high, 16 * bit, 1), low)
            out[a | bit] = jnp.where(upper, high, pltpu.roll(low, 128 - 16 * bit, 1))
        parts = out
    return parts


def dispatch_kernel(
    nx, ny, obs_ref, owner_ref, x_ref, y_ref, vert_ref, state_ref,
    at_ref, xi_ref, yi_ref, pos_ref, cnt_ref, nb_ref, base_ref, xh_ref, yh_ref,
    plane, sb, rb, mb, rows, xe, ye, xr, yr,
    load_sem, s1_send, s1_recv, s2_send, s2_recv, h_send, h_recv,
):
    i, j = lax.axis_index("gx"), lax.axis_index("gy")
    load = pltpu.make_async_copy(state_ref, plane, load_sem)
    load.start()
    barrier = pltpu.get_barrier_semaphore()
    for d in range(1, ny):
        pl.semaphore_signal(
            barrier, inc=1, device_id=(i, lax.rem(j + d, ny)), device_id_type=MESH
        )
    for d in range(1, nx):
        pl.semaphore_signal(
            barrier, inc=1, device_id=(lax.rem(i + d, nx), j), device_id_type=MESH
        )

    recs = obs_ref.shape[0]
    planes, tile_x, lanes = plane.shape
    slots = sb.shape[0]
    cap = slots // ny
    vert = vert_ref[...]
    var = iota((planes, lanes), 0) // 8
    basis = jnp.concatenate([jnp.where(var == v, vert, 0.0) for v in range(3)], axis=1)
    basis = jnp.concatenate([basis, jnp.zeros((lanes - planes, 3 * lanes), F32)], axis=0)
    payload = dot_t(obs_ref[...], basis, HIGHEST)
    eye = iota((recs, recs), 0) == iota((recs, recs), 1)
    x_col = jnp.sum(jnp.where(eye, x_ref[...].astype(F32), 0.0), axis=1, keepdims=True)
    y_col = jnp.sum(jnp.where(eye, y_ref[...].astype(F32), 0.0), axis=1, keepdims=True)
    lane = iota((recs, lanes), 1)
    payload = jnp.where(lane == 24, x_col, payload)
    payload = jnp.where(lane == 25, y_col, payload)
    payload = jnp.where(lane == 26, 1.0, payload)
    owner = owner_ref[...]
    onehot = jnp.where(owner == lane, 1.0, 0.0)
    earlier = jnp.where(iota((recs, recs), 0) > iota((recs, recs), 1), 1.0, 0.0)
    rank = jnp.sum(dot(earlier, onehot) * onehot, axis=1, keepdims=True)
    slot = owner.astype(F32) * cap + rank
    slot_row = jnp.sum(jnp.where(eye, slot, 0.0), axis=0, keepdims=True).astype(I32)
    place = jnp.where(iota((slots, recs), 0) == slot_row, 1.0, 0.0)
    sb[...] = dot(place, payload, HIGHEST)

    pl.semaphore_wait(barrier, nx + ny - 2)
    first = []
    for d in range(1, ny):
        c = lax.rem(j + d, ny)
        copy = pltpu.make_async_remote_copy(
            src_ref=sb.at[pl.ds(pl.multiple_of(c * cap, cap), cap)],
            dst_ref=rb.at[pl.ds(pl.multiple_of(j * cap, cap), cap)],
            send_sem=s1_send.at[d], recv_sem=s1_recv.at[d],
            device_id=(i, c), device_id_type=MESH,
        )
        copy.start()
        first.append(copy)
    own = pl.ds(pl.multiple_of(j * cap, cap), cap)
    rb[own, :] = sb[own, :]

    load.wait()
    for k in range(planes):
        xe[0, k : k + 1, :] = plane[k, tile_x - 1 : tile_x, :]
        xe[1, k : k + 1, :] = plane[k, 0:1, :]
    edge_lane = iota((tile_x, lanes), 1)

    def gather_edges(k, edges):
        turned = pltpu.roll(plane[k], 2 * k + 1, 1)
        return jnp.where(edge_lane // 2 == k, turned, edges)

    edges = lax.fori_loop(0, planes, gather_edges, jnp.zeros((tile_x, lanes), F32))
    ye[...] = edges.T[: 2 * planes]
    halo = []
    for n, (src, dst, to) in enumerate((
        (xe.at[0], xr.at[0], (lax.rem(i + 1, nx), j)),
        (xe.at[1], xr.at[1], (lax.rem(i + nx - 1, nx), j)),
        (ye, yr.at[0], (i, lax.rem(j + 1, ny))),
        (ye, yr.at[1], (i, lax.rem(j + ny - 1, ny))),
    )):
        copy = pltpu.make_async_remote_copy(
            src_ref=src, dst_ref=dst, send_sem=h_send.at[n], recv_sem=h_recv.at[n],
            device_id=to, device_id_type=MESH,
        )
        copy.start()
        halo.append(copy)

    for copy in first:
        copy.wait()
    got = rb[...]
    got_t = got.T[:FEATURES]
    valid = got[:, 26:27]
    before = jnp.where(iota((slots, slots), 0) > iota((slots, slots), 1), 1.0, 0.0)
    rank = dot(before, jnp.broadcast_to(valid, (slots, lanes)))[:, 0:1]
    place = jnp.where(
        (iota((slots, slots), 1) == rank.astype(I32)) & (valid > 0.5), 1.0, 0.0
    )
    compact = dot(got_t, place, HIGHEST)
    at_ref[...] = compact
    mb[i] = compact[24:32]
    second = []
    for d in range(1, nx):
        copy = pltpu.make_async_remote_copy(
            src_ref=mb.at[i], dst_ref=mb.at[i],
            send_sem=s2_send.at[d], recv_sem=s2_recv.at[d],
            device_id=(lax.rem(i + d, nx), j), device_id_type=MESH,
        )
        copy.start()
        second.append(copy)
    for copy in halo:
        copy.wait()
    xh_ref[0] = jnp.where(i > 0, xr[0], 0.0)
    xh_ref[1] = jnp.where(i < nx - 1, xr[1], 0.0)
    even = iota((2 * planes, tile_x), 0) % 2 == 0
    south = jnp.where(j > 0, yr[0], 0.0)
    north = jnp.where(j < ny - 1, yr[1], 0.0)
    yh_ref[...] = jnp.where(even, south, north)
    for copy in second:
        copy.wait()

    for k in range(nx):
        for f in range(3):
            rows[f, k : k + 1, :] = mb[k, f : f + 1, :]
    y_cells = rows[1].astype(I32)
    valid = rows[2] > 0.5
    group = jnp.where(valid, y_cells // (lanes // GROUPS), GROUPS)
    masks = jnp.concatenate(
        [jnp.where(group == g, 1.0, 0.0) for g in range(GROUPS)], axis=0
    )
    lines = GROUPS * nx
    after = jnp.where(iota((slots, slots), 0) < iota((slots, slots), 1), 1.0, 0.0)
    rank = dot(masks, after)
    total = jnp.broadcast_to(jnp.sum(masks, axis=1, keepdims=True), (lines, lanes))
    line, other = iota((lines, lines), 0), iota((lines, lines), 1)
    same = line // nx == other // nx
    offset = dot(jnp.where(same & (other < line), 1.0, 0.0), total, HIGHEST)
    whole = dot(jnp.where(same, 1.0, 0.0), total, HIGHEST)
    count = (whole.astype(I32) + (BLOCK - 1)) // BLOCK
    base = dot(
        jnp.where((other // nx < line // nx) & (other % nx == 0), 1.0, 0.0),
        count.astype(F32),
        HIGHEST,
    )
    placed = masks * (base[:, 0:1] * BLOCK + offset[:, 0:1] + rank)
    pos = placed[0:nx]
    for g in range(1, GROUPS):
        pos = pos + placed[g * nx : (g + 1) * nx]
    dump = (slots * nx // BLOCK + GROUPS) * BLOCK
    pos_ref[...] = jnp.where(valid, pos.astype(I32), dump)
    xi_ref[...] = rows[0].astype(I32)
    yi_ref[...] = y_cells % (lanes // GROUPS)
    cnt_ref[...] = jnp.broadcast_to(
        jnp.sum(rows[2], axis=1, keepdims=True), (nx, lanes)
    ).astype(I32)
    nb_ref[...] = count
    base_ref[...] = base.astype(I32)


def gather_kernel(
    nx, xi, yi, pos, cnt, nb, base, cress_hbm, state_hbm,
    part_ref, wt_hi_ref, wt_lo_ref,
    cress, plane, sorted_w, sorted_y, st_hi, st_lo, sums, by_slot, sem,
):
    slots = xi.shape[1]
    planes, tile_x, lanes = plane.shape
    load_w = pltpu.make_async_copy(cress_hbm, cress, sem.at[0])
    load_s = pltpu.make_async_copy(state_hbm, plane, sem.at[1])
    load_w.start()
    load_s.start()
    for g in range(GROUPS):
        blocks = nb[g * nx, 0]

        @pl.when(blocks > 0)
        def _():
            start = pl.multiple_of((base[g * nx, 0] + blocks - 1) * BLOCK, BLOCK)
            sorted_w[pl.ds(start, BLOCK), :] = jnp.zeros((BLOCK, tile_x), F32)
            sorted_y[pl.ds(start, BLOCK), :] = jnp.full((BLOCK, lanes), -1, I32)

    load_w.wait()
    for k in range(nx):

        def bring(n, carry):
            for m in range(8):
                s = n * 8 + m
                p = pos[k, s]
                sorted_w[pl.ds(p, 1), :] = cress[pl.ds(xi[k, s], 1), :]
                sorted_y[pl.ds(p, 1), :] = jnp.full((1, lanes), yi[k, s], I32)
            return carry

        lax.fori_loop(0, (cnt[k, 0] + 7) // 8, bring, 0)

    load_s.wait()
    chunk = 32

    def regroup_chunk(n, carry):
        where = pl.ds(pl.multiple_of(n * chunk, chunk), chunk)
        for v in range(3):
            parts = regroup([plane[v * 8 + z, where, :] for z in range(8)])
            for g in range(GROUPS):
                high, low = split(parts[g])
                st_hi[g, where, v * lanes : (v + 1) * lanes] = high
                st_lo[g, where, v * lanes : (v + 1) * lanes] = low
        return carry

    lax.fori_loop(0, tile_x // chunk, regroup_chunk, 0)

    wide = 3 * lanes
    yy = iota((BLOCK, wide), 1) % 16
    fold = jnp.where(iota((wide, lanes), 0) // 16 == iota((wide, lanes), 1), 1.0, 0.0).astype(BF16)
    lane = iota((BLOCK, lanes), 1)

    def group_sums(g, carry):
        first = base[g * nx, 0]

        def block_sums(b, carry):
            where = pl.ds(pl.multiple_of((first + b) * BLOCK, BLOCK), BLOCK)
            w = sorted_w[where, :]
            high, low = split(w)
            s_hi, s_lo = st_hi[g], st_lo[g]
            products = dot(high, s_hi) + dot(high, s_lo) + dot(low, s_hi)
            y_here = sorted_y[where, :]
            y_wide = jnp.concatenate([y_here, y_here, y_here], axis=1)
            p_hi, p_lo = split(jnp.where(yy == y_wide, products, 0.0))
            colsum = dot(p_hi, fold) + dot(p_lo, fold)
            total = jnp.sum(w, axis=1, keepdims=True)
            sums[where, :] = jnp.where(lane == 24, total, colsum)
            t_hi, t_lo = split(w.T)
            wt_hi_ref[:, where] = t_hi
            wt_lo_ref[:, where] = t_lo
            return carry

        return lax.fori_loop(0, nb[g * nx, 0], block_sums, carry)

    lax.fori_loop(0, GROUPS, group_sums, 0)

    by_slot[...] = jnp.zeros(by_slot.shape, F32)
    for k in range(nx):

        def give(n, carry):
            for m in range(8):
                s = n * 8 + m
                by_slot[pl.ds(k * slots + s, 1), :] = sums[pl.ds(pos[k, s], 1), :]
            return carry

        lax.fori_loop(0, (cnt[k, 0] + 7) // 8, give, 0)
        part_ref[k] = by_slot[k * slots : (k + 1) * slots, :].T[:FEATURES]


def reduce_kernel(
    nx, part_ref, at_ref, vert_ref, out_ref, rs, ag, send1, recv1, send2, recv2
):
    i, j = lax.axis_index("gx"), lax.axis_index("gy")
    barrier = pltpu.get_barrier_semaphore()
    for d in range(1, nx):
        pl.semaphore_signal(
            barrier, inc=1, device_id=(lax.rem(i + d, nx), j), device_id_type=MESH
        )
    pl.semaphore_wait(barrier, nx - 1)
    copies = []
    for d in range(1, nx):
        k = lax.rem(i + d, nx)
        copy = pltpu.make_async_remote_copy(
            src_ref=part_ref.at[k], dst_ref=rs.at[i],
            send_sem=send1.at[d], recv_sem=recv1.at[d],
            device_id=(k, j), device_id_type=MESH,
        )
        copy.start()
        copies.append(copy)
    rs[i] = part_ref[i]
    lanes = vert_ref.shape[1]
    vert = jnp.concatenate([vert_ref[...], jnp.zeros((8, lanes), F32)], axis=0)
    same = iota((FEATURES, FEATURES), 0) // 8 == iota((FEATURES, FEATURES), 1) // 8
    gram = jnp.where(same, dot_t(vert, vert, HIGHEST), 0.0)
    at = at_ref[...]
    row = iota(at.shape, 0)
    for copy in copies:
        copy.wait()
    total = rs[0]
    for k in range(1, nx):
        total = total + rs[k]
    weight = total[24:25, :]
    mean = jnp.where(row < 24, total / jnp.where(weight > 0.0, weight, 1.0), 0.0)
    spread = spread_gain * (at - dot(gram, mean, HIGHEST))
    ag[i] = jnp.where(row < 24, spread, at)
    copies = []
    for d in range(1, nx):
        copy = pltpu.make_async_remote_copy(
            src_ref=ag.at[i], dst_ref=ag.at[i],
            send_sem=send2.at[d], recv_sem=recv2.at[d],
            device_id=(lax.rem(i + d, nx), j), device_id_type=MESH,
        )
        copy.start()
        copies.append(copy)
    for copy in copies:
        copy.wait()
    out_ref[...] = ag[...]


def update_kernel(
    nx, pos, cnt, nb, base, spread_ref, xh_ref, yh_ref, wt_hi_hbm, wt_lo_hbm, state_hbm,
    out_ref, plane, wt_hi, wt_lo, by_slot, sorted_s, halo, nudge, num, weights, sem,
):
    slots = spread_ref.shape[2]
    planes, padded_x, lanes = plane.shape
    tile_x = padded_x - 16
    load_s = pltpu.make_async_copy(state_hbm, plane.at[:, 8 : 8 + tile_x, :], sem.at[0])
    load_h = pltpu.make_async_copy(wt_hi_hbm, wt_hi, sem.at[1])
    load_l = pltpu.make_async_copy(wt_lo_hbm, wt_lo, sem.at[2])
    load_h.start()
    load_l.start()
    load_s.start()
    for g in range(GROUPS):
        blocks = nb[g * nx, 0]

        @pl.when(blocks > 0)
        def _():
            start = pl.multiple_of((base[g * nx, 0] + blocks - 1) * BLOCK, BLOCK)
            sorted_s[pl.ds(start, BLOCK), :] = jnp.full((BLOCK, lanes), -1.0, F32)

    pad = jnp.zeros((lanes - FEATURES, slots), F32)
    for k in range(nx):
        by_slot[k * slots : (k + 1) * slots, :] = jnp.concatenate(
            [spread_ref[k], pad], axis=0
        ).T

        def bring(n, carry):
            for m in range(8):
                s = n * 8 + m
                sorted_s[pl.ds(pos[k, s], 1), :] = by_slot[pl.ds(k * slots + s, 1), :]
            return carry

        lax.fori_loop(0, (cnt[k, 0] + 7) // 8, bring, 0)

    halo[...] = jnp.concatenate(
        [yh_ref[...], jnp.zeros((lanes - 2 * planes, tile_x), F32)], axis=0
    ).T

    wide = 3 * lanes
    yy = iota((BLOCK, wide), 1) % 16
    widen = jnp.where(iota((lanes, wide), 1) // 16 == iota((lanes, wide), 0), 1.0, 0.0).astype(BF16)
    load_h.wait()
    load_l.wait()

    def group_update(g, carry):
        first = base[g * nx, 0]
        num[...] = jnp.zeros(num.shape, F32)
        weights[...] = jnp.zeros(weights.shape, F32)

        def block_update(b, carry):
            where = pl.ds(pl.multiple_of((first + b) * BLOCK, BLOCK), BLOCK)
            value = sorted_s[where, :]
            y_here = (value[:, 25:26] + 0.5).astype(I32)
            match = (value[:, 25:26] > -0.5) & (yy == y_here % 16)
            high, low = split(value)
            s_hi = jnp.where(match, dot(high, widen), 0.0).astype(BF16)
            s_lo = jnp.where(match, dot(low, widen), 0.0).astype(BF16)
            ones = jnp.where(match[:, :lanes], 1.0, 0.0).astype(BF16)
            w_hi, w_lo = wt_hi[:, where], wt_lo[:, where]
            num[...] += dot(w_hi, s_hi) + dot(w_hi, s_lo) + dot(w_lo, s_hi)
            weights[...] += dot(w_hi, ones) + dot(w_lo, ones)
            return carry

        lax.fori_loop(0, nb[g * nx, 0], block_update, 0)
        scale = 1.0 / jnp.maximum(weights[...], 1.0)
        for v in range(3):
            nudge[g, :, v * lanes : (v + 1) * lanes] = num[:, v * lanes : (v + 1) * lanes] * scale
        return carry

    lax.fori_loop(0, GROUPS, group_update, 0)

    load_s.wait()
    for k in range(planes):
        plane[k, 7:8, :] = xh_ref[0, k : k + 1, :]
        plane[k, 8 + tile_x : 9 + tile_x, :] = xh_ref[1, k : k + 1, :]

    chunk = 16
    lane = iota((chunk, lanes), 1)

    def finish(n, carry):
        start = pl.multiple_of(n * chunk, chunk)
        edges = halo[pl.ds(start, chunk), :]
        centers = []
        for k in range(planes):
            centers.append(plane[k, pl.ds(pl.multiple_of(start + 8, 8), chunk), :])
        for v in range(3):
            gains = regroup(
                [nudge[g, pl.ds(start, chunk), v * lanes : (v + 1) * lanes] for g in range(GROUPS)]
            )
            for z in range(8):
                k = v * 8 + z
                center = centers[k]
                window = plane[k, pl.ds(start, chunk + 16), :]
                west = window[7 : 7 + chunk]
                east = window[9 : 9 + chunk]
                beside = pltpu.roll(edges, (lanes - 1 - 2 * k) % lanes, 1)
                south = pltpu.roll(jnp.where(lane == lanes - 1, beside, center), 1, 1)
                north = pltpu.roll(jnp.where(lane == 0, beside, center), lanes - 1, 1)
                upper = centers[v * 8 + min(z + 1, 7)]
                lower = centers[v * 8 + max(z - 1, 0)]
                wind_u, wind_v = centers[z], centers[8 + z]
                advection = (-0.5 * advect_coef) * (
                    wind_u * (east - west) + wind_v * (north - south)
                )
                laplace = east + west + north + south - 4.0 * center
                tendency = (
                    advection + diffuse_h * laplace + diffuse_z * (upper + lower - 2.0 * center)
                )
                out_ref[k, pl.ds(start, chunk), :] = center + time_step * (
                    tendency + nudge_gain * gains[z]
                )
        return carry

    lax.fori_loop(0, tile_x // chunk, finish, 0)


VM = pltpu.MemorySpace.VMEM


def vmem():
    return pl.BlockSpec(memory_space=VM)


def smem():
    return pl.BlockSpec(memory_space=pltpu.MemorySpace.SMEM)


def hbm():
    return pl.BlockSpec(memory_space=pl.ANY)


def local(nx, ny, model_state, obs_val, obs_owner, obs_x, obs_y, cressman, vertical):
    fields, levels, tile_x, lanes = model_state.shape
    planes = fields * levels
    recs = obs_val.shape[0]
    cap = max(2, 2 * recs // ny)
    slots = ny * cap
    rows = (slots * nx // BLOCK + GROUPS) * BLOCK
    state = model_state.reshape(planes, tile_x, lanes)
    vert = vertical.reshape(planes, vertical.shape[2])
    shape = jax.ShapeDtypeStruct
    dma = pltpu.SemaphoreType.DMA
    limit = 56 * 1024 * 1024

    at, xi, yi, pos, cnt, nb, base, xh, yh = pl.pallas_call(
        functools.partial(dispatch_kernel, nx, ny),
        out_shape=(
            shape((FEATURES, slots), F32),
            shape((nx, slots), I32),
            shape((nx, slots), I32),
            shape((nx, slots), I32),
            shape((nx, lanes), I32),
            shape((GROUPS * nx, lanes), I32),
            shape((GROUPS * nx, lanes), I32),
            shape((2, planes, lanes), F32),
            shape((2 * planes, tile_x), F32),
        ),
        in_specs=[vmem()] * 5 + [hbm()],
        out_specs=[vmem()] * 9,
        scratch_shapes=[
            pltpu.VMEM((planes, tile_x, lanes), F32),
            pltpu.VMEM((slots, lanes), F32),
            pltpu.VMEM((slots, lanes), F32),
            pltpu.VMEM((nx, 8, slots), F32),
            pltpu.VMEM((3, nx, slots), F32),
            pltpu.VMEM((2, planes, lanes), F32),
            pltpu.VMEM((2 * planes, tile_x), F32),
            pltpu.VMEM((2, planes, lanes), F32),
            pltpu.VMEM((2, 2 * planes, tile_x), F32),
            dma,
            dma((ny,)),
            dma((ny,)),
            dma((nx,)),
            dma((nx,)),
            dma((4,)),
            dma((4,)),
        ],
        compiler_params=pltpu.CompilerParams(
            collective_id=0, has_side_effects=True, vmem_limit_bytes=limit
        ),
        name="dispatch",
    )(obs_val, obs_owner, obs_x.reshape(1, recs), obs_y.reshape(1, recs), vert, state)

    part, wt_hi, wt_lo = pl.pallas_call(
        functools.partial(gather_kernel, nx),
        out_shape=(
            shape((nx, FEATURES, slots), F32),
            shape((tile_x, rows), BF16),
            shape((tile_x, rows), BF16),
        ),
        in_specs=[smem()] * 6 + [hbm()] * 2,
        out_specs=[vmem()] * 3,
        scratch_shapes=[
            pltpu.VMEM(cressman.shape, F32),
            pltpu.VMEM((planes, tile_x, lanes), F32),
            pltpu.VMEM((rows + 8, tile_x), F32),
            pltpu.VMEM((rows + 8, lanes), I32),
            pltpu.VMEM((GROUPS, tile_x, 3 * lanes), BF16),
            pltpu.VMEM((GROUPS, tile_x, 3 * lanes), BF16),
            pltpu.VMEM((rows + 8, lanes), F32),
            pltpu.VMEM((nx * slots, lanes), F32),
            dma((2,)),
        ],
        compiler_params=pltpu.CompilerParams(vmem_limit_bytes=limit),
        name="column_sums",
    )(xi, yi, pos, cnt, nb, base, cressman, state)

    spread = pl.pallas_call(
        functools.partial(reduce_kernel, nx),
        out_shape=shape((nx, FEATURES, slots), F32),
        in_specs=[vmem()] * 3,
        out_specs=vmem(),
        scratch_shapes=[
            pltpu.VMEM((nx, FEATURES, slots), F32),
            pltpu.VMEM((nx, FEATURES, slots), F32),
            dma((nx,)),
            dma((nx,)),
            dma((nx,)),
            dma((nx,)),
        ],
        compiler_params=pltpu.CompilerParams(
            collective_id=1, has_side_effects=True, vmem_limit_bytes=limit
        ),
        name="innovations",
    )(part, at, vert)

    out = pl.pallas_call(
        functools.partial(update_kernel, nx),
        out_shape=shape((planes, tile_x, lanes), F32),
        in_specs=[smem()] * 4 + [vmem()] * 3 + [hbm()] * 3,
        out_specs=vmem(),
        scratch_shapes=[
            pltpu.VMEM((planes, tile_x + 16, lanes), F32),
            pltpu.VMEM((tile_x, rows), BF16),
            pltpu.VMEM((tile_x, rows), BF16),
            pltpu.VMEM((nx * slots, lanes), F32),
            pltpu.VMEM((rows + 8, lanes), F32),
            pltpu.VMEM((tile_x, lanes), F32),
            pltpu.VMEM((GROUPS, tile_x, 3 * lanes), F32),
            pltpu.VMEM((tile_x, 3 * lanes), F32),
            pltpu.VMEM((tile_x, lanes), F32),
            dma((3,)),
        ],
        compiler_params=pltpu.CompilerParams(vmem_limit_bytes=limit),
        name="update",
    )(pos, cnt, nb, base, spread, xh, yh, wt_hi, wt_lo, state)
    return out.reshape(model_state.shape)


def solution(mesh):
    in_specs = (
        P(None, None, "gx", "gy"),
        P(("gx", "gy"), None),
        P(("gx", "gy"), None),
        P(("gx", "gy")),
        P(("gx", "gy")),
        P(None, "gx"),
        P(),
    )
    out_specs = P(None, None, "gx", "gy")
    return jax.shard_map(
        functools.partial(local, mesh.shape["gx"], mesh.shape["gy"]),
        mesh=mesh, in_specs=in_specs, out_specs=out_specs, check_vma=False,
    )
```

```python
import functools

import jax
import jax.numpy as jnp
from jax import lax
from jax.experimental import pallas as pl
from jax.experimental.pallas import tpu as pltpu
from jax.sharding import PartitionSpec as P

F32 = jnp.float32
BF16 = jnp.bfloat16
I32 = jnp.int32
HIGHEST = lax.Precision.HIGHEST
MESH = pl.DeviceIdType.MESH

advect_coef = 0.5
diffuse_h = 0.2
diffuse_z = 0.1
time_step = 0.5
nudge_gain = 1.0
spread_gain = 0.125

FEATURES = 32
GROUPS = 8
BLOCK = 128


def iota(shape, dim):
    return lax.broadcasted_iota(I32, shape, dim)


def dot(a, b, precision=None):
    return lax.dot_general(
        a, b, (((1,), (0,)), ((), ())), precision=precision, preferred_element_type=F32
    )


def dot_t(a, b, precision=None):
    return lax.dot_general(
        a, b, (((1,), (1,)), ((), ())), precision=precision, preferred_element_type=F32
    )


def split(value):
    high = value.astype(BF16)
    return high, (value - high.astype(F32)).astype(BF16)


def barrel(parts):
    block = iota(parts[0].shape, 1) // 16
    for bit in (1, 2, 4):
        upper = (block & bit) != 0
        parts = [jnp.where(upper, parts[(c + bit) % 8], parts[c]) for c in range(8)]
    return parts


def to_groups(parts):
    parts = barrel([pltpu.roll(p, 16 * z, 1) if z else p for z, p in enumerate(parts)])
    return [parts[-g % 8] for g in range(8)]


def to_levels(parts):
    parts = barrel(parts)
    return [
        pltpu.roll(parts[-z % 8], 128 - 16 * z, 1) if z else parts[0] for z in range(8)
    ]


def group_of(lane, g):
    return lane // 128 * 8 + (lane // 16 + 8 - g) % 8


def dispatch_kernel(
    nx, ny, obs_ref, owner_ref, x_ref, y_ref, vert_ref, state_hbm,
    at_ref, info_ref, meta_ref, base_hbm, high_hbm, low_hbm,
    plane, moved, st_hi, st_lo, sb, rb, mb, rows, xe, ye, xr, yr,
    load_sem, store_sem, s1_send, s1_recv, s2_send, s2_recv, h_send, h_recv,
):
    i, j = lax.axis_index("gx"), lax.axis_index("gy")
    planes, padded_x, lanes = plane.shape
    tile_x = padded_x - 16
    load = pltpu.make_async_copy(state_hbm, plane.at[:, 8 : 8 + tile_x, :], load_sem)
    load.start()
    barrier = pltpu.get_barrier_semaphore()
    for d in range(1, ny):
        pl.semaphore_signal(
            barrier, inc=1, device_id=(i, lax.rem(j + d, ny)), device_id_type=MESH
        )
    for d in range(1, nx):
        pl.semaphore_signal(
            barrier, inc=1, device_id=(lax.rem(i + d, nx), j), device_id_type=MESH
        )

    recs = obs_ref.shape[0]
    slots = sb.shape[0]
    cap = slots // ny
    vert = vert_ref[...]
    var = iota((planes, lanes), 0) // 8
    basis = jnp.concatenate([jnp.where(var == v, vert, 0.0) for v in range(3)], axis=1)
    basis = jnp.concatenate([basis, jnp.zeros((lanes - planes, 3 * lanes), F32)], axis=0)
    payload = dot_t(obs_ref[...], basis, HIGHEST)
    eye = iota((recs, recs), 0) == iota((recs, recs), 1)
    x_col = jnp.sum(jnp.where(eye, x_ref[...].astype(F32), 0.0), axis=1, keepdims=True)
    y_col = jnp.sum(jnp.where(eye, y_ref[...].astype(F32), 0.0), axis=1, keepdims=True)
    lane = iota((recs, lanes), 1)
    payload = jnp.where(lane == 24, x_col, payload)
    payload = jnp.where(lane == 25, y_col, payload)
    payload = jnp.where(lane == 26, 1.0, payload)
    owner = jnp.sum(jnp.where(eye, owner_ref[...], 0), axis=1, keepdims=True)
    onehot = jnp.where(owner == lane, 1.0, 0.0)
    earlier = jnp.where(iota((recs, recs), 0) > iota((recs, recs), 1), 1.0, 0.0)
    rank = jnp.sum(dot(earlier, onehot) * onehot, axis=1, keepdims=True)
    slot = owner.astype(F32) * cap + rank
    slot_row = jnp.sum(jnp.where(eye, slot, 0.0), axis=0, keepdims=True).astype(I32)
    place = jnp.where(iota((slots, recs), 0) == slot_row, 1.0, 0.0)
    sb[...] = dot(place, payload, HIGHEST)

    pl.semaphore_wait(barrier, nx + ny - 2)
    first = []
    for d in range(1, ny):
        c = lax.rem(j + d, ny)
        copy = pltpu.make_async_remote_copy(
            src_ref=sb.at[pl.ds(pl.multiple_of(c * cap, cap), cap)],
            dst_ref=rb.at[pl.ds(pl.multiple_of(j * cap, cap), cap)],
            send_sem=s1_send.at[d], recv_sem=s1_recv.at[d],
            device_id=(i, c), device_id_type=MESH,
        )
        copy.start()
        first.append(copy)
    own = pl.ds(pl.multiple_of(j * cap, cap), cap)
    rb[own, :] = sb[own, :]

    load.wait()
    for k in range(planes):
        xe[0, k : k + 1, :] = plane[k, 7 + tile_x : 8 + tile_x, :]
        xe[1, k : k + 1, :] = plane[k, 8:9, :]
    edge_lane = iota((tile_x, lanes), 1)

    def gather_edges(k, edges):
        turned = pltpu.roll(plane[k, 8 : 8 + tile_x, :], 2 * k + 1, 1)
        return jnp.where(edge_lane // 2 == k, turned, edges)

    edges = lax.fori_loop(0, planes, gather_edges, jnp.zeros((tile_x, lanes), F32))
    ye[...] = edges.T[: 2 * planes]
    halo = []
    for n, (src, dst, to) in enumerate((
        (xe.at[0], xr.at[0], (lax.rem(i + 1, nx), j)),
        (xe.at[1], xr.at[1], (lax.rem(i + nx - 1, nx), j)),
        (ye, yr.at[0], (i, lax.rem(j + 1, ny))),
        (ye, yr.at[1], (i, lax.rem(j + ny - 1, ny))),
    )):
        copy = pltpu.make_async_remote_copy(
            src_ref=src, dst_ref=dst, send_sem=h_send.at[n], recv_sem=h_recv.at[n],
            device_id=to, device_id_type=MESH,
        )
        copy.start()
        halo.append(copy)

    chunk = 32

    def group_chunk(n, carry):
        start = pl.multiple_of(n * chunk, chunk)
        here = pl.ds(start, chunk)
        for v in range(3):
            parts = to_groups(
                [plane[v * 8 + z, pl.ds(pl.multiple_of(start + 8, 8), chunk), :] for z in range(8)]
            )
            for g in range(GROUPS):
                high, low = split(parts[g])
                st_hi[g, here, v * lanes : (v + 1) * lanes] = high
                st_lo[g, here, v * lanes : (v + 1) * lanes] = low
        return carry

    lax.fori_loop(0, tile_x // chunk, group_chunk, 0)
    stores = [
        pltpu.make_async_copy(st_hi, high_hbm, store_sem.at[0]),
        pltpu.make_async_copy(st_lo, low_hbm, store_sem.at[1]),
    ]
    for copy in stores:
        copy.start()

    for copy in first:
        copy.wait()
    got = rb[...]
    got_t = got.T[:FEATURES]
    valid = got[:, 26:27]
    before = jnp.where(iota((slots, slots), 0) > iota((slots, slots), 1), 1.0, 0.0)
    rank = dot(before, jnp.broadcast_to(valid, (slots, lanes)))[:, 0:1]
    place = jnp.where(
        (iota((slots, slots), 1) == rank.astype(I32)) & (valid > 0.5), 1.0, 0.0
    )
    compact = dot(got_t, place, HIGHEST)
    at_ref[...] = compact
    mb[i] = compact[24:32]
    second = []
    for d in range(1, nx):
        copy = pltpu.make_async_remote_copy(
            src_ref=mb.at[i], dst_ref=mb.at[i],
            send_sem=s2_send.at[d], recv_sem=s2_recv.at[d],
            device_id=(lax.rem(i + d, nx), j), device_id_type=MESH,
        )
        copy.start()
        second.append(copy)
    for copy in halo:
        copy.wait()
    for k in range(planes):
        plane[k, 7:8, :] = jnp.where(i > 0, xr[0, k : k + 1, :], 0.0)
        plane[k, 8 + tile_x : 9 + tile_x, :] = jnp.where(i < nx - 1, xr[1, k : k + 1, :], 0.0)
    even = iota((2 * planes, tile_x), 0) % 2 == 0
    south = jnp.where(j > 0, yr[0], 0.0)
    north = jnp.where(j < ny - 1, yr[1], 0.0)
    beside = jnp.concatenate(
        [jnp.where(even, south, north), jnp.zeros((lanes - 2 * planes, tile_x), F32)], axis=0
    ).T
    beside_high, beside_low = split(beside)
    beside = jnp.where(
        iota((tile_x, lanes), 1) < lanes // 2,
        beside_high.astype(F32),
        pltpu.roll(beside_low.astype(F32), lanes // 2, 1),
    ).astype(BF16)
    near = time_step * diffuse_h
    wind = time_step * 0.5 * advect_coef
    own_part = 1.0 - time_step * (4.0 * diffuse_h + 2.0 * diffuse_z)
    here = pl.ds(8, tile_x)
    source, target = iota((lanes, 2 * lanes), 0), iota((lanes, 2 * lanes), 1)
    turn = (source == target + 1) | ((target >= lanes) & (source == target - lanes - 1))
    turn = jnp.where(turn, 1.0, 0.0).astype(BF16)

    def move(k, carry):
        z = k % 8
        center = plane[k, here, :]
        high, low = split(center)
        fill = ((source % (lanes // 2) == 2 * k + 1) & (target == lanes - 1)) | (
            (source % (lanes // 2) == 2 * k) & (target == lanes)
        )
        fill = jnp.where(fill, 1.0, 0.0).astype(BF16)
        sides = dot(
            jnp.concatenate([high, low, beside], axis=1),
            jnp.concatenate([turn, turn, fill], axis=0),
        )
        wind_u = wind * plane[z, here, :]
        wind_v = wind * plane[8 + z, here, :]
        upper = plane[k + jnp.where(z < 7, 1, 0), here, :]
        lower = plane[k - jnp.where(z > 0, 1, 0), here, :]
        moved[k] = (
            own_part * center
            + (near - wind_u) * plane[k, 9 : 9 + tile_x, :]
            + (near + wind_u) * plane[k, 7 : 7 + tile_x, :]
            + (near - wind_v) * sides[:, :lanes]
            + (near + wind_v) * sides[:, lanes:]
            + (time_step * diffuse_z) * (upper + lower)
        )
        return carry

    lax.fori_loop(0, planes, move, 0)
    stores.append(pltpu.make_async_copy(moved, base_hbm, store_sem.at[2]))
    stores[2].start()
    for copy in second:
        copy.wait()

    for k in range(nx):
        for f in range(3):
            rows[f, k : k + 1, :] = mb[k, f : f + 1, :]
    y_cells = rows[1].astype(I32)
    valid = rows[2] > 0.5
    group = jnp.where(valid, y_cells // (lanes // GROUPS), GROUPS)
    masks = jnp.concatenate(
        [jnp.where(group == g, 1.0, 0.0) for g in range(GROUPS)], axis=0
    )
    lines = GROUPS * nx
    after = jnp.where(iota((slots, slots), 0) < iota((slots, slots), 1), 1.0, 0.0)
    rank = dot(masks, after)
    total = jnp.broadcast_to(jnp.sum(masks, axis=1, keepdims=True), (lines, lanes))
    line, other = iota((lines, lines), 0), iota((lines, lines), 1)
    same = line // nx == other // nx
    offset = dot(jnp.where(same & (other < line), 1.0, 0.0), total, HIGHEST)
    whole = dot(jnp.where(same, 1.0, 0.0), total, HIGHEST)
    count = (whole.astype(I32) + (BLOCK - 1)) // BLOCK
    base = dot(
        jnp.where((other // nx < line // nx) & (other % nx == 0), 1.0, 0.0),
        count.astype(F32),
        HIGHEST,
    )
    placed = masks * (base[:, 0:1] * BLOCK + offset[:, 0:1] + rank)
    pos = placed[0:nx]
    for g in range(1, GROUPS):
        pos = pos + placed[g * nx : (g + 1) * nx]
    dump = (slots * nx // BLOCK + GROUPS + 1) * BLOCK
    info_ref[0:nx, :] = rows[0].astype(I32)
    info_ref[nx : 2 * nx, :] = y_cells % (lanes // GROUPS)
    info_ref[2 * nx : 3 * nx, :] = jnp.where(valid, pos.astype(I32), dump)
    info_ref[3 * nx : 4 * nx, :] = jnp.broadcast_to(
        jnp.sum(rows[2], axis=1, keepdims=True), (nx, slots)
    ).astype(I32)
    base = base.astype(I32)
    for g in range(GROUPS):
        info_ref[4 * nx + g : 4 * nx + g + 1, 0:lanes] = base[g * nx : g * nx + 1, :]
        info_ref[4 * nx + g : 4 * nx + g + 1, lanes : 2 * lanes] = count[g * nx : g * nx + 1, :]
    meta_ref[...] = mb[...]
    for copy in stores:
        copy.wait()


def block_tools(nx, lanes, info):
    def base(g):
        return info[4 * nx + g, 0]

    def count(g):
        return info[4 * nx + g, lanes]

    def group(b):
        found = 0
        for g in range(1, GROUPS):
            found = found + jnp.where(b >= base(g), 1, 0)
        return found

    return base, count, group, base(GROUPS - 1) + count(GROUPS - 1)


def gather_kernel(
    nx, info, cress_hbm, high_hbm, low_hbm, part_ref, wt_hi_hbm, wt_lo_hbm,
    cress, st_hi, st_lo, sorted_w, sorted_y, wt_hi, wt_lo, sums, by_slot, fold, sem,
):
    slots = info.shape[1]
    pieces, _, lanes = cress.shape
    tile_x = pieces * lanes
    base, count, group, blocks = block_tools(nx, lanes, info)
    loads = [
        pltpu.make_async_copy(
            cress_hbm.at[:, c * lanes : (c + 1) * lanes], cress.at[c], sem.at[c]
        )
        for c in range(pieces)
    ]
    state_loads = [
        pltpu.make_async_copy(high_hbm, st_hi, sem.at[3]),
        pltpu.make_async_copy(low_hbm, st_lo, sem.at[4]),
    ]
    for copy in loads + state_loads:
        copy.start()

    def clear(b):
        where = pl.ds(pl.multiple_of(b * BLOCK, BLOCK), BLOCK)
        for c in range(pieces):
            sorted_w[c, where, :] = jnp.zeros((BLOCK, lanes), F32)
        sorted_y[where, :] = jnp.full((BLOCK, lanes), -1, I32)

    for g in range(GROUPS):
        pl.when(count(g) > 0)(functools.partial(clear, base(g) + count(g) - 1))
    clear(blocks)
    wide = 3 * lanes
    for g in range(GROUPS):
        fold[g] = jnp.where(
            group_of(iota((wide, lanes), 0), g) == iota((wide, lanes), 1), 1.0, 0.0
        ).astype(BF16)

    for copy in loads:
        copy.wait()
    for k in range(nx):

        def bring(n, carry):
            at = [n * 8 + m for m in range(8)]
            cells = [info[k, s] for s in at]
            places = [info[2 * nx + k, s] for s in at]
            got = [[cress[c, pl.ds(x, 1), :] for c in range(pieces)] for x in cells]
            for p, found in zip(places, got):
                for c in range(pieces):
                    sorted_w[c, pl.ds(p, 1), :] = found[c]
            for p, s in zip(places, at):
                sorted_y[pl.ds(p, 1), :] = jnp.full((1, lanes), info[nx + k, s], I32)
            return carry

        lax.fori_loop(0, (info[3 * nx + k, 0] + 7) // 8, bring, 0)

    for copy in state_loads:
        copy.wait()
    yy = iota((BLOCK, wide), 1) % 16
    lane = iota((BLOCK, lanes), 1)

    def block_sums(b):
        where = pl.ds(pl.multiple_of(b * BLOCK, BLOCK), BLOCK)
        g = group(b)
        parts = [sorted_w[c, where, :] for c in range(pieces)]
        high, low = split(jnp.concatenate(parts, axis=1))
        both = dot(jnp.concatenate([high, low], axis=0), st_hi[g])
        products = both[:BLOCK] + both[BLOCK:] + dot(high, st_lo[g])
        y_here = sorted_y[where, :]
        y_wide = jnp.concatenate([y_here, y_here, y_here], axis=1)
        chosen = split(jnp.where(yy == y_wide, products, 0.0))
        both = dot(jnp.concatenate(chosen, axis=0), fold[g])
        total = jnp.sum(parts[0] + parts[1] + parts[2], axis=1, keepdims=True)
        result = jnp.where(lane == 24, total, both[:BLOCK] + both[BLOCK:])
        turned = [split(part.T) for part in parts]
        return where, result, turned

    def two_blocks(n, carry):
        for where, result, turned in [block_sums(2 * n), block_sums(2 * n + 1)]:
            sums[where, :] = result
            for c in range(pieces):
                wt_hi[c * lanes : (c + 1) * lanes, where] = turned[c][0]
                wt_lo[c * lanes : (c + 1) * lanes, where] = turned[c][1]
        return carry

    lax.fori_loop(0, (blocks + 1) // 2, two_blocks, 0)
    stores = [
        pltpu.make_async_copy(wt_hi, wt_hi_hbm, sem.at[5]),
        pltpu.make_async_copy(wt_lo, wt_lo_hbm, sem.at[6]),
    ]
    for copy in stores:
        copy.start()

    by_slot[...] = jnp.zeros(by_slot.shape, F32)
    for k in range(nx):

        def give(n, carry):
            start = pl.multiple_of(n * 8, 8)
            got = [sums[pl.ds(info[2 * nx + k, start + m], 1), :] for m in range(8)]
            by_slot[pl.ds(k * slots + start, 8), :] = jnp.concatenate(got, axis=0)
            return carry

        lax.fori_loop(0, (info[3 * nx + k, 0] + 7) // 8, give, 0)
        part_ref[k] = by_slot[k * slots : (k + 1) * slots, :].T[:FEATURES]
    for copy in stores:
        copy.wait()


def reduce_kernel(
    nx, part_ref, at_ref, vert_ref, out_ref, rs, ag, send1, recv1, send2, recv2
):
    i, j = lax.axis_index("gx"), lax.axis_index("gy")
    barrier = pltpu.get_barrier_semaphore()
    for d in range(1, nx):
        pl.semaphore_signal(
            barrier, inc=1, device_id=(lax.rem(i + d, nx), j), device_id_type=MESH
        )
    pl.semaphore_wait(barrier, nx - 1)
    copies = []
    for d in range(1, nx):
        k = lax.rem(i + d, nx)
        copy = pltpu.make_async_remote_copy(
            src_ref=part_ref.at[k], dst_ref=rs.at[i],
            send_sem=send1.at[d], recv_sem=recv1.at[d],
            device_id=(k, j), device_id_type=MESH,
        )
        copy.start()
        copies.append(copy)
    rs[i] = part_ref[i]
    lanes = vert_ref.shape[1]
    vert = jnp.concatenate([vert_ref[...], jnp.zeros((8, lanes), F32)], axis=0)
    same = iota((FEATURES, FEATURES), 0) // 8 == iota((FEATURES, FEATURES), 1) // 8
    gram = jnp.where(same, dot_t(vert, vert, HIGHEST), 0.0)
    at = at_ref[...]
    row = iota(at.shape, 0)
    for copy in copies:
        copy.wait()
    total = rs[0]
    for k in range(1, nx):
        total = total + rs[k]
    weight = total[24:25, :]
    mean = jnp.where(row < 24, total / jnp.where(weight > 0.0, weight, 1.0), 0.0)
    spread = spread_gain * (at - dot(gram, mean, HIGHEST))
    ag[i] = spread[: ag.shape[1]]
    copies = []
    for d in range(1, nx):
        copy = pltpu.make_async_remote_copy(
            src_ref=ag.at[i], dst_ref=ag.at[i],
            send_sem=send2.at[d], recv_sem=recv2.at[d],
            device_id=(lax.rem(i + d, nx), j), device_id_type=MESH,
        )
        copy.start()
        copies.append(copy)
    for copy in copies:
        copy.wait()
    out_ref[...] = ag[...]


def update_kernel(
    nx, info, spread_ref, meta_ref, wt_hi_hbm, wt_lo_hbm, base_hbm,
    out_hbm, moved, wt_hi, wt_lo, by_slot, sorted_s, num, weights, widen, sem,
):
    slots = spread_ref.shape[2]
    planes, tile_x, lanes = moved.shape
    base, count, group, blocks = block_tools(nx, lanes, info)
    load_h = pltpu.make_async_copy(wt_hi_hbm, wt_hi, sem.at[1])
    load_l = pltpu.make_async_copy(wt_lo_hbm, wt_lo, sem.at[2])
    load_s = pltpu.make_async_copy(base_hbm, moved, sem.at[0])
    load_h.start()
    load_l.start()
    load_s.start()

    def clear(b):
        where = pl.ds(pl.multiple_of(b * BLOCK, BLOCK), BLOCK)
        sorted_s[where, :] = jnp.full((BLOCK, lanes), -1.0, F32)

    for g in range(GROUPS):
        pl.when(count(g) > 0)(functools.partial(clear, base(g) + count(g) - 1))
    clear(blocks)
    wide = 3 * lanes
    for g in range(GROUPS):
        widen[g] = jnp.where(
            group_of(iota((lanes, wide), 1), g) == iota((lanes, wide), 0), 1.0, 0.0
        ).astype(BF16)
    num[...] = jnp.zeros(num.shape, F32)
    weights[...] = jnp.zeros(weights.shape, F32)

    pad = jnp.zeros((lanes - FEATURES, slots), F32)
    for k in range(nx):
        by_slot[k * slots : (k + 1) * slots, :] = jnp.concatenate(
            [spread_ref[k], meta_ref[k], pad], axis=0
        ).T

        def bring(n, carry):
            start = pl.multiple_of(n * 8, 8)
            got = by_slot[pl.ds(k * slots + start, 8), :]
            for m in range(8):
                sorted_s[pl.ds(info[2 * nx + k, start + m], 1), :] = got[m : m + 1, :]
            return carry

        lax.fori_loop(0, (info[3 * nx + k, 0] + 7) // 8, bring, 0)

    yy = iota((BLOCK, wide), 1) % 16
    load_h.wait()
    load_l.wait()

    def block_update(b):
        where = pl.ds(pl.multiple_of(b * BLOCK, BLOCK), BLOCK)
        g = group(b)
        value = sorted_s[where, :]
        y_here = value[:, 25:26].astype(I32)
        match = (value[:, 26:27] > 0.5) & (yy == y_here % 16)
        both = dot(jnp.concatenate(split(value), axis=0), widen[g])
        s_hi = jnp.where(match, both[:BLOCK], 0.0).astype(BF16)
        s_lo = jnp.where(match, both[BLOCK:], 0.0).astype(BF16)
        ones = jnp.where(match[:, :lanes], 1.0, 0.0).astype(BF16)
        w_hi, w_lo = wt_hi[:, where], wt_lo[:, where]
        right = jnp.concatenate([s_hi, ones], axis=1)
        added = dot(
            jnp.concatenate([w_hi, w_hi, w_lo], axis=1),
            jnp.concatenate(
                [right, jnp.concatenate([s_lo, jnp.zeros_like(ones)], axis=1), right], axis=0
            ),
        )
        return g, added

    def two_blocks(n, carry):
        for g, added in [block_update(2 * n), block_update(2 * n + 1)]:
            num[g] += added[:, :wide]
            weights[g] += added[:, wide:]
        return carry

    lax.fori_loop(0, (blocks + 1) // 2, two_blocks, 0)

    load_s.wait()
    chunk, parts = 8, 4
    length = tile_x // parts
    stores = []
    for part in range(parts):

        def finish(n, carry):
            here = pl.ds(pl.multiple_of(part * length + n * chunk, chunk), chunk)
            scale = [
                (time_step * nudge_gain) / jnp.maximum(weights[g, here, :], 1.0)
                for g in range(GROUPS)
            ]
            for v in range(3):
                gains = to_levels(
                    [num[g, here, v * lanes : (v + 1) * lanes] * scale[g] for g in range(GROUPS)]
                )
                for z in range(8):
                    moved[v * 8 + z, here, :] += gains[z]
            return carry

        lax.fori_loop(0, length // chunk, finish, 0)
        rows = pl.ds(part * length, length)
        stores.append(
            pltpu.make_async_copy(moved.at[:, rows, :], out_hbm.at[:, rows, :], sem.at[3 + part])
        )
        stores[-1].start()
    for copy in stores:
        copy.wait()


VM = pltpu.MemorySpace.VMEM


def vmem():
    return pl.BlockSpec(memory_space=VM)


def smem():
    return pl.BlockSpec(memory_space=pltpu.MemorySpace.SMEM)


def hbm():
    return pl.BlockSpec(memory_space=pl.ANY)


def gather_scratch(nx, slots, rows, cress_shape, grouped, lanes):
    across, tile_x = cress_shape
    return [
        pltpu.VMEM((tile_x // lanes, across, lanes), F32),
        pltpu.VMEM(grouped, BF16),
        pltpu.VMEM(grouped, BF16),
        pltpu.VMEM((tile_x // lanes, rows + 8, lanes), F32),
        pltpu.VMEM((rows + 8, lanes), I32),
        pltpu.VMEM((tile_x, rows), BF16),
        pltpu.VMEM((tile_x, rows), BF16),
        pltpu.VMEM((rows + 8, lanes), F32),
        pltpu.VMEM((nx * slots, lanes), F32),
        pltpu.VMEM((GROUPS, 3 * lanes, lanes), BF16),
        pltpu.SemaphoreType.DMA((7,)),
    ]


def update_scratch(nx, slots, rows, grouped, planes, lanes):
    tile_x = grouped[1]
    return [
        pltpu.VMEM((planes, tile_x, lanes), F32),
        pltpu.VMEM((tile_x, rows), BF16),
        pltpu.VMEM((tile_x, rows), BF16),
        pltpu.VMEM((nx * slots, lanes), F32),
        pltpu.VMEM((rows + 8, lanes), F32),
        pltpu.VMEM(grouped, F32),
        pltpu.VMEM((GROUPS, tile_x, lanes), F32),
        pltpu.VMEM((GROUPS, lanes, 3 * lanes), BF16),
        pltpu.SemaphoreType.DMA((7,)),
    ]


def local(nx, ny, model_state, obs_val, obs_owner, obs_x, obs_y, cressman, vertical):
    fields, levels, tile_x, lanes = model_state.shape
    planes = fields * levels
    recs = obs_val.shape[0]
    cap = max(2, 2 * recs // ny)
    slots = ny * cap
    rows = (slots * nx // BLOCK + GROUPS + 1) * BLOCK
    state = model_state.reshape(planes, tile_x, lanes)
    vert = vertical.reshape(planes, vertical.shape[2])
    shape = jax.ShapeDtypeStruct
    dma = pltpu.SemaphoreType.DMA
    limit = 56 * 1024 * 1024

    grouped = (GROUPS, tile_x, fields * lanes)
    at, info, meta, base, st_hi, st_lo = pl.pallas_call(
        functools.partial(dispatch_kernel, nx, ny),
        out_shape=(
            shape((FEATURES, slots), F32),
            shape((4 * nx + GROUPS, slots), I32),
            shape((nx, 8, slots), F32),
            shape((planes, tile_x, lanes), F32),
            shape(grouped, BF16),
            shape(grouped, BF16),
        ),
        in_specs=[vmem()] * 5 + [hbm()],
        out_specs=[vmem()] * 3 + [hbm()] * 3,
        scratch_shapes=[
            pltpu.VMEM((planes, tile_x + 16, lanes), F32),
            pltpu.VMEM((planes, tile_x, lanes), F32),
            pltpu.VMEM(grouped, BF16),
            pltpu.VMEM(grouped, BF16),
            pltpu.VMEM((slots, lanes), F32),
            pltpu.VMEM((slots, lanes), F32),
            pltpu.VMEM((nx, 8, slots), F32),
            pltpu.VMEM((3, nx, slots), F32),
            pltpu.VMEM((2, planes, lanes), F32),
            pltpu.VMEM((2 * planes, tile_x), F32),
            pltpu.VMEM((2, planes, lanes), F32),
            pltpu.VMEM((2, 2 * planes, tile_x), F32),
            dma,
            dma((3,)),
            dma((ny,)),
            dma((ny,)),
            dma((nx,)),
            dma((nx,)),
            dma((4,)),
            dma((4,)),
        ],
        compiler_params=pltpu.CompilerParams(
            collective_id=0, has_side_effects=True, vmem_limit_bytes=limit
        ),
        name="dispatch",
    )(
        obs_val, obs_owner.reshape(1, recs), obs_x.reshape(1, recs), obs_y.reshape(1, recs),
        vert, state,
    )

    part, wt_hi, wt_lo = pl.pallas_call(
        functools.partial(gather_kernel, nx),
        out_shape=(
            shape((nx, FEATURES, slots), F32),
            shape((tile_x, rows), BF16),
            shape((tile_x, rows), BF16),
        ),
        in_specs=[smem()] + [hbm()] * 3,
        out_specs=[vmem()] + [hbm()] * 2,
        scratch_shapes=gather_scratch(nx, slots, rows, cressman.shape, grouped, lanes),
        compiler_params=pltpu.CompilerParams(vmem_limit_bytes=limit),
        name="column_sums",
    )(info, cressman, st_hi, st_lo)

    spread = pl.pallas_call(
        functools.partial(reduce_kernel, nx),
        out_shape=shape((nx, planes, slots), F32),
        in_specs=[vmem()] * 3,
        out_specs=vmem(),
        scratch_shapes=[
            pltpu.VMEM((nx, FEATURES, slots), F32),
            pltpu.VMEM((nx, planes, slots), F32),
            dma((nx,)),
            dma((nx,)),
            dma((nx,)),
            dma((nx,)),
        ],
        compiler_params=pltpu.CompilerParams(
            collective_id=1, has_side_effects=True, vmem_limit_bytes=limit
        ),
        name="innovations",
    )(part, at, vert)

    out = pl.pallas_call(
        functools.partial(update_kernel, nx),
        out_shape=shape((planes, tile_x, lanes), F32),
        in_specs=[smem()] + [vmem()] * 2 + [hbm()] * 3,
        out_specs=hbm(),
        scratch_shapes=update_scratch(nx, slots, rows, grouped, planes, lanes),
        compiler_params=pltpu.CompilerParams(vmem_limit_bytes=limit),
        name="update",
    )(info, spread, meta, wt_hi, wt_lo, base)
    return out.reshape(model_state.shape)


def solution(mesh):
    in_specs = (
        P(None, None, "gx", "gy"),
        P(("gx", "gy"), None),
        P(("gx", "gy"), None),
        P(("gx", "gy")),
        P(("gx", "gy")),
        P(None, "gx"),
        P(),
    )
    out_specs = P(None, None, "gx", "gy")
    return jax.shard_map(
        functools.partial(local, mesh.shape["gx"], mesh.shape["gy"]),
        mesh=mesh, in_specs=in_specs, out_specs=out_specs, check_vma=False,
    )
```

```python
import functools

import jax
import jax.numpy as jnp
from jax import lax
from jax.experimental import pallas as pl
from jax.experimental.pallas import tpu as pltpu
from jax.sharding import PartitionSpec as P

F32 = jnp.float32
BF16 = jnp.bfloat16
I32 = jnp.int32
HIGHEST = lax.Precision.HIGHEST
MESH = pl.DeviceIdType.MESH

advect_coef = 0.5
diffuse_h = 0.2
diffuse_z = 0.1
time_step = 0.5
nudge_gain = 1.0
spread_gain = 0.125

FEATURES = 32
GROUPS = 8
BLOCK = 128
CELLS = 4096
STEP = 32


def iota(shape, dim):
    return lax.broadcasted_iota(I32, shape, dim)


def dot(a, b, precision=None):
    return lax.dot_general(
        a, b, (((1,), (0,)), ((), ())), precision=precision, preferred_element_type=F32
    )


def dot_t(a, b, precision=None):
    return lax.dot_general(
        a, b, (((1,), (1,)), ((), ())), precision=precision, preferred_element_type=F32
    )


def split(value):
    high = value.astype(BF16)
    return high, (value - high.astype(F32)).astype(BF16)


def barrel(parts):
    block = iota(parts[0].shape, 1) // 16
    for bit in (1, 2, 4):
        upper = (block & bit) != 0
        parts = [jnp.where(upper, parts[(c + bit) % 8], parts[c]) for c in range(8)]
    return parts


def to_groups(parts):
    parts = barrel([pltpu.roll(p, 16 * z, 1) if z else p for z, p in enumerate(parts)])
    return [parts[-g % 8] for g in range(8)]


def to_levels(parts):
    parts = barrel(parts)
    return [
        pltpu.roll(parts[-z % 8], 128 - 16 * z, 1) if z else parts[0] for z in range(8)
    ]


def group_of(lane, g):
    return lane // 128 * 8 + (lane // 16 + 8 - g) % 8


def dispatch_kernel(
    nx, ny, obs_ref, owner_ref, x_ref, y_ref, vert_ref, state_hbm,
    at_ref, info_ref, meta_ref, xh_ref, yh_ref, high_hbm, low_hbm,
    plane, st_hi, st_lo, sb, rb, mb, rows, xe, ye, xr, yr,
    load_sem, store_sem, s1_send, s1_recv, s2_send, s2_recv, h_send, h_recv,
):
    i, j = lax.axis_index("gx"), lax.axis_index("gy")
    planes, tile_x, lanes = plane.shape
    load = pltpu.make_async_copy(state_hbm, plane, load_sem)
    load.start()
    barrier = pltpu.get_barrier_semaphore()
    for d in range(1, ny):
        pl.semaphore_signal(
            barrier, inc=1, device_id=(i, lax.rem(j + d, ny)), device_id_type=MESH
        )
    for d in range(1, nx):
        pl.semaphore_signal(
            barrier, inc=1, device_id=(lax.rem(i + d, nx), j), device_id_type=MESH
        )

    recs = obs_ref.shape[0]
    slots = sb.shape[0]
    cap = slots // ny
    vert = vert_ref[...]
    var = iota((planes, lanes), 0) // 8
    basis = jnp.concatenate([jnp.where(var == v, vert, 0.0) for v in range(3)], axis=1)
    basis = jnp.concatenate([basis, jnp.zeros((lanes - planes, 3 * lanes), F32)], axis=0)
    payload = dot_t(obs_ref[...], basis, HIGHEST)
    eye = iota((recs, recs), 0) == iota((recs, recs), 1)
    x_col = jnp.sum(jnp.where(eye, x_ref[...].astype(F32), 0.0), axis=1, keepdims=True)
    y_col = jnp.sum(jnp.where(eye, y_ref[...].astype(F32), 0.0), axis=1, keepdims=True)
    lane = iota((recs, lanes), 1)
    payload = jnp.where(lane == 24, x_col, payload)
    payload = jnp.where(lane == 25, y_col, payload)
    payload = jnp.where(lane == 26, 1.0, payload)
    owner = jnp.sum(jnp.where(eye, owner_ref[...], 0), axis=1, keepdims=True)
    onehot = jnp.where(owner == lane, 1.0, 0.0)
    earlier = jnp.where(iota((recs, recs), 0) > iota((recs, recs), 1), 1.0, 0.0)
    rank = jnp.sum(dot(earlier, onehot) * onehot, axis=1, keepdims=True)
    slot = owner.astype(F32) * cap + rank
    slot_row = jnp.sum(jnp.where(eye, slot, 0.0), axis=0, keepdims=True).astype(I32)
    place = jnp.where(iota((slots, recs), 0) == slot_row, 1.0, 0.0)
    sb[...] = dot(place, payload, HIGHEST)

    pl.semaphore_wait(barrier, nx + ny - 2)
    first = []
    for d in range(1, ny):
        c = lax.rem(j + d, ny)
        copy = pltpu.make_async_remote_copy(
            src_ref=sb.at[pl.ds(pl.multiple_of(c * cap, cap), cap)],
            dst_ref=rb.at[pl.ds(pl.multiple_of(j * cap, cap), cap)],
            send_sem=s1_send.at[d], recv_sem=s1_recv.at[d],
            device_id=(i, c), device_id_type=MESH,
        )
        copy.start()
        first.append(copy)
    own = pl.ds(pl.multiple_of(j * cap, cap), cap)
    rb[own, :] = sb[own, :]

    load.wait()
    for k in range(planes):
        xe[0, k : k + 1, :] = plane[k, tile_x - 1 : tile_x, :]
        xe[1, k : k + 1, :] = plane[k, 0:1, :]
    edge_lane = iota((tile_x, lanes), 1)

    def gather_edges(k, edges):
        turned = pltpu.roll(plane[k], 2 * k + 1, 1)
        return jnp.where(edge_lane // 2 == k, turned, edges)

    edges = lax.fori_loop(0, planes, gather_edges, jnp.zeros((tile_x, lanes), F32))
    ye[...] = edges.T[: 2 * planes]
    halo = []
    for n, (src, dst, to) in enumerate((
        (xe.at[0], xr.at[0], (lax.rem(i + 1, nx), j)),
        (xe.at[1], xr.at[1], (lax.rem(i + nx - 1, nx), j)),
        (ye, yr.at[0], (i, lax.rem(j + 1, ny))),
        (ye, yr.at[1], (i, lax.rem(j + ny - 1, ny))),
    )):
        copy = pltpu.make_async_remote_copy(
            src_ref=src, dst_ref=dst, send_sem=h_send.at[n], recv_sem=h_recv.at[n],
            device_id=to, device_id_type=MESH,
        )
        copy.start()
        halo.append(copy)

    for copy in first:
        copy.wait()
    got = rb[...]
    got_t = got.T[:FEATURES]
    valid = got[:, 26:27]
    before = jnp.where(iota((slots, slots), 0) > iota((slots, slots), 1), 1.0, 0.0)
    rank = dot(before, jnp.broadcast_to(valid, (slots, lanes)))[:, 0:1]
    place = jnp.where(
        (iota((slots, slots), 1) == rank.astype(I32)) & (valid > 0.5), 1.0, 0.0
    )
    compact = dot(got_t, place, HIGHEST)
    at_ref[...] = compact
    mb[i] = compact[24:32]
    second = []
    for d in range(1, nx):
        copy = pltpu.make_async_remote_copy(
            src_ref=mb.at[i], dst_ref=mb.at[i],
            send_sem=s2_send.at[d], recv_sem=s2_recv.at[d],
            device_id=(lax.rem(i + d, nx), j), device_id_type=MESH,
        )
        copy.start()
        second.append(copy)
    chunk = 32

    def group_chunk(n, carry):
        here = pl.ds(pl.multiple_of(n * chunk, chunk), chunk)
        for v in range(3):
            parts = to_groups([plane[v * 8 + z, here, :] for z in range(8)])
            for g in range(GROUPS):
                high, low = split(parts[g])
                st_hi[g, here, v * lanes : (v + 1) * lanes] = high
                st_lo[g, here, v * lanes : (v + 1) * lanes] = low
        return carry

    lax.fori_loop(0, tile_x // chunk, group_chunk, 0)
    stores = [
        pltpu.make_async_copy(st_hi, high_hbm, store_sem.at[0]),
        pltpu.make_async_copy(st_lo, low_hbm, store_sem.at[1]),
    ]
    for copy in stores:
        copy.start()

    for copy in halo:
        copy.wait()
    xh_ref[0] = jnp.where(i > 0, xr[0], 0.0)
    xh_ref[1] = jnp.where(i < nx - 1, xr[1], 0.0)
    even = iota((2 * planes, tile_x), 0) % 2 == 0
    south = jnp.where(j > 0, yr[0], 0.0)
    north = jnp.where(j < ny - 1, yr[1], 0.0)
    yh_ref[...] = jnp.where(even, south, north)
    for copy in second:
        copy.wait()

    for k in range(nx):
        for f in range(3):
            rows[f, k : k + 1, :] = mb[k, f : f + 1, :]
    y_cells = rows[1].astype(I32)
    valid = rows[2] > 0.5
    group = jnp.where(valid, y_cells // (lanes // GROUPS), GROUPS)
    masks = jnp.concatenate(
        [jnp.where(group == g, 1.0, 0.0) for g in range(GROUPS)], axis=0
    )
    lines = GROUPS * nx
    after = jnp.where(iota((slots, slots), 0) < iota((slots, slots), 1), 1.0, 0.0)
    rank = dot(masks, after)
    total = jnp.broadcast_to(jnp.sum(masks, axis=1, keepdims=True), (lines, lanes))
    line, other = iota((lines, lines), 0), iota((lines, lines), 1)
    same = line // nx == other // nx
    offset = dot(jnp.where(same & (other < line), 1.0, 0.0), total, HIGHEST)
    whole = dot(jnp.where(same, 1.0, 0.0), total, HIGHEST)
    count = (whole.astype(I32) + (BLOCK - 1)) // BLOCK
    base = dot(
        jnp.where((other // nx < line // nx) & (other % nx == 0), 1.0, 0.0),
        count.astype(F32),
        HIGHEST,
    )
    placed = masks * (base[:, 0:1] * BLOCK + offset[:, 0:1] + rank)
    pos = placed[0:nx]
    for g in range(1, GROUPS):
        pos = pos + placed[g * nx : (g + 1) * nx]
    dump = (slots * nx // BLOCK + GROUPS + 1) * BLOCK
    place = jnp.where(valid, pos.astype(I32), dump)
    info_ref[0:nx, :] = (
        place + (rows[0].astype(I32) + y_cells % (lanes // GROUPS) * CELLS) * CELLS
    )
    info_ref[nx : 2 * nx, :] = jnp.broadcast_to(
        jnp.sum(rows[2], axis=1, keepdims=True), (nx, slots)
    ).astype(I32)
    base = base.astype(I32)
    for g in range(GROUPS):
        info_ref[2 * nx + g : 2 * nx + g + 1, 0:lanes] = base[g * nx : g * nx + 1, :]
        info_ref[2 * nx + g : 2 * nx + g + 1, lanes : 2 * lanes] = count[g * nx : g * nx + 1, :]
    meta_ref[...] = mb[...]
    for copy in stores:
        copy.wait()


def block_tools(nx, lanes, info):
    def base(g):
        return info[2 * nx + g, 0]

    def count(g):
        return info[2 * nx + g, lanes]

    def group(b):
        found = 0
        for g in range(1, GROUPS):
            found = found + jnp.where(b >= base(g), 1, 0)
        return found

    return base, count, group, base(GROUPS - 1) + count(GROUPS - 1)


def gather_kernel(
    nx, info, cress_hbm, high_hbm, low_hbm, part_ref, wt_hi_hbm, wt_lo_hbm,
    cress, st_hi, st_lo, sorted_w, chosen, totals, wt_hi, wt_lo, sums, by_slot, fold, sem,
):
    slots = info.shape[1]
    lanes = cress.shape[2]
    tile_x = cress_hbm.shape[1]
    pieces = tile_x // lanes
    rows = wt_hi.shape[1]
    base, count, group, blocks = block_tools(nx, lanes, info)
    loads = [
        pltpu.make_async_copy(
            cress_hbm.at[:, c * lanes : (c + 1) * lanes], cress.at[:, c, :], sem.at[c]
        )
        for c in range(pieces)
    ]
    state_loads = [
        pltpu.make_async_copy(high_hbm, st_hi, sem.at[3]),
        pltpu.make_async_copy(low_hbm, st_lo, sem.at[4]),
    ]
    for copy in loads + state_loads:
        copy.start()
    y_line = iota((8, lanes), 0) == pieces
    blank = jnp.where(y_line, -1.0, jnp.zeros((8, lanes), F32))

    def clear(b):
        where = pl.ds(pl.multiple_of(b * BLOCK, BLOCK), BLOCK)
        sorted_w[where] = jnp.broadcast_to(blank[None], (BLOCK, 8, lanes))

    for g in range(GROUPS):
        pl.when(count(g) > 0)(functools.partial(clear, base(g) + count(g) - 1))
    clear(blocks)
    wide = 3 * lanes
    for g in range(GROUPS):
        fold[g] = jnp.where(
            group_of(iota((wide, lanes), 0), g) == iota((wide, lanes), 1), 1.0, 0.0
        ).astype(BF16)

    for copy in loads:
        copy.wait()
    for k in range(nx):

        def bring(n, carry):
            entries = [info[k, n * STEP + m] for m in range(STEP)]
            got = [
                jnp.where(y_line, (lax.shift_right_logical(e, 24)).astype(F32), cress[lax.shift_right_logical(e, 12) & (CELLS - 1)])
                for e in entries
            ]
            for e, row in zip(entries, got):
                sorted_w[e & (CELLS - 1)] = row
            return carry

        lax.fori_loop(0, (info[nx + k, 0] + STEP - 1) // STEP, bring, 0)

    for copy in state_loads:
        copy.wait()
    yy = (iota((BLOCK, wide), 1) % 16).astype(F32)
    lane = iota((BLOCK, lanes), 1)

    def multiply(b):
        b = jnp.minimum(b, blocks)
        where = pl.ds(pl.multiple_of(b * BLOCK, BLOCK), BLOCK)
        g = group(b)
        parts = [sorted_w[where, c, :] for c in range(pieces)]
        high, low = split(jnp.concatenate(parts, axis=1))
        both = dot(jnp.concatenate([high, low], axis=0), st_hi[g])
        products = both[:BLOCK] + both[BLOCK:] + dot(high, st_lo[g])
        y_here = sorted_w[where, pieces, :]
        y_wide = jnp.concatenate([y_here, y_here, y_here], axis=1)
        high, low = split(jnp.where(yy == y_wide, products, 0.0))
        total = jnp.sum(parts[0] + parts[1] + parts[2], axis=1, keepdims=True)
        return where, high, low, total, [split(part.T) for part in parts]

    def two_blocks(n, carry):
        for m in range(2):
            b = 2 * n - 2 + m
            both = dot(chosen[m], fold[group(b)])
            result = jnp.where(lane == 24, totals[m], both[:BLOCK] + both[BLOCK:])
            start = jnp.where(b < 0, rows + m * BLOCK, b * BLOCK)
            sums[pl.ds(pl.multiple_of(start, BLOCK), BLOCK), :] = result
        for m, (where, high, low, total, turned) in enumerate(
            [multiply(2 * n), multiply(2 * n + 1)]
        ):
            chosen[m, :BLOCK, :] = high
            chosen[m, BLOCK:, :] = low
            totals[m] = jnp.broadcast_to(total, (BLOCK, lanes))
            for c in range(pieces):
                wt_hi[c * lanes : (c + 1) * lanes, where] = turned[c][0]
                wt_lo[c * lanes : (c + 1) * lanes, where] = turned[c][1]
        return carry

    lax.fori_loop(0, (blocks + 1) // 2 + 1, two_blocks, 0)
    stores = [
        pltpu.make_async_copy(wt_hi, wt_hi_hbm, sem.at[5]),
        pltpu.make_async_copy(wt_lo, wt_lo_hbm, sem.at[6]),
    ]
    for copy in stores:
        copy.start()

    by_slot[...] = jnp.zeros(by_slot.shape, F32)
    for k in range(nx):

        def give(n, carry):
            start = pl.multiple_of(k * slots + n * STEP, STEP)
            entries = [info[k, n * STEP + m] for m in range(STEP)]
            got = [sums[pl.ds(e & (CELLS - 1), 1), :] for e in entries]
            for m in range(STEP):
                by_slot[pl.ds(start + m, 1), :] = got[m]
            return carry

        lax.fori_loop(0, (info[nx + k, 0] + STEP - 1) // STEP, give, 0)
        part_ref[k] = by_slot[k * slots : (k + 1) * slots, :].T[:FEATURES]
    for copy in stores:
        copy.wait()


def reduce_kernel(
    nx, part_ref, at_ref, vert_ref, xh_ref, yh_ref, state_hbm, out_ref, base_hbm,
    plane, moved, rs, ag, load_sem, store_sem, send1, recv1, send2, recv2,
):
    i, j = lax.axis_index("gx"), lax.axis_index("gy")
    planes, padded_x, lanes = plane.shape
    tile_x = padded_x - 16
    load = pltpu.make_async_copy(state_hbm, plane.at[:, 8 : 8 + tile_x, :], load_sem)
    load.start()
    barrier = pltpu.get_barrier_semaphore()
    for d in range(1, nx):
        pl.semaphore_signal(
            barrier, inc=1, device_id=(lax.rem(i + d, nx), j), device_id_type=MESH
        )
    for k in range(planes):
        plane[k, 7:8, :] = xh_ref[0, k : k + 1, :]
        plane[k, 8 + tile_x : 9 + tile_x, :] = xh_ref[1, k : k + 1, :]
    beside = jnp.concatenate(
        [yh_ref[...], jnp.zeros((lanes - 2 * planes, tile_x), F32)], axis=0
    ).T
    beside_high, beside_low = split(beside)
    beside = jnp.where(
        iota((tile_x, lanes), 1) < lanes // 2,
        beside_high.astype(F32),
        pltpu.roll(beside_low.astype(F32), lanes // 2, 1),
    ).astype(BF16)
    near = time_step * diffuse_h
    wind = time_step * 0.5 * advect_coef
    own_part = 1.0 - time_step * (4.0 * diffuse_h + 2.0 * diffuse_z)
    here = pl.ds(8, tile_x)
    source, target = iota((lanes, 2 * lanes), 0), iota((lanes, 2 * lanes), 1)
    turn = (source == target + 1) | ((target >= lanes) & (source == target - lanes - 1))
    turn = jnp.where(turn, 1.0, 0.0).astype(BF16)

    def move(k, carry):
        z = k % 8
        center = plane[k, here, :]
        high, low = split(center)
        fill = ((source % (lanes // 2) == 2 * k + 1) & (target == lanes - 1)) | (
            (source % (lanes // 2) == 2 * k) & (target == lanes)
        )
        fill = jnp.where(fill, 1.0, 0.0).astype(BF16)
        sides = dot(
            jnp.concatenate([high, low, beside], axis=1),
            jnp.concatenate([turn, turn, fill], axis=0),
        )
        wind_u = wind * plane[z, here, :]
        wind_v = wind * plane[8 + z, here, :]
        upper = plane[k + jnp.where(z < 7, 1, 0), here, :]
        lower = plane[k - jnp.where(z > 0, 1, 0), here, :]
        moved[k] = (
            own_part * center
            + (near - wind_u) * plane[k, 9 : 9 + tile_x, :]
            + (near + wind_u) * plane[k, 7 : 7 + tile_x, :]
            + (near - wind_v) * sides[:, :lanes]
            + (near + wind_v) * sides[:, lanes:]
            + (time_step * diffuse_z) * (upper + lower)
        )
        return carry

    vert = jnp.concatenate([vert_ref[...], jnp.zeros((8, lanes), F32)], axis=0)
    same = iota((FEATURES, FEATURES), 0) // 8 == iota((FEATURES, FEATURES), 1) // 8
    gram = jnp.where(same, dot_t(vert, vert, HIGHEST), 0.0)
    at = at_ref[...]
    row = iota(at.shape, 0)

    pl.semaphore_wait(barrier, nx - 1)
    copies = []
    for d in range(1, nx):
        k = lax.rem(i + d, nx)
        copy = pltpu.make_async_remote_copy(
            src_ref=part_ref.at[k], dst_ref=rs.at[i],
            send_sem=send1.at[d], recv_sem=recv1.at[d],
            device_id=(k, j), device_id_type=MESH,
        )
        copy.start()
        copies.append(copy)
    rs[i] = part_ref[i]
    load.wait()
    half = planes // 2
    lax.fori_loop(0, half, move, 0)
    stores = [pltpu.make_async_copy(moved.at[0:half], base_hbm.at[0:half], store_sem.at[0])]
    stores[0].start()
    for copy in copies:
        copy.wait()
    total = rs[0]
    for k in range(1, nx):
        total = total + rs[k]
    weight = total[24:25, :]
    mean = jnp.where(row < 24, total / jnp.where(weight > 0.0, weight, 1.0), 0.0)
    spread = spread_gain * (at - dot(gram, mean, HIGHEST))
    ag[i] = spread[: ag.shape[1]]
    copies = []
    for d in range(1, nx):
        copy = pltpu.make_async_remote_copy(
            src_ref=ag.at[i], dst_ref=ag.at[i],
            send_sem=send2.at[d], recv_sem=recv2.at[d],
            device_id=(lax.rem(i + d, nx), j), device_id_type=MESH,
        )
        copy.start()
        copies.append(copy)
    lax.fori_loop(half, planes, move, 0)
    stores.append(
        pltpu.make_async_copy(moved.at[half:planes], base_hbm.at[half:planes], store_sem.at[1])
    )
    stores[1].start()
    for copy in copies:
        copy.wait()
    out_ref[...] = ag[...]
    for copy in stores:
        copy.wait()


def update_kernel(
    nx, info, spread_ref, meta_ref, wt_hi_hbm, wt_lo_hbm, base_hbm,
    out_hbm, moved, wt_hi, wt_lo, by_slot, sorted_s, right, num, weights, widen, sem,
):
    slots = spread_ref.shape[2]
    planes, tile_x, lanes = moved.shape
    base, count, group, blocks = block_tools(nx, lanes, info)
    load_h = pltpu.make_async_copy(wt_hi_hbm, wt_hi, sem.at[1])
    load_l = pltpu.make_async_copy(wt_lo_hbm, wt_lo, sem.at[2])
    load_s = pltpu.make_async_copy(base_hbm, moved, sem.at[0])
    load_h.start()
    load_l.start()
    load_s.start()

    def clear(b):
        where = pl.ds(pl.multiple_of(b * BLOCK, BLOCK), BLOCK)
        sorted_s[where, :] = jnp.full((BLOCK, lanes), -1.0, F32)

    for g in range(GROUPS):
        pl.when(count(g) > 0)(functools.partial(clear, base(g) + count(g) - 1))
    clear(blocks)
    wide = 3 * lanes
    for g in range(GROUPS):
        widen[g] = jnp.where(
            group_of(iota((lanes, wide), 1), g) == iota((lanes, wide), 0), 1.0, 0.0
        ).astype(BF16)
    num[...] = jnp.zeros(num.shape, F32)
    weights[...] = jnp.zeros(weights.shape, F32)

    pad = jnp.zeros((lanes - FEATURES, slots), F32)
    for k in range(nx):
        by_slot[k * slots : (k + 1) * slots, :] = jnp.concatenate(
            [spread_ref[k], meta_ref[k], pad], axis=0
        ).T

        def bring(n, carry):
            start = pl.multiple_of(k * slots + n * STEP, STEP)
            entries = [info[k, n * STEP + m] for m in range(STEP)]
            got = [by_slot[pl.ds(start + m, 1), :] for m in range(STEP)]
            for e, row in zip(entries, got):
                sorted_s[pl.ds(e & (CELLS - 1), 1), :] = row
            return carry

        lax.fori_loop(0, (info[nx + k, 0] + STEP - 1) // STEP, bring, 0)

    yy = iota((BLOCK, wide), 1) % 16
    load_h.wait()
    load_l.wait()

    right[...] = jnp.zeros(right.shape, BF16)

    def widened(b):
        where = pl.ds(pl.multiple_of(jnp.minimum(b, blocks) * BLOCK, BLOCK), BLOCK)
        value = sorted_s[where, :]
        y_here = value[:, 25:26].astype(I32)
        match = (value[:, 26:27] > 0.5) & (yy == y_here % 16)
        both = dot(jnp.concatenate(split(value), axis=0), widen[group(b)])
        s_hi = jnp.where(match, both[:BLOCK], 0.0).astype(BF16)
        s_lo = jnp.where(match, both[BLOCK:], 0.0).astype(BF16)
        ones = jnp.where(match[:, :lanes], 1.0, 0.0).astype(BF16)
        return s_hi, s_lo, ones

    def block_update(b, m):
        where = pl.ds(pl.multiple_of(jnp.maximum(b, 0) * BLOCK, BLOCK), BLOCK)
        w_hi, w_lo = wt_hi[:, where], wt_lo[:, where]
        return group(b), dot(jnp.concatenate([w_hi, w_hi, w_lo], axis=1), right[m])

    def two_blocks(n, carry):
        results = [block_update(2 * n - 2 + m, m) for m in range(2)]
        for m, (s_hi, s_lo, ones) in enumerate([widened(2 * n), widened(2 * n + 1)]):
            right[m, 0:BLOCK, :wide] = s_hi
            right[m, BLOCK : 2 * BLOCK, :wide] = s_lo
            right[m, 2 * BLOCK : 3 * BLOCK, :wide] = s_hi
            right[m, 0:BLOCK, wide:] = ones
            right[m, 2 * BLOCK : 3 * BLOCK, wide:] = ones
        for g, added in results:
            num[g] += added[:, :wide]
            weights[g] += added[:, wide:]
        return carry

    lax.fori_loop(0, (blocks + 1) // 2 + 1, two_blocks, 0)

    load_s.wait()
    chunk, parts = 8, 4
    length = tile_x // parts
    stores = []
    for part in range(parts):

        def finish(n, carry):
            here = pl.ds(pl.multiple_of(part * length + n * chunk, chunk), chunk)
            scale = [
                (time_step * nudge_gain) / jnp.maximum(weights[g, here, :], 1.0)
                for g in range(GROUPS)
            ]
            for v in range(3):
                gains = to_levels(
                    [num[g, here, v * lanes : (v + 1) * lanes] * scale[g] for g in range(GROUPS)]
                )
                for z in range(8):
                    moved[v * 8 + z, here, :] += gains[z]
            return carry

        lax.fori_loop(0, length // chunk, finish, 0)
        rows = pl.ds(part * length, length)
        stores.append(
            pltpu.make_async_copy(moved.at[:, rows, :], out_hbm.at[:, rows, :], sem.at[3 + part])
        )
        stores[-1].start()
    for copy in stores:
        copy.wait()


VM = pltpu.MemorySpace.VMEM


def vmem():
    return pl.BlockSpec(memory_space=VM)


def smem():
    return pl.BlockSpec(memory_space=pltpu.MemorySpace.SMEM)


def hbm():
    return pl.BlockSpec(memory_space=pl.ANY)


def gather_scratch(nx, slots, rows, cress_shape, grouped, lanes):
    across, tile_x = cress_shape
    return [
        pltpu.VMEM((across, 8, lanes), F32),
        pltpu.VMEM(grouped, BF16),
        pltpu.VMEM(grouped, BF16),
        pltpu.VMEM((rows + 8, 8, lanes), F32),
        pltpu.VMEM((2, 2 * BLOCK, 3 * lanes), BF16),
        pltpu.VMEM((2, BLOCK, lanes), F32),
        pltpu.VMEM((tile_x, rows), BF16),
        pltpu.VMEM((tile_x, rows), BF16),
        pltpu.VMEM((rows + 2 * BLOCK, lanes), F32),
        pltpu.VMEM((nx * slots, lanes), F32),
        pltpu.VMEM((GROUPS, 3 * lanes, lanes), BF16),
        pltpu.SemaphoreType.DMA((7,)),
    ]


def update_scratch(nx, slots, rows, grouped, planes, lanes):
    tile_x = grouped[1]
    return [
        pltpu.VMEM((planes, tile_x, lanes), F32),
        pltpu.VMEM((tile_x, rows), BF16),
        pltpu.VMEM((tile_x, rows), BF16),
        pltpu.VMEM((nx * slots, lanes), F32),
        pltpu.VMEM((rows + 8, lanes), F32),
        pltpu.VMEM((2, 3 * BLOCK, 4 * lanes), BF16),
        pltpu.VMEM(grouped, F32),
        pltpu.VMEM((GROUPS, tile_x, lanes), F32),
        pltpu.VMEM((GROUPS, lanes, 3 * lanes), BF16),
        pltpu.SemaphoreType.DMA((7,)),
    ]


def local(nx, ny, model_state, obs_val, obs_owner, obs_x, obs_y, cressman, vertical):
    fields, levels, tile_x, lanes = model_state.shape
    planes = fields * levels
    recs = obs_val.shape[0]
    cap = max(2, 2 * recs // ny)
    slots = ny * cap
    rows = (slots * nx // BLOCK + GROUPS + 1) * BLOCK
    state = model_state.reshape(planes, tile_x, lanes)
    vert = vertical.reshape(planes, vertical.shape[2])
    shape = jax.ShapeDtypeStruct
    dma = pltpu.SemaphoreType.DMA
    limit = 56 * 1024 * 1024

    grouped = (GROUPS, tile_x, fields * lanes)
    at, info, meta, xh, yh, st_hi, st_lo = pl.pallas_call(
        functools.partial(dispatch_kernel, nx, ny),
        out_shape=(
            shape((FEATURES, slots), F32),
            shape((2 * nx + GROUPS, slots), I32),
            shape((nx, 8, slots), F32),
            shape((2, planes, lanes), F32),
            shape((2 * planes, tile_x), F32),
            shape(grouped, BF16),
            shape(grouped, BF16),
        ),
        in_specs=[vmem()] * 5 + [hbm()],
        out_specs=[vmem()] * 5 + [hbm()] * 2,
        scratch_shapes=[
            pltpu.VMEM((planes, tile_x, lanes), F32),
            pltpu.VMEM(grouped, BF16),
            pltpu.VMEM(grouped, BF16),
            pltpu.VMEM((slots, lanes), F32),
            pltpu.VMEM((slots, lanes), F32),
            pltpu.VMEM((nx, 8, slots), F32),
            pltpu.VMEM((3, nx, slots), F32),
            pltpu.VMEM((2, planes, lanes), F32),
            pltpu.VMEM((2 * planes, tile_x), F32),
            pltpu.VMEM((2, planes, lanes), F32),
            pltpu.VMEM((2, 2 * planes, tile_x), F32),
            dma,
            dma((2,)),
            dma((ny,)),
            dma((ny,)),
            dma((nx,)),
            dma((nx,)),
            dma((4,)),
            dma((4,)),
        ],
        compiler_params=pltpu.CompilerParams(
            collective_id=0, has_side_effects=True, vmem_limit_bytes=limit
        ),
        name="dispatch",
    )(
        obs_val, obs_owner.reshape(1, recs), obs_x.reshape(1, recs), obs_y.reshape(1, recs),
        vert, state,
    )

    part, wt_hi, wt_lo = pl.pallas_call(
        functools.partial(gather_kernel, nx),
        out_shape=(
            shape((nx, FEATURES, slots), F32),
            shape((tile_x, rows), BF16),
            shape((tile_x, rows), BF16),
        ),
        in_specs=[smem()] + [hbm()] * 3,
        out_specs=[vmem()] + [hbm()] * 2,
        scratch_shapes=gather_scratch(nx, slots, rows, cressman.shape, grouped, lanes),
        compiler_params=pltpu.CompilerParams(vmem_limit_bytes=limit),
        name="column_sums",
    )(info, cressman, st_hi, st_lo)

    spread, base = pl.pallas_call(
        functools.partial(reduce_kernel, nx),
        out_shape=(shape((nx, planes, slots), F32), shape((planes, tile_x, lanes), F32)),
        in_specs=[vmem()] * 5 + [hbm()],
        out_specs=[vmem(), hbm()],
        scratch_shapes=[
            pltpu.VMEM((planes, tile_x + 16, lanes), F32),
            pltpu.VMEM((planes, tile_x, lanes), F32),
            pltpu.VMEM((nx, FEATURES, slots), F32),
            pltpu.VMEM((nx, planes, slots), F32),
            dma,
            dma((2,)),
            dma((nx,)),
            dma((nx,)),
            dma((nx,)),
            dma((nx,)),
        ],
        compiler_params=pltpu.CompilerParams(
            collective_id=1, has_side_effects=True, vmem_limit_bytes=limit
        ),
        name="innovations",
    )(part, at, vert, xh, yh, state)

    out = pl.pallas_call(
        functools.partial(update_kernel, nx),
        out_shape=shape((planes, tile_x, lanes), F32),
        in_specs=[smem()] + [vmem()] * 2 + [hbm()] * 3,
        out_specs=hbm(),
        scratch_shapes=update_scratch(nx, slots, rows, grouped, planes, lanes),
        compiler_params=pltpu.CompilerParams(vmem_limit_bytes=limit),
        name="update",
    )(info, spread, meta, wt_hi, wt_lo, base)
    return out.reshape(model_state.shape)


def solution(mesh):
    in_specs = (
        P(None, None, "gx", "gy"),
        P(("gx", "gy"), None),
        P(("gx", "gy"), None),
        P(("gx", "gy")),
        P(("gx", "gy")),
        P(None, "gx"),
        P(),
    )
    out_specs = P(None, None, "gx", "gy")
    return jax.shard_map(
        functools.partial(local, mesh.shape["gx"], mesh.shape["gy"]),
        mesh=mesh, in_specs=in_specs, out_specs=out_specs, check_vma=False,
    )
```

```python
import functools

import jax
import jax.numpy as jnp
from jax import lax
from jax.experimental import pallas as pl
from jax.experimental.pallas import tpu as pltpu
from jax.sharding import PartitionSpec as P

F32 = jnp.float32
BF16 = jnp.bfloat16
I32 = jnp.int32
HIGHEST = lax.Precision.HIGHEST
MESH = pl.DeviceIdType.MESH

advect_coef = 0.5
diffuse_h = 0.2
diffuse_z = 0.1
time_step = 0.5
nudge_gain = 1.0
spread_gain = 0.125

FEATURES = 32
GROUPS = 8
BLOCK = 128
CELLS = 4096
STEP = 32


def iota(shape, dim):
    return lax.broadcasted_iota(I32, shape, dim)


def dot(a, b, precision=None):
    return lax.dot_general(
        a, b, (((1,), (0,)), ((), ())), precision=precision, preferred_element_type=F32
    )


def dot_t(a, b, precision=None):
    return lax.dot_general(
        a, b, (((1,), (1,)), ((), ())), precision=precision, preferred_element_type=F32
    )


def split(value):
    high = value.astype(BF16)
    return high, (value - high.astype(F32)).astype(BF16)


def barrel(parts):
    block = iota(parts[0].shape, 1) // 16
    for bit in (1, 2, 4):
        upper = (block & bit) != 0
        parts = [jnp.where(upper, parts[(c + bit) % 8], parts[c]) for c in range(8)]
    return parts


def to_groups(parts):
    parts = barrel([pltpu.roll(p, 16 * z, 1) if z else p for z, p in enumerate(parts)])
    return [parts[-g % 8] for g in range(8)]


def to_levels(parts):
    parts = barrel(parts)
    return [
        pltpu.roll(parts[-z % 8], 128 - 16 * z, 1) if z else parts[0] for z in range(8)
    ]


def group_of(lane, g):
    return lane // 128 * 8 + (lane // 16 + 8 - g) % 8


def dispatch_kernel(
    nx, ny, obs_ref, owner_ref, x_ref, y_ref, vert_ref, state_hbm,
    info_ref, meta_ref, xh_ref, yh_ref, high_hbm, low_hbm,
    plane, st_hi, st_lo, sb, rb, mb, rows, xe, ye, xr, yr,
    load_sem, store_sem, s1_send, s1_recv, s2_send, s2_recv, h_send, h_recv,
):
    i, j = lax.axis_index("gx"), lax.axis_index("gy")
    planes, tile_x, lanes = plane.shape
    load = pltpu.make_async_copy(state_hbm, plane, load_sem)
    load.start()
    barrier = pltpu.get_barrier_semaphore()
    for d in range(1, ny):
        pl.semaphore_signal(
            barrier, inc=1, device_id=(i, lax.rem(j + d, ny)), device_id_type=MESH
        )
    for d in range(1, nx):
        pl.semaphore_signal(
            barrier, inc=1, device_id=(lax.rem(i + d, nx), j), device_id_type=MESH
        )

    recs = obs_ref.shape[0]
    slots = sb.shape[0]
    cap = slots // ny
    vert = vert_ref[...]
    var = iota((planes, lanes), 0) // 8
    basis = jnp.concatenate([jnp.where(var == v, vert, 0.0) for v in range(3)], axis=1)
    basis = jnp.concatenate([basis, jnp.zeros((lanes - planes, 3 * lanes), F32)], axis=0)
    payload = dot_t(obs_ref[...], basis, HIGHEST)
    eye = iota((recs, recs), 0) == iota((recs, recs), 1)
    x_col = jnp.sum(jnp.where(eye, x_ref[...].astype(F32), 0.0), axis=1, keepdims=True)
    y_col = jnp.sum(jnp.where(eye, y_ref[...].astype(F32), 0.0), axis=1, keepdims=True)
    lane = iota((recs, lanes), 1)
    payload = jnp.where(lane == 24, x_col, payload)
    payload = jnp.where(lane == 25, y_col, payload)
    payload = jnp.where(lane == 26, 1.0, payload)
    owner = jnp.sum(jnp.where(eye, owner_ref[...], 0), axis=1, keepdims=True)
    onehot = jnp.where(owner == lane, 1.0, 0.0)
    earlier = jnp.where(iota((recs, recs), 0) > iota((recs, recs), 1), 1.0, 0.0)
    rank = jnp.sum(dot(earlier, onehot) * onehot, axis=1, keepdims=True)
    slot = owner.astype(F32) * cap + rank
    slot_row = jnp.sum(jnp.where(eye, slot, 0.0), axis=0, keepdims=True).astype(I32)
    place = jnp.where(iota((slots, recs), 0) == slot_row, 1.0, 0.0)
    sb[...] = dot(place, payload, HIGHEST)

    pl.semaphore_wait(barrier, nx + ny - 2)
    first = []
    for d in range(1, ny):
        c = lax.rem(j + d, ny)
        copy = pltpu.make_async_remote_copy(
            src_ref=sb.at[pl.ds(pl.multiple_of(c * cap, cap), cap)],
            dst_ref=rb.at[pl.ds(pl.multiple_of(j * cap, cap), cap)],
            send_sem=s1_send.at[d], recv_sem=s1_recv.at[d],
            device_id=(i, c), device_id_type=MESH,
        )
        copy.start()
        first.append(copy)
    own = pl.ds(pl.multiple_of(j * cap, cap), cap)
    rb[own, :] = sb[own, :]

    load.wait()
    for k in range(planes):
        xe[0, k : k + 1, :] = plane[k, tile_x - 1 : tile_x, :]
        xe[1, k : k + 1, :] = plane[k, 0:1, :]
    edge_lane = iota((tile_x, lanes), 1)

    def gather_edges(k, edges):
        turned = pltpu.roll(plane[k], 2 * k + 1, 1)
        return jnp.where(edge_lane // 2 == k, turned, edges)

    edges = lax.fori_loop(0, planes, gather_edges, jnp.zeros((tile_x, lanes), F32))
    ye[...] = edges.T[: 2 * planes]
    halo = []
    for n, (src, dst, to) in enumerate((
        (xe.at[0], xr.at[0], (lax.rem(i + 1, nx), j)),
        (xe.at[1], xr.at[1], (lax.rem(i + nx - 1, nx), j)),
        (ye, yr.at[0], (i, lax.rem(j + 1, ny))),
        (ye, yr.at[1], (i, lax.rem(j + ny - 1, ny))),
    )):
        copy = pltpu.make_async_remote_copy(
            src_ref=src, dst_ref=dst, send_sem=h_send.at[n], recv_sem=h_recv.at[n],
            device_id=to, device_id_type=MESH,
        )
        copy.start()
        halo.append(copy)

    for copy in first:
        copy.wait()
    got = rb[...]
    got_t = got.T[:FEATURES]
    valid = got[:, 26:27]
    before = jnp.where(iota((slots, slots), 0) > iota((slots, slots), 1), 1.0, 0.0)
    rank = dot(before, jnp.broadcast_to(valid, (slots, lanes)))[:, 0:1]
    place = jnp.where(
        (iota((slots, slots), 1) == rank.astype(I32)) & (valid > 0.5), 1.0, 0.0
    )
    mb[i] = dot(got_t, place, HIGHEST)
    second = []
    for d in range(1, nx):
        copy = pltpu.make_async_remote_copy(
            src_ref=mb.at[i], dst_ref=mb.at[i],
            send_sem=s2_send.at[d], recv_sem=s2_recv.at[d],
            device_id=(lax.rem(i + d, nx), j), device_id_type=MESH,
        )
        copy.start()
        second.append(copy)
    chunk = 32

    def group_chunk(n, carry):
        here = pl.ds(pl.multiple_of(n * chunk, chunk), chunk)
        for v in range(3):
            parts = to_groups([plane[v * 8 + z, here, :] for z in range(8)])
            for g in range(GROUPS):
                high, low = split(parts[g])
                st_hi[g, here, v * lanes : (v + 1) * lanes] = high
                st_lo[g, here, v * lanes : (v + 1) * lanes] = low
        return carry

    lax.fori_loop(0, tile_x // chunk, group_chunk, 0)
    stores = [
        pltpu.make_async_copy(st_hi, high_hbm, store_sem.at[0]),
        pltpu.make_async_copy(st_lo, low_hbm, store_sem.at[1]),
    ]
    for copy in stores:
        copy.start()

    for copy in halo:
        copy.wait()
    xh_ref[0] = jnp.where(i > 0, xr[0], 0.0)
    xh_ref[1] = jnp.where(i < nx - 1, xr[1], 0.0)
    even = iota((2 * planes, tile_x), 0) % 2 == 0
    south = jnp.where(j > 0, yr[0], 0.0)
    north = jnp.where(j < ny - 1, yr[1], 0.0)
    yh_ref[...] = jnp.where(even, south, north)
    for copy in second:
        copy.wait()

    for k in range(nx):
        for f in range(3):
            rows[f, k : k + 1, :] = mb[k, 24 + f : 25 + f, :]
    y_cells = rows[1].astype(I32)
    valid = rows[2] > 0.5
    group = jnp.where(valid, y_cells // (lanes // GROUPS), GROUPS)
    masks = jnp.concatenate(
        [jnp.where(group == g, 1.0, 0.0) for g in range(GROUPS)], axis=0
    )
    lines = GROUPS * nx
    after = jnp.where(iota((slots, slots), 0) < iota((slots, slots), 1), 1.0, 0.0)
    rank = dot(masks, after)
    total = jnp.broadcast_to(jnp.sum(masks, axis=1, keepdims=True), (lines, lanes))
    line, other = iota((lines, lines), 0), iota((lines, lines), 1)
    same = line // nx == other // nx
    offset = dot(jnp.where(same & (other < line), 1.0, 0.0), total, HIGHEST)
    whole = dot(jnp.where(same, 1.0, 0.0), total, HIGHEST)
    count = (whole.astype(I32) + (BLOCK - 1)) // BLOCK
    base = dot(
        jnp.where((other // nx < line // nx) & (other % nx == 0), 1.0, 0.0),
        count.astype(F32),
        HIGHEST,
    )
    placed = masks * (base[:, 0:1] * BLOCK + offset[:, 0:1] + rank)
    pos = placed[0:nx]
    for g in range(1, GROUPS):
        pos = pos + placed[g * nx : (g + 1) * nx]
    dump = (slots * nx // BLOCK + GROUPS) * BLOCK
    info_ref[0:nx, :] = jnp.where(valid, pos.astype(I32), dump) + rows[0].astype(I32) * CELLS
    info_ref[nx : 2 * nx, :] = jnp.broadcast_to(
        jnp.sum(rows[2], axis=1, keepdims=True), (nx, slots)
    ).astype(I32)
    base = base.astype(I32)
    for g in range(GROUPS):
        info_ref[2 * nx + g : 2 * nx + g + 1, 0:lanes] = base[g * nx : g * nx + 1, :]
        info_ref[2 * nx + g : 2 * nx + g + 1, lanes : 2 * lanes] = count[g * nx : g * nx + 1, :]
    meta_ref[...] = mb[...]
    for copy in stores:
        copy.wait()


def block_tools(nx, lanes, info):
    def base(g):
        return info[2 * nx + g, 0]

    def count(g):
        return info[2 * nx + g, lanes]

    def group(b):
        found = 0
        for g in range(1, GROUPS):
            found = found + jnp.where(b >= base(g), 1, 0)
        return found

    return base, count, group, base(GROUPS - 1) + count(GROUPS - 1)


def gather_kernel(
    nx, info, meta_ref, cress_hbm, high_hbm, low_hbm, part_ref, values_ref, wt_hi_hbm, wt_lo_hbm,
    cress, st_hi, st_lo, sorted_w, wt_hi, wt_lo, by_slot, fold, sem,
):
    slots = info.shape[1]
    lanes = cress.shape[2]
    tile_x = cress_hbm.shape[1]
    pieces = tile_x // lanes
    base, count, group, blocks = block_tools(nx, lanes, info)
    loads = [
        pltpu.make_async_copy(
            cress_hbm.at[:, c * lanes : (c + 1) * lanes], cress.at[:, c, :], sem.at[c]
        )
        for c in range(pieces)
    ]
    state_loads = [
        pltpu.make_async_copy(high_hbm, st_hi, sem.at[3]),
        pltpu.make_async_copy(low_hbm, st_lo, sem.at[4]),
    ]
    for copy in loads + state_loads:
        copy.start()
    own_line = iota((8, lanes), 0) == pieces
    y_lane = FEATURES + 25
    blank = jnp.where(own_line & (iota((8, lanes), 1) == y_lane), -1.0, 0.0)

    def clear(b):
        where = pl.ds(pl.multiple_of(b * BLOCK, BLOCK), BLOCK)
        sorted_w[where] = jnp.broadcast_to(blank[None], (BLOCK, 8, lanes))

    for g in range(GROUPS):
        pl.when(count(g) > 0)(functools.partial(clear, base(g) + count(g) - 1))
    clear(blocks)
    part_ref[...] = jnp.zeros(part_ref.shape, F32)
    values_ref[...] = jnp.zeros(values_ref.shape, F32)
    wide = 3 * lanes
    for g in range(GROUPS):
        fold[g] = jnp.where(
            group_of(iota((wide, lanes), 0), g) == iota((wide, lanes), 1), 1.0, 0.0
        ).astype(BF16)
    above = jnp.zeros((FEATURES, slots), F32)
    below = jnp.zeros((lanes - 2 * FEATURES, slots), F32)
    for k in range(nx):
        by_slot[k * slots : (k + 1) * slots, :] = jnp.concatenate(
            [above, meta_ref[k], below], axis=0
        ).T

    for copy in loads:
        copy.wait()
    for k in range(nx):

        def bring(n, carry):
            start = pl.multiple_of(k * slots + n * STEP, STEP)
            entries = [info[k, n * STEP + m] for m in range(STEP)]
            for m, e in enumerate(entries):
                sorted_w[e & (CELLS - 1)] = jnp.where(
                    own_line,
                    by_slot[pl.ds(start + m, 1), :],
                    cress[lax.shift_right_logical(e, 12)],
                )
            return carry

        lax.fori_loop(0, (info[nx + k, 0] + STEP - 1) // STEP, bring, 0)

    for copy in state_loads:
        copy.wait()
    yy = (iota((BLOCK, wide), 1) % 16).astype(F32)
    lane = iota((BLOCK, lanes), 1)

    def block_sums(b):
        where = pl.ds(pl.multiple_of(b * BLOCK, BLOCK), BLOCK)
        g = group(b)
        parts = [sorted_w[where, c, :] for c in range(pieces)]
        own = sorted_w[where, pieces, :]
        high, low = split(jnp.concatenate(parts, axis=1))
        both = dot(jnp.concatenate([high, low], axis=0), st_hi[g])
        products = both[:BLOCK] + both[BLOCK:] + dot(high, st_lo[g])
        y_here = own[:, y_lane : y_lane + 1]
        y_here = y_here - jnp.floor(y_here * (1.0 / 16.0)) * 16.0
        valid = own[:, y_lane + 1 : y_lane + 2] > 0.5
        chosen = split(jnp.where(valid & (yy == y_here), products, 0.0))
        both = dot(jnp.concatenate(chosen, axis=0), fold[g])
        total = jnp.sum(parts[0] + parts[1] + parts[2], axis=1, keepdims=True)
        result = jnp.where(lane == 24, total, both[:BLOCK] + both[BLOCK:])
        result = jnp.where(lane < FEATURES, result, own).T
        return b, where, result, [split(part.T) for part in parts]

    per_device = part_ref.shape[2] // BLOCK

    def two_blocks(n, carry):
        for b, where, result, turned in [block_sums(2 * n), block_sums(2 * n + 1)]:
            k = b // per_device
            here = pl.ds(pl.multiple_of((b - k * per_device) * BLOCK, BLOCK), BLOCK)
            part_ref[k, :, here] = result[:FEATURES]
            values_ref[k, :, here] = result[FEATURES : 2 * FEATURES]
            for c in range(pieces):
                wt_hi[c * lanes : (c + 1) * lanes, where] = turned[c][0]
                wt_lo[c * lanes : (c + 1) * lanes, where] = turned[c][1]
        return carry

    lax.fori_loop(0, (blocks + 1) // 2, two_blocks, 0)
    stores = [
        pltpu.make_async_copy(wt_hi, wt_hi_hbm, sem.at[5]),
        pltpu.make_async_copy(wt_lo, wt_lo_hbm, sem.at[6]),
    ]
    for copy in stores:
        copy.start()
    for copy in stores:
        copy.wait()


def reduce_kernel(
    nx, part_ref, vert_ref, xh_ref, yh_ref, values_hbm, state_hbm, out_ref, base_hbm,
    plane, moved, rs, ag, values, load_sem, own_sem, store_sem, send1, recv1, send2, recv2,
):
    i, j = lax.axis_index("gx"), lax.axis_index("gy")
    planes, padded_x, lanes = plane.shape
    tile_x = padded_x - 16
    load = pltpu.make_async_copy(state_hbm, plane.at[:, 8 : 8 + tile_x, :], load_sem)
    load.start()
    own = pltpu.make_async_copy(values_hbm.at[i], values, own_sem)
    own.start()
    barrier = pltpu.get_barrier_semaphore()
    for d in range(1, nx):
        pl.semaphore_signal(
            barrier, inc=1, device_id=(lax.rem(i + d, nx), j), device_id_type=MESH
        )
    for k in range(planes):
        plane[k, 7:8, :] = xh_ref[0, k : k + 1, :]
        plane[k, 8 + tile_x : 9 + tile_x, :] = xh_ref[1, k : k + 1, :]
    beside = jnp.concatenate(
        [yh_ref[...], jnp.zeros((lanes - 2 * planes, tile_x), F32)], axis=0
    ).T
    beside_high, beside_low = split(beside)
    beside = jnp.where(
        iota((tile_x, lanes), 1) < lanes // 2,
        beside_high.astype(F32),
        pltpu.roll(beside_low.astype(F32), lanes // 2, 1),
    ).astype(BF16)
    near = time_step * diffuse_h
    wind = time_step * 0.5 * advect_coef
    own_part = 1.0 - time_step * (4.0 * diffuse_h + 2.0 * diffuse_z)
    here = pl.ds(8, tile_x)
    source, target = iota((lanes, 2 * lanes), 0), iota((lanes, 2 * lanes), 1)
    turn = (source == target + 1) | ((target >= lanes) & (source == target - lanes - 1))
    turn = jnp.where(turn, 1.0, 0.0).astype(BF16)

    def move(k, carry):
        z = k % 8
        center = plane[k, here, :]
        high, low = split(center)
        fill = ((source % (lanes // 2) == 2 * k + 1) & (target == lanes - 1)) | (
            (source % (lanes // 2) == 2 * k) & (target == lanes)
        )
        fill = jnp.where(fill, 1.0, 0.0).astype(BF16)
        sides = dot(
            jnp.concatenate([high, low, beside], axis=1),
            jnp.concatenate([turn, turn, fill], axis=0),
        )
        wind_u = wind * plane[z, here, :]
        wind_v = wind * plane[8 + z, here, :]
        upper = plane[k + jnp.where(z < 7, 1, 0), here, :]
        lower = plane[k - jnp.where(z > 0, 1, 0), here, :]
        moved[k] = (
            own_part * center
            + (near - wind_u) * plane[k, 9 : 9 + tile_x, :]
            + (near + wind_u) * plane[k, 7 : 7 + tile_x, :]
            + (near - wind_v) * sides[:, :lanes]
            + (near + wind_v) * sides[:, lanes:]
            + (time_step * diffuse_z) * (upper + lower)
        )
        return carry

    vert = jnp.concatenate([vert_ref[...], jnp.zeros((8, lanes), F32)], axis=0)
    same = iota((FEATURES, FEATURES), 0) // 8 == iota((FEATURES, FEATURES), 1) // 8
    gram = jnp.where(same, dot_t(vert, vert, HIGHEST), 0.0)
    own.wait()
    at = values[...]
    row = iota(at.shape, 0)

    pl.semaphore_wait(barrier, nx - 1)
    copies = []
    for d in range(1, nx):
        k = lax.rem(i + d, nx)
        copy = pltpu.make_async_remote_copy(
            src_ref=part_ref.at[k], dst_ref=rs.at[i],
            send_sem=send1.at[d], recv_sem=recv1.at[d],
            device_id=(k, j), device_id_type=MESH,
        )
        copy.start()
        copies.append(copy)
    rs[i] = part_ref[i]
    load.wait()
    half = planes // 2
    lax.fori_loop(0, half, move, 0)
    stores = [pltpu.make_async_copy(moved.at[0:half], base_hbm.at[0:half], store_sem.at[0])]
    stores[0].start()
    for copy in copies:
        copy.wait()
    total = rs[0]
    for k in range(1, nx):
        total = total + rs[k]
    weight = total[24:25, :]
    mean = jnp.where(row < 24, total / jnp.where(weight > 0.0, weight, 1.0), 0.0)
    spread = spread_gain * (at - dot(gram, mean, HIGHEST))
    ag[i] = spread[: ag.shape[1]]
    copies = []
    for d in range(1, nx):
        copy = pltpu.make_async_remote_copy(
            src_ref=ag.at[i], dst_ref=ag.at[i],
            send_sem=send2.at[d], recv_sem=recv2.at[d],
            device_id=(lax.rem(i + d, nx), j), device_id_type=MESH,
        )
        copy.start()
        copies.append(copy)
    lax.fori_loop(half, planes, move, 0)
    stores.append(
        pltpu.make_async_copy(moved.at[half:planes], base_hbm.at[half:planes], store_sem.at[1])
    )
    stores[1].start()
    for copy in copies:
        copy.wait()
    out_ref[...] = ag[...]
    for copy in stores:
        copy.wait()


def update_kernel(
    nx, info, spread_ref, values_ref, wt_hi_hbm, wt_lo_hbm, base_hbm,
    out_hbm, moved, wt_hi, wt_lo, right, num, weights, widen, sem,
):
    planes, tile_x, lanes = moved.shape
    base, count, group, blocks = block_tools(nx, lanes, info)
    load_h = pltpu.make_async_copy(wt_hi_hbm, wt_hi, sem.at[1])
    load_l = pltpu.make_async_copy(wt_lo_hbm, wt_lo, sem.at[2])
    load_s = pltpu.make_async_copy(base_hbm, moved, sem.at[0])
    load_h.start()
    load_l.start()
    load_s.start()

    wide = 3 * lanes
    for g in range(GROUPS):
        widen[g] = jnp.where(
            group_of(iota((lanes, wide), 1), g) == iota((lanes, wide), 0), 1.0, 0.0
        ).astype(BF16)
    num[...] = jnp.zeros(num.shape, F32)
    weights[...] = jnp.zeros(weights.shape, F32)

    yy = iota((BLOCK, wide), 1) % 16
    load_h.wait()
    load_l.wait()

    right[...] = jnp.zeros(right.shape, BF16)
    per_device = spread_ref.shape[2] // BLOCK
    pad = jnp.zeros((lanes - FEATURES, BLOCK), F32)

    def widened(b):
        b = jnp.minimum(b, blocks)
        k = b // per_device
        here = pl.ds(pl.multiple_of((b - k * per_device) * BLOCK, BLOCK), BLOCK)
        value = jnp.concatenate(
            [spread_ref[k, :, here], values_ref[k, planes:, here], pad], axis=0
        ).T
        y_here = value[:, 25:26].astype(I32)
        match = (value[:, 26:27] > 0.5) & (yy == y_here % 16)
        both = dot(jnp.concatenate(split(value), axis=0), widen[group(b)])
        s_hi = jnp.where(match, both[:BLOCK], 0.0).astype(BF16)
        s_lo = jnp.where(match, both[BLOCK:], 0.0).astype(BF16)
        ones = jnp.where(match[:, :lanes], 1.0, 0.0).astype(BF16)
        return s_hi, s_lo, ones

    def block_update(b, m):
        where = pl.ds(pl.multiple_of(jnp.maximum(b, 0) * BLOCK, BLOCK), BLOCK)
        w_hi, w_lo = wt_hi[:, where], wt_lo[:, where]
        return group(b), dot(jnp.concatenate([w_hi, w_hi, w_lo], axis=1), right[m])

    def two_blocks(n, carry):
        results = [block_update(2 * n - 2 + m, m) for m in range(2)]
        for m, (s_hi, s_lo, ones) in enumerate([widened(2 * n), widened(2 * n + 1)]):
            right[m, 0:BLOCK, :wide] = s_hi
            right[m, BLOCK : 2 * BLOCK, :wide] = s_lo
            right[m, 2 * BLOCK : 3 * BLOCK, :wide] = s_hi
            right[m, 0:BLOCK, wide:] = ones
            right[m, 2 * BLOCK : 3 * BLOCK, wide:] = ones
        for g, added in results:
            num[g] += added[:, :wide]
            weights[g] += added[:, wide:]
        return carry

    lax.fori_loop(0, (blocks + 1) // 2 + 1, two_blocks, 0)

    load_s.wait()
    chunk, parts = 8, 4
    length = tile_x // parts
    stores = []
    for part in range(parts):

        def finish(n, carry):
            here = pl.ds(pl.multiple_of(part * length + n * chunk, chunk), chunk)
            scale = [
                (time_step * nudge_gain) / jnp.maximum(weights[g, here, :], 1.0)
                for g in range(GROUPS)
            ]
            for v in range(3):
                gains = to_levels(
                    [num[g, here, v * lanes : (v + 1) * lanes] * scale[g] for g in range(GROUPS)]
                )
                for z in range(8):
                    moved[v * 8 + z, here, :] += gains[z]
            return carry

        lax.fori_loop(0, length // chunk, finish, 0)
        rows = pl.ds(part * length, length)
        stores.append(
            pltpu.make_async_copy(moved.at[:, rows, :], out_hbm.at[:, rows, :], sem.at[3 + part])
        )
        stores[-1].start()
    for copy in stores:
        copy.wait()


VM = pltpu.MemorySpace.VMEM


def vmem():
    return pl.BlockSpec(memory_space=VM)


def smem():
    return pl.BlockSpec(memory_space=pltpu.MemorySpace.SMEM)


def hbm():
    return pl.BlockSpec(memory_space=pl.ANY)


def gather_scratch(nx, slots, rows, cress_shape, grouped, lanes):
    across, tile_x = cress_shape
    return [
        pltpu.VMEM((across, 8, lanes), F32),
        pltpu.VMEM(grouped, BF16),
        pltpu.VMEM(grouped, BF16),
        pltpu.VMEM((rows + 8, 8, lanes), F32),
        pltpu.VMEM((tile_x, rows), BF16),
        pltpu.VMEM((tile_x, rows), BF16),
        pltpu.VMEM((nx * slots, lanes), F32),
        pltpu.VMEM((GROUPS, 3 * lanes, lanes), BF16),
        pltpu.SemaphoreType.DMA((7,)),
    ]


def update_scratch(nx, slots, rows, grouped, planes, lanes):
    tile_x = grouped[1]
    return [
        pltpu.VMEM((planes, tile_x, lanes), F32),
        pltpu.VMEM((tile_x, rows), BF16),
        pltpu.VMEM((tile_x, rows), BF16),
        pltpu.VMEM((2, 3 * BLOCK, 4 * lanes), BF16),
        pltpu.VMEM(grouped, F32),
        pltpu.VMEM((GROUPS, tile_x, lanes), F32),
        pltpu.VMEM((GROUPS, lanes, 3 * lanes), BF16),
        pltpu.SemaphoreType.DMA((7,)),
    ]


def local(nx, ny, model_state, obs_val, obs_owner, obs_x, obs_y, cressman, vertical):
    fields, levels, tile_x, lanes = model_state.shape
    planes = fields * levels
    recs = obs_val.shape[0]
    cap = max(2, 2 * recs // ny)
    slots = ny * cap
    rows = (slots * nx // BLOCK + GROUPS) * BLOCK
    chunk = rows // nx
    state = model_state.reshape(planes, tile_x, lanes)
    vert = vertical.reshape(planes, vertical.shape[2])
    shape = jax.ShapeDtypeStruct
    dma = pltpu.SemaphoreType.DMA
    limit = 56 * 1024 * 1024

    grouped = (GROUPS, tile_x, fields * lanes)
    info, meta, xh, yh, st_hi, st_lo = pl.pallas_call(
        functools.partial(dispatch_kernel, nx, ny),
        out_shape=(
            shape((2 * nx + GROUPS, slots), I32),
            shape((nx, FEATURES, slots), F32),
            shape((2, planes, lanes), F32),
            shape((2 * planes, tile_x), F32),
            shape(grouped, BF16),
            shape(grouped, BF16),
        ),
        in_specs=[vmem()] * 5 + [hbm()],
        out_specs=[vmem()] * 4 + [hbm()] * 2,
        scratch_shapes=[
            pltpu.VMEM((planes, tile_x, lanes), F32),
            pltpu.VMEM(grouped, BF16),
            pltpu.VMEM(grouped, BF16),
            pltpu.VMEM((slots, lanes), F32),
            pltpu.VMEM((slots, lanes), F32),
            pltpu.VMEM((nx, FEATURES, slots), F32),
            pltpu.VMEM((3, nx, slots), F32),
            pltpu.VMEM((2, planes, lanes), F32),
            pltpu.VMEM((2 * planes, tile_x), F32),
            pltpu.VMEM((2, planes, lanes), F32),
            pltpu.VMEM((2, 2 * planes, tile_x), F32),
            dma,
            dma((2,)),
            dma((ny,)),
            dma((ny,)),
            dma((nx,)),
            dma((nx,)),
            dma((4,)),
            dma((4,)),
        ],
        compiler_params=pltpu.CompilerParams(
            collective_id=0, has_side_effects=True, vmem_limit_bytes=limit
        ),
        name="dispatch",
    )(
        obs_val, obs_owner.reshape(1, recs), obs_x.reshape(1, recs), obs_y.reshape(1, recs),
        vert, state,
    )

    part, values, wt_hi, wt_lo = pl.pallas_call(
        functools.partial(gather_kernel, nx),
        out_shape=(
            shape((nx, FEATURES, chunk), F32),
            shape((nx, FEATURES, chunk), F32),
            shape((tile_x, rows), BF16),
            shape((tile_x, rows), BF16),
        ),
        in_specs=[smem(), vmem()] + [hbm()] * 3,
        out_specs=[vmem()] * 2 + [hbm()] * 2,
        scratch_shapes=gather_scratch(nx, slots, rows, cressman.shape, grouped, lanes),
        compiler_params=pltpu.CompilerParams(vmem_limit_bytes=limit),
        name="column_sums",
    )(info, meta, cressman, st_hi, st_lo)

    spread, base = pl.pallas_call(
        functools.partial(reduce_kernel, nx),
        out_shape=(shape((nx, planes, chunk), F32), shape((planes, tile_x, lanes), F32)),
        in_specs=[vmem()] * 4 + [hbm()] * 2,
        out_specs=[vmem(), hbm()],
        scratch_shapes=[
            pltpu.VMEM((planes, tile_x + 16, lanes), F32),
            pltpu.VMEM((planes, tile_x, lanes), F32),
            pltpu.VMEM((nx, FEATURES, chunk), F32),
            pltpu.VMEM((nx, planes, chunk), F32),
            pltpu.VMEM((FEATURES, chunk), F32),
            dma,
            dma,
            dma((2,)),
            dma((nx,)),
            dma((nx,)),
            dma((nx,)),
            dma((nx,)),
        ],
        compiler_params=pltpu.CompilerParams(
            collective_id=1, has_side_effects=True, vmem_limit_bytes=limit
        ),
        name="innovations",
    )(part, vert, xh, yh, values, state)

    out = pl.pallas_call(
        functools.partial(update_kernel, nx),
        out_shape=shape((planes, tile_x, lanes), F32),
        in_specs=[smem()] + [vmem()] * 2 + [hbm()] * 3,
        out_specs=hbm(),
        scratch_shapes=update_scratch(nx, slots, rows, grouped, planes, lanes),
        compiler_params=pltpu.CompilerParams(vmem_limit_bytes=limit),
        name="update",
    )(info, spread, values, wt_hi, wt_lo, base)
    return out.reshape(model_state.shape)


def solution(mesh):
    in_specs = (
        P(None, None, "gx", "gy"),
        P(("gx", "gy"), None),
        P(("gx", "gy"), None),
        P(("gx", "gy")),
        P(("gx", "gy")),
        P(None, "gx"),
        P(),
    )
    out_specs = P(None, None, "gx", "gy")
    return jax.shard_map(
        functools.partial(local, mesh.shape["gx"], mesh.shape["gy"]),
        mesh=mesh, in_specs=in_specs, out_specs=out_specs, check_vma=False,
    )
```

```python
import functools

import jax
import jax.numpy as jnp
from jax import lax
from jax.experimental import pallas as pl
from jax.experimental.pallas import tpu as pltpu
from jax.sharding import PartitionSpec as P

F32 = jnp.float32
BF16 = jnp.bfloat16
I32 = jnp.int32
HIGHEST = lax.Precision.HIGHEST
MESH = pl.DeviceIdType.MESH

advect_coef = 0.5
diffuse_h = 0.2
diffuse_z = 0.1
time_step = 0.5
nudge_gain = 1.0
spread_gain = 0.125

FEATURES = 32
GROUPS = 8
BLOCK = 128
CELLS = 4096
STEP = 32


def iota(shape, dim):
    return lax.broadcasted_iota(I32, shape, dim)


def dot(a, b, precision=None):
    return lax.dot_general(
        a, b, (((1,), (0,)), ((), ())), precision=precision, preferred_element_type=F32
    )


def dot_t(a, b, precision=None):
    return lax.dot_general(
        a, b, (((1,), (1,)), ((), ())), precision=precision, preferred_element_type=F32
    )


def split(value):
    high = value.astype(BF16)
    return high, (value - high.astype(F32)).astype(BF16)


def barrel(parts):
    block = iota(parts[0].shape, 1) // 16
    for bit in (1, 2, 4):
        upper = (block & bit) != 0
        parts = [jnp.where(upper, parts[(c + bit) % 8], parts[c]) for c in range(8)]
    return parts


def to_groups(parts):
    parts = barrel([pltpu.roll(p, 16 * z, 1) if z else p for z, p in enumerate(parts)])
    return [parts[-g % 8] for g in range(8)]


def to_levels(parts):
    parts = barrel(parts)
    return [
        pltpu.roll(parts[-z % 8], 128 - 16 * z, 1) if z else parts[0] for z in range(8)
    ]


def group_of(lane, g):
    return lane // 128 * 8 + (lane // 16 + 8 - g) % 8


def dispatch_kernel(
    nx, ny, obs_ref, owner_ref, x_ref, y_ref, vert_ref, state_hbm,
    info_ref, meta_ref, xh_ref, yh_ref, high_hbm, low_hbm,
    plane, st_hi, st_lo, sb, rb, mb, rows, xe, ye, xr, yr,
    load_sem, store_sem, s1_send, s1_recv, s2_send, s2_recv, h_send, h_recv,
):
    i, j = lax.axis_index("gx"), lax.axis_index("gy")
    planes, tile_x, lanes = plane.shape
    load = pltpu.make_async_copy(state_hbm, plane, load_sem)
    load.start()
    barrier = pltpu.get_barrier_semaphore()
    for d in range(1, ny):
        pl.semaphore_signal(
            barrier, inc=1, device_id=(i, lax.rem(j + d, ny)), device_id_type=MESH
        )
    for d in range(1, nx):
        pl.semaphore_signal(
            barrier, inc=1, device_id=(lax.rem(i + d, nx), j), device_id_type=MESH
        )

    recs = obs_ref.shape[0]
    slots = sb.shape[0]
    cap = slots // ny
    vert = vert_ref[...]
    var = iota((planes, lanes), 0) // 8
    basis = jnp.concatenate([jnp.where(var == v, vert, 0.0) for v in range(3)], axis=1)
    basis = jnp.concatenate([basis, jnp.zeros((lanes - planes, 3 * lanes), F32)], axis=0)
    payload = dot_t(obs_ref[...], basis, HIGHEST)
    eye = iota((recs, recs), 0) == iota((recs, recs), 1)
    x_col = jnp.sum(jnp.where(eye, x_ref[...].astype(F32), 0.0), axis=1, keepdims=True)
    y_col = jnp.sum(jnp.where(eye, y_ref[...].astype(F32), 0.0), axis=1, keepdims=True)
    lane = iota((recs, lanes), 1)
    payload = jnp.where(lane == 24, x_col, payload)
    payload = jnp.where(lane == 25, y_col, payload)
    payload = jnp.where(lane == 26, 1.0, payload)
    owner = jnp.sum(jnp.where(eye, owner_ref[...], 0), axis=1, keepdims=True)
    onehot = jnp.where(owner == lane, 1.0, 0.0)
    earlier = jnp.where(iota((recs, recs), 0) > iota((recs, recs), 1), 1.0, 0.0)
    rank = jnp.sum(dot(earlier, onehot) * onehot, axis=1, keepdims=True)
    slot = owner.astype(F32) * cap + rank
    slot_row = jnp.sum(jnp.where(eye, slot, 0.0), axis=0, keepdims=True).astype(I32)
    place = jnp.where(iota((slots, recs), 0) == slot_row, 1.0, 0.0)
    sb[...] = dot(place, payload, HIGHEST)

    pl.semaphore_wait(barrier, nx + ny - 2)
    first = []
    for d in range(1, ny):
        c = lax.rem(j + d, ny)
        copy = pltpu.make_async_remote_copy(
            src_ref=sb.at[pl.ds(pl.multiple_of(c * cap, cap), cap)],
            dst_ref=rb.at[pl.ds(pl.multiple_of(j * cap, cap), cap)],
            send_sem=s1_send.at[d], recv_sem=s1_recv.at[d],
            device_id=(i, c), device_id_type=MESH,
        )
        copy.start()
        first.append(copy)
    own = pl.ds(pl.multiple_of(j * cap, cap), cap)
    rb[own, :] = sb[own, :]

    load.wait()
    for k in range(planes):
        xe[0, k : k + 1, :] = plane[k, tile_x - 1 : tile_x, :]
        xe[1, k : k + 1, :] = plane[k, 0:1, :]
    edge_lane = iota((tile_x, lanes), 1)

    def gather_edges(k, edges):
        turned = pltpu.roll(plane[k], 2 * k + 1, 1)
        return jnp.where(edge_lane // 2 == k, turned, edges)

    edges = lax.fori_loop(0, planes, gather_edges, jnp.zeros((tile_x, lanes), F32))
    ye[...] = edges.T[: 2 * planes]
    halo = []
    for n, (src, dst, to) in enumerate((
        (xe.at[0], xr.at[0], (lax.rem(i + 1, nx), j)),
        (xe.at[1], xr.at[1], (lax.rem(i + nx - 1, nx), j)),
        (ye, yr.at[0], (i, lax.rem(j + 1, ny))),
        (ye, yr.at[1], (i, lax.rem(j + ny - 1, ny))),
    )):
        copy = pltpu.make_async_remote_copy(
            src_ref=src, dst_ref=dst, send_sem=h_send.at[n], recv_sem=h_recv.at[n],
            device_id=to, device_id_type=MESH,
        )
        copy.start()
        halo.append(copy)

    for copy in first:
        copy.wait()
    got = rb[...]
    got_t = got.T[:FEATURES]
    valid = got[:, 26:27]
    before = jnp.where(iota((slots, slots), 0) > iota((slots, slots), 1), 1.0, 0.0)
    rank = dot(before, jnp.broadcast_to(valid, (slots, lanes)))[:, 0:1]
    place = jnp.where(
        (iota((slots, slots), 1) == rank.astype(I32)) & (valid > 0.5), 1.0, 0.0
    )
    mb[i] = dot(got_t, place, HIGHEST)
    second = []
    for d in range(1, nx):
        copy = pltpu.make_async_remote_copy(
            src_ref=mb.at[i], dst_ref=mb.at[i],
            send_sem=s2_send.at[d], recv_sem=s2_recv.at[d],
            device_id=(lax.rem(i + d, nx), j), device_id_type=MESH,
        )
        copy.start()
        second.append(copy)
    chunk = 32

    def group_chunk(n, carry):
        here = pl.ds(pl.multiple_of(n * chunk, chunk), chunk)
        for v in range(3):
            parts = to_groups([plane[v * 8 + z, here, :] for z in range(8)])
            for g in range(GROUPS):
                high, low = split(parts[g])
                st_hi[g, here, v * lanes : (v + 1) * lanes] = high
                st_lo[g, here, v * lanes : (v + 1) * lanes] = low
        return carry

    lax.fori_loop(0, tile_x // chunk, group_chunk, 0)
    stores = [
        pltpu.make_async_copy(st_hi, high_hbm, store_sem.at[0]),
        pltpu.make_async_copy(st_lo, low_hbm, store_sem.at[1]),
    ]
    for copy in stores:
        copy.start()

    for copy in halo:
        copy.wait()
    xh_ref[0] = jnp.where(i > 0, xr[0], 0.0)
    xh_ref[1] = jnp.where(i < nx - 1, xr[1], 0.0)
    even = iota((2 * planes, tile_x), 0) % 2 == 0
    south = jnp.where(j > 0, yr[0], 0.0)
    north = jnp.where(j < ny - 1, yr[1], 0.0)
    yh_ref[...] = jnp.where(even, south, north)
    for copy in second:
        copy.wait()

    for k in range(nx):
        for f in range(3):
            rows[f, k : k + 1, :] = mb[k, 24 + f : 25 + f, :]
    y_cells = rows[1].astype(I32)
    valid = rows[2] > 0.5
    group = jnp.where(valid, y_cells // (lanes // GROUPS), GROUPS)
    masks = jnp.concatenate(
        [jnp.where(group == g, 1.0, 0.0) for g in range(GROUPS)], axis=0
    )
    lines = GROUPS * nx
    after = jnp.where(iota((slots, slots), 0) < iota((slots, slots), 1), 1.0, 0.0)
    rank = dot(masks, after)
    total = jnp.broadcast_to(jnp.sum(masks, axis=1, keepdims=True), (lines, lanes))
    line, other = iota((lines, lines), 0), iota((lines, lines), 1)
    same = line // nx == other // nx
    offset = dot(jnp.where(same & (other < line), 1.0, 0.0), total, HIGHEST)
    whole = dot(jnp.where(same, 1.0, 0.0), total, HIGHEST)
    count = (whole.astype(I32) + (BLOCK - 1)) // BLOCK
    base = dot(
        jnp.where((other // nx < line // nx) & (other % nx == 0), 1.0, 0.0),
        count.astype(F32),
        HIGHEST,
    )
    placed = masks * (base[:, 0:1] * BLOCK + offset[:, 0:1] + rank)
    pos = placed[0:nx]
    for g in range(1, GROUPS):
        pos = pos + placed[g * nx : (g + 1) * nx]
    dump = (slots * nx // BLOCK + GROUPS) * BLOCK
    info_ref[0:nx, :] = jnp.where(valid, pos.astype(I32), dump) + rows[0].astype(I32) * CELLS
    info_ref[nx : 2 * nx, :] = jnp.broadcast_to(
        jnp.sum(rows[2], axis=1, keepdims=True), (nx, slots)
    ).astype(I32)
    base = base.astype(I32)
    for g in range(GROUPS):
        info_ref[2 * nx + g : 2 * nx + g + 1, 0:lanes] = base[g * nx : g * nx + 1, :]
        info_ref[2 * nx + g : 2 * nx + g + 1, lanes : 2 * lanes] = count[g * nx : g * nx + 1, :]
    meta_ref[...] = mb[...]
    for copy in stores:
        copy.wait()


def block_tools(nx, lanes, info):
    def base(g):
        return info[2 * nx + g, 0]

    def count(g):
        return info[2 * nx + g, lanes]

    def group(b):
        found = 0
        for g in range(1, GROUPS):
            found = found + jnp.where(b >= base(g), 1, 0)
        return found

    return base, count, group, base(GROUPS - 1) + count(GROUPS - 1)


def gather_kernel(
    nx, info, meta_ref, cress_hbm, high_hbm, low_hbm, part_ref, values_ref, wt_hi_hbm, wt_lo_hbm,
    cress, st_hi, st_lo, sorted_w, wt_hi, wt_lo, by_slot, fold, sem,
):
    slots = info.shape[1]
    lanes = cress.shape[2]
    tile_x = cress_hbm.shape[1]
    pieces = tile_x // lanes
    base, count, group, blocks = block_tools(nx, lanes, info)
    loads = [
        pltpu.make_async_copy(
            cress_hbm.at[:, c * lanes : (c + 1) * lanes], cress.at[:, c, :], sem.at[c]
        )
        for c in range(pieces)
    ]
    state_loads = [
        pltpu.make_async_copy(high_hbm, st_hi, sem.at[3]),
        pltpu.make_async_copy(low_hbm, st_lo, sem.at[4]),
    ]
    for copy in loads + state_loads:
        copy.start()
    own_line = iota((8, lanes), 0) == pieces
    y_lane = FEATURES + 25
    blank = jnp.where(own_line & (iota((8, lanes), 1) == y_lane), -1.0, 0.0)

    def clear(b):
        where = pl.ds(pl.multiple_of(b * BLOCK, BLOCK), BLOCK)
        sorted_w[where] = jnp.broadcast_to(blank[None], (BLOCK, 8, lanes))

    for g in range(GROUPS):
        pl.when(count(g) > 0)(functools.partial(clear, base(g) + count(g) - 1))
    clear(blocks)
    part_ref[...] = jnp.zeros(part_ref.shape, F32)
    values_ref[...] = jnp.zeros(values_ref.shape, F32)
    wide = 3 * lanes
    for g in range(GROUPS):
        fold[g] = jnp.where(
            group_of(iota((wide, lanes), 0), g) == iota((wide, lanes), 1), 1.0, 0.0
        ).astype(BF16)
    above = jnp.zeros((FEATURES, slots), F32)
    below = jnp.zeros((lanes - 2 * FEATURES, slots), F32)
    y_row = iota((FEATURES, slots), 0) == 25
    for k in range(nx):
        own = meta_ref[k]
        cell = own - jnp.floor(own * (1.0 / 16.0)) * 16.0
        by_slot[k * slots : (k + 1) * slots, :] = jnp.concatenate(
            [above, jnp.where(y_row, cell, own), below], axis=0
        ).T

    for copy in loads:
        copy.wait()
    for k in range(nx):

        def bring(n, carry):
            start = pl.multiple_of(k * slots + n * STEP, STEP)
            entries = [info[k, n * STEP + m] for m in range(STEP)]
            for m, e in enumerate(entries):
                sorted_w[e & (CELLS - 1)] = jnp.where(
                    own_line,
                    by_slot[pl.ds(start + m, 1), :],
                    cress[lax.shift_right_logical(e, 12)],
                )
            return carry

        lax.fori_loop(0, (info[nx + k, 0] + STEP - 1) // STEP, bring, 0)

    for copy in state_loads:
        copy.wait()
    yy = (iota((BLOCK, wide), 1) % 16).astype(F32)
    lane = iota((BLOCK, lanes), 1)

    def block_sums(b):
        where = pl.ds(pl.multiple_of(b * BLOCK, BLOCK), BLOCK)
        g = group(b)
        parts = [sorted_w[where, c, :] for c in range(pieces)]
        own = sorted_w[where, pieces, :]
        high, low = split(jnp.concatenate(parts, axis=1))
        s_hi, s_lo = st_hi[g], st_lo[g]
        products = dot(
            jnp.concatenate([high, low, high], axis=1), jnp.concatenate([s_hi, s_hi, s_lo], axis=0)
        )
        chosen = split(jnp.where(yy == own[:, y_lane : y_lane + 1], products, 0.0))
        both = dot(jnp.concatenate(chosen, axis=0), fold[g])
        total = jnp.sum(parts[0] + parts[1] + parts[2], axis=1, keepdims=True)
        result = jnp.where(lane == 24, total, both[:BLOCK] + both[BLOCK:])
        result = jnp.where(lane < FEATURES, result, own).T
        return b, where, result, [split(part.T) for part in parts]

    per_device = part_ref.shape[2] // BLOCK

    def four_blocks(n, carry):
        for b, where, result, turned in [
            block_sums(jnp.minimum(4 * n + m, blocks)) for m in range(4)
        ]:
            k = b // per_device
            here = pl.ds(pl.multiple_of((b - k * per_device) * BLOCK, BLOCK), BLOCK)
            part_ref[k, :, here] = result[:FEATURES]
            values_ref[k, :, here] = result[FEATURES : 2 * FEATURES]
            for c in range(pieces):
                wt_hi[c * lanes : (c + 1) * lanes, where] = turned[c][0]
                wt_lo[c * lanes : (c + 1) * lanes, where] = turned[c][1]
        return carry

    lax.fori_loop(0, (blocks + 3) // 4, four_blocks, 0)
    stores = [
        pltpu.make_async_copy(wt_hi, wt_hi_hbm, sem.at[5]),
        pltpu.make_async_copy(wt_lo, wt_lo_hbm, sem.at[6]),
    ]
    for copy in stores:
        copy.start()
    for copy in stores:
        copy.wait()


def reduce_kernel(
    nx, part_ref, vert_ref, xh_ref, yh_ref, values_hbm, state_hbm, out_ref, base_hbm,
    plane, moved, rs, ag, values, load_sem, own_sem, store_sem, send1, recv1, send2, recv2,
):
    i, j = lax.axis_index("gx"), lax.axis_index("gy")
    planes, padded_x, lanes = plane.shape
    tile_x = padded_x - 16
    load = pltpu.make_async_copy(state_hbm, plane.at[:, 8 : 8 + tile_x, :], load_sem)
    load.start()
    own = pltpu.make_async_copy(values_hbm.at[i], values, own_sem)
    own.start()
    barrier = pltpu.get_barrier_semaphore()
    for d in range(1, nx):
        pl.semaphore_signal(
            barrier, inc=1, device_id=(lax.rem(i + d, nx), j), device_id_type=MESH
        )
    for k in range(planes):
        plane[k, 7:8, :] = xh_ref[0, k : k + 1, :]
        plane[k, 8 + tile_x : 9 + tile_x, :] = xh_ref[1, k : k + 1, :]
    beside = jnp.concatenate(
        [yh_ref[...], jnp.zeros((lanes - 2 * planes, tile_x), F32)], axis=0
    ).T
    beside_high, beside_low = split(beside)
    beside = jnp.where(
        iota((tile_x, lanes), 1) < lanes // 2,
        beside_high.astype(F32),
        pltpu.roll(beside_low.astype(F32), lanes // 2, 1),
    ).astype(BF16)
    near = time_step * diffuse_h
    wind = time_step * 0.5 * advect_coef
    own_part = 1.0 - time_step * (4.0 * diffuse_h + 2.0 * diffuse_z)
    here = pl.ds(8, tile_x)
    source, target = iota((lanes, 2 * lanes), 0), iota((lanes, 2 * lanes), 1)
    turn = (source == target + 1) | ((target >= lanes) & (source == target - lanes - 1))
    turn = jnp.where(turn, 1.0, 0.0).astype(BF16)

    def move(k, carry):
        z = k % 8
        center = plane[k, here, :]
        high, low = split(center)
        fill = ((source % (lanes // 2) == 2 * k + 1) & (target == lanes - 1)) | (
            (source % (lanes // 2) == 2 * k) & (target == lanes)
        )
        fill = jnp.where(fill, 1.0, 0.0).astype(BF16)
        sides = dot(
            jnp.concatenate([high, low, beside], axis=1),
            jnp.concatenate([turn, turn, fill], axis=0),
        )
        wind_u = wind * plane[z, here, :]
        wind_v = wind * plane[8 + z, here, :]
        upper = plane[k + jnp.where(z < 7, 1, 0), here, :]
        lower = plane[k - jnp.where(z > 0, 1, 0), here, :]
        moved[k] = (
            own_part * center
            + (near - wind_u) * plane[k, 9 : 9 + tile_x, :]
            + (near + wind_u) * plane[k, 7 : 7 + tile_x, :]
            + (near - wind_v) * sides[:, :lanes]
            + (near + wind_v) * sides[:, lanes:]
            + (time_step * diffuse_z) * (upper + lower)
        )
        return carry

    vert = jnp.concatenate([vert_ref[...], jnp.zeros((8, lanes), F32)], axis=0)
    same = iota((FEATURES, FEATURES), 0) // 8 == iota((FEATURES, FEATURES), 1) // 8
    gram = jnp.where(same, dot_t(vert, vert, HIGHEST), 0.0)
    own.wait()
    at = values[...]
    row = iota(at.shape, 0)

    pl.semaphore_wait(barrier, nx - 1)
    copies = []
    for d in range(1, nx):
        k = lax.rem(i + d, nx)
        copy = pltpu.make_async_remote_copy(
            src_ref=part_ref.at[k], dst_ref=rs.at[i],
            send_sem=send1.at[d], recv_sem=recv1.at[d],
            device_id=(k, j), device_id_type=MESH,
        )
        copy.start()
        copies.append(copy)
    rs[i] = part_ref[i]
    load.wait()
    half = planes // 2
    lax.fori_loop(0, half, move, 0)
    stores = [pltpu.make_async_copy(moved.at[0:half], base_hbm.at[0:half], store_sem.at[0])]
    stores[0].start()
    for copy in copies:
        copy.wait()
    total = rs[0]
    for k in range(1, nx):
        total = total + rs[k]
    weight = total[24:25, :]
    mean = jnp.where(row < 24, total / jnp.where(weight > 0.0, weight, 1.0), 0.0)
    spread = spread_gain * (at - dot(gram, mean, HIGHEST))
    ag[i] = spread[: ag.shape[1]]
    copies = []
    for d in range(1, nx):
        copy = pltpu.make_async_remote_copy(
            src_ref=ag.at[i], dst_ref=ag.at[i],
            send_sem=send2.at[d], recv_sem=recv2.at[d],
            device_id=(lax.rem(i + d, nx), j), device_id_type=MESH,
        )
        copy.start()
        copies.append(copy)
    lax.fori_loop(half, planes, move, 0)
    stores.append(
        pltpu.make_async_copy(moved.at[half:planes], base_hbm.at[half:planes], store_sem.at[1])
    )
    stores[1].start()
    for copy in copies:
        copy.wait()
    out_ref[...] = ag[...]
    for copy in stores:
        copy.wait()


def update_kernel(
    nx, info, spread_ref, values_ref, wt_hi_hbm, wt_lo_hbm, base_hbm,
    out_hbm, moved, wt_hi, wt_lo, right, num, weights, widen, sem,
):
    planes, tile_x, lanes = moved.shape
    base, count, group, blocks = block_tools(nx, lanes, info)
    load_h = pltpu.make_async_copy(wt_hi_hbm, wt_hi, sem.at[1])
    load_l = pltpu.make_async_copy(wt_lo_hbm, wt_lo, sem.at[2])
    load_s = pltpu.make_async_copy(base_hbm, moved, sem.at[0])
    load_h.start()
    load_l.start()
    load_s.start()

    wide = 3 * lanes
    for g in range(GROUPS):
        widen[g] = jnp.where(
            group_of(iota((lanes, wide), 1), g) == iota((lanes, wide), 0), 1.0, 0.0
        ).astype(BF16)
    num[...] = jnp.zeros(num.shape, F32)
    weights[...] = jnp.zeros(weights.shape, F32)

    yy = (iota((BLOCK, wide), 1) % 16).astype(F32)
    load_h.wait()
    load_l.wait()

    right[...] = jnp.zeros(right.shape, BF16)
    per_device = spread_ref.shape[2] // BLOCK
    pad = jnp.zeros((lanes - FEATURES, BLOCK), F32)

    def widened(b):
        b = jnp.minimum(b, blocks)
        k = b // per_device
        here = pl.ds(pl.multiple_of((b - k * per_device) * BLOCK, BLOCK), BLOCK)
        value = jnp.concatenate(
            [spread_ref[k, :, here], values_ref[k, planes:, here], pad], axis=0
        ).T
        match = yy == value[:, 25:26]
        both = dot(jnp.concatenate(split(value), axis=0), widen[group(b)])
        s_hi = jnp.where(match, both[:BLOCK], 0.0).astype(BF16)
        s_lo = jnp.where(match, both[BLOCK:], 0.0).astype(BF16)
        ones = jnp.where(match[:, :lanes], 1.0, 0.0).astype(BF16)
        return s_hi, s_lo, ones

    def block_update(b, m):
        where = pl.ds(pl.multiple_of(jnp.maximum(b, 0) * BLOCK, BLOCK), BLOCK)
        w_hi, w_lo = wt_hi[:, where], wt_lo[:, where]
        return group(b), dot(jnp.concatenate([w_hi, w_hi, w_lo], axis=1), right[m])

    def two_blocks(n, carry):
        results = [block_update(2 * n - 2 + m, m) for m in range(2)]
        for m, (s_hi, s_lo, ones) in enumerate([widened(2 * n), widened(2 * n + 1)]):
            right[m, 0:BLOCK, :wide] = s_hi
            right[m, BLOCK : 2 * BLOCK, :wide] = s_lo
            right[m, 2 * BLOCK : 3 * BLOCK, :wide] = s_hi
            right[m, 0:BLOCK, wide:] = ones
            right[m, 2 * BLOCK : 3 * BLOCK, wide:] = ones
        for g, added in results:
            num[g] += added[:, :wide]
            weights[g] += added[:, wide:]
        return carry

    lax.fori_loop(0, (blocks + 1) // 2 + 1, two_blocks, 0)

    load_s.wait()
    chunk, parts = 32, 4
    length = tile_x // parts
    stores = []
    for part in range(parts):

        def finish(n, carry):
            here = pl.ds(pl.multiple_of(part * length + n * chunk, chunk), chunk)
            scale = [
                (time_step * nudge_gain) / jnp.maximum(weights[g, here, :], 1.0)
                for g in range(GROUPS)
            ]
            for v in range(3):
                gains = to_levels(
                    [num[g, here, v * lanes : (v + 1) * lanes] * scale[g] for g in range(GROUPS)]
                )
                for z in range(8):
                    moved[v * 8 + z, here, :] += gains[z]
            return carry

        lax.fori_loop(0, length // chunk, finish, 0)
        rows = pl.ds(part * length, length)
        stores.append(
            pltpu.make_async_copy(moved.at[:, rows, :], out_hbm.at[:, rows, :], sem.at[3 + part])
        )
        stores[-1].start()
    for copy in stores:
        copy.wait()


VM = pltpu.MemorySpace.VMEM


def vmem():
    return pl.BlockSpec(memory_space=VM)


def smem():
    return pl.BlockSpec(memory_space=pltpu.MemorySpace.SMEM)


def hbm():
    return pl.BlockSpec(memory_space=pl.ANY)


def gather_scratch(nx, slots, rows, cress_shape, grouped, lanes):
    across, tile_x = cress_shape
    return [
        pltpu.VMEM((across, 8, lanes), F32),
        pltpu.VMEM(grouped, BF16),
        pltpu.VMEM(grouped, BF16),
        pltpu.VMEM((rows + 8, 8, lanes), F32),
        pltpu.VMEM((tile_x, rows), BF16),
        pltpu.VMEM((tile_x, rows), BF16),
        pltpu.VMEM((nx * slots, lanes), F32),
        pltpu.VMEM((GROUPS, 3 * lanes, lanes), BF16),
        pltpu.SemaphoreType.DMA((7,)),
    ]


def update_scratch(nx, slots, rows, grouped, planes, lanes):
    tile_x = grouped[1]
    return [
        pltpu.VMEM((planes, tile_x, lanes), F32),
        pltpu.VMEM((tile_x, rows), BF16),
        pltpu.VMEM((tile_x, rows), BF16),
        pltpu.VMEM((2, 3 * BLOCK, 4 * lanes), BF16),
        pltpu.VMEM(grouped, F32),
        pltpu.VMEM((GROUPS, tile_x, lanes), F32),
        pltpu.VMEM((GROUPS, lanes, 3 * lanes), BF16),
        pltpu.SemaphoreType.DMA((7,)),
    ]


def local(nx, ny, model_state, obs_val, obs_owner, obs_x, obs_y, cressman, vertical):
    fields, levels, tile_x, lanes = model_state.shape
    planes = fields * levels
    recs = obs_val.shape[0]
    cap = max(2, 2 * recs // ny)
    slots = ny * cap
    rows = (slots * nx // BLOCK + GROUPS) * BLOCK
    chunk = rows // nx
    state = model_state.reshape(planes, tile_x, lanes)
    vert = vertical.reshape(planes, vertical.shape[2])
    shape = jax.ShapeDtypeStruct
    dma = pltpu.SemaphoreType.DMA
    limit = 56 * 1024 * 1024

    grouped = (GROUPS, tile_x, fields * lanes)
    info, meta, xh, yh, st_hi, st_lo = pl.pallas_call(
        functools.partial(dispatch_kernel, nx, ny),
        out_shape=(
            shape((2 * nx + GROUPS, slots), I32),
            shape((nx, FEATURES, slots), F32),
            shape((2, planes, lanes), F32),
            shape((2 * planes, tile_x), F32),
            shape(grouped, BF16),
            shape(grouped, BF16),
        ),
        in_specs=[vmem()] * 5 + [hbm()],
        out_specs=[vmem()] * 4 + [hbm()] * 2,
        scratch_shapes=[
            pltpu.VMEM((planes, tile_x, lanes), F32),
            pltpu.VMEM(grouped, BF16),
            pltpu.VMEM(grouped, BF16),
            pltpu.VMEM((slots, lanes), F32),
            pltpu.VMEM((slots, lanes), F32),
            pltpu.VMEM((nx, FEATURES, slots), F32),
            pltpu.VMEM((3, nx, slots), F32),
            pltpu.VMEM((2, planes, lanes), F32),
            pltpu.VMEM((2 * planes, tile_x), F32),
            pltpu.VMEM((2, planes, lanes), F32),
            pltpu.VMEM((2, 2 * planes, tile_x), F32),
            dma,
            dma((2,)),
            dma((ny,)),
            dma((ny,)),
            dma((nx,)),
            dma((nx,)),
            dma((4,)),
            dma((4,)),
        ],
        compiler_params=pltpu.CompilerParams(
            collective_id=0, has_side_effects=True, vmem_limit_bytes=limit
        ),
        name="dispatch",
    )(
        obs_val, obs_owner.reshape(1, recs), obs_x.reshape(1, recs), obs_y.reshape(1, recs),
        vert, state,
    )

    part, values, wt_hi, wt_lo = pl.pallas_call(
        functools.partial(gather_kernel, nx),
        out_shape=(
            shape((nx, FEATURES, chunk), F32),
            shape((nx, FEATURES, chunk), F32),
            shape((tile_x, rows), BF16),
            shape((tile_x, rows), BF16),
        ),
        in_specs=[smem(), vmem()] + [hbm()] * 3,
        out_specs=[vmem()] * 2 + [hbm()] * 2,
        scratch_shapes=gather_scratch(nx, slots, rows, cressman.shape, grouped, lanes),
        compiler_params=pltpu.CompilerParams(vmem_limit_bytes=limit),
        name="column_sums",
    )(info, meta, cressman, st_hi, st_lo)

    spread, base = pl.pallas_call(
        functools.partial(reduce_kernel, nx),
        out_shape=(shape((nx, planes, chunk), F32), shape((planes, tile_x, lanes), F32)),
        in_specs=[vmem()] * 4 + [hbm()] * 2,
        out_specs=[vmem(), hbm()],
        scratch_shapes=[
            pltpu.VMEM((planes, tile_x + 16, lanes), F32),
            pltpu.VMEM((planes, tile_x, lanes), F32),
            pltpu.VMEM((nx, FEATURES, chunk), F32),
            pltpu.VMEM((nx, planes, chunk), F32),
            pltpu.VMEM((FEATURES, chunk), F32),
            dma,
            dma,
            dma((2,)),
            dma((nx,)),
            dma((nx,)),
            dma((nx,)),
            dma((nx,)),
        ],
        compiler_params=pltpu.CompilerParams(
            collective_id=1, has_side_effects=True, vmem_limit_bytes=limit
        ),
        name="innovations",
    )(part, vert, xh, yh, values, state)

    out = pl.pallas_call(
        functools.partial(update_kernel, nx),
        out_shape=shape((planes, tile_x, lanes), F32),
        in_specs=[smem()] + [vmem()] * 2 + [hbm()] * 3,
        out_specs=hbm(),
        scratch_shapes=update_scratch(nx, slots, rows, grouped, planes, lanes),
        compiler_params=pltpu.CompilerParams(vmem_limit_bytes=limit),
        name="update",
    )(info, spread, values, wt_hi, wt_lo, base)
    return out.reshape(model_state.shape)


def solution(mesh):
    in_specs = (
        P(None, None, "gx", "gy"),
        P(("gx", "gy"), None),
        P(("gx", "gy"), None),
        P(("gx", "gy")),
        P(("gx", "gy")),
        P(None, "gx"),
        P(),
    )
    out_specs = P(None, None, "gx", "gy")
    return jax.shard_map(
        functools.partial(local, mesh.shape["gx"], mesh.shape["gy"]),
        mesh=mesh, in_specs=in_specs, out_specs=out_specs, check_vma=False,
    )
```

```python
import functools

import jax
import jax.numpy as jnp
from jax import lax
from jax.experimental import pallas as pl
from jax.experimental.pallas import tpu as pltpu
from jax.sharding import PartitionSpec as P

F32 = jnp.float32
BF16 = jnp.bfloat16
I32 = jnp.int32
HIGHEST = lax.Precision.HIGHEST
MESH = pl.DeviceIdType.MESH

advect_coef = 0.5
diffuse_h = 0.2
diffuse_z = 0.1
time_step = 0.5
nudge_gain = 1.0
spread_gain = 0.125

FEATURES = 32
GROUPS = 8
BLOCK = 128
CELLS = 4096
STEP = 32


def iota(shape, dim):
    return lax.broadcasted_iota(I32, shape, dim)


def dot(a, b, precision=None):
    return lax.dot_general(
        a, b, (((1,), (0,)), ((), ())), precision=precision, preferred_element_type=F32
    )


def dot_t(a, b, precision=None):
    return lax.dot_general(
        a, b, (((1,), (1,)), ((), ())), precision=precision, preferred_element_type=F32
    )


def split(value):
    high = value.astype(BF16)
    return high, (value - high.astype(F32)).astype(BF16)


def barrel(parts):
    block = iota(parts[0].shape, 1) // 16
    for bit in (1, 2, 4):
        upper = (block & bit) != 0
        parts = [jnp.where(upper, parts[(c + bit) % 8], parts[c]) for c in range(8)]
    return parts


def to_groups(parts):
    parts = barrel([pltpu.roll(p, 16 * z, 1) if z else p for z, p in enumerate(parts)])
    return [parts[-g % 8] for g in range(8)]


def to_levels(parts):
    parts = barrel(parts)
    return [
        pltpu.roll(parts[-z % 8], 128 - 16 * z, 1) if z else parts[0] for z in range(8)
    ]


def group_of(lane, g):
    return lane // 128 * 8 + (lane // 16 + 8 - g) % 8


def dispatch_kernel(
    nx, ny, obs_ref, owner_ref, x_ref, y_ref, vert_ref, state_hbm,
    info_ref, meta_ref, xh_ref, yh_ref, high_hbm, low_hbm,
    plane, st_hi, st_lo, sb, rb, mb, rows, xe, ye, xr, yr,
    load_sem, store_sem, s1_send, s1_recv, s2_send, s2_recv, h_send, h_recv,
):
    i, j = lax.axis_index("gx"), lax.axis_index("gy")
    planes, tile_x, lanes = plane.shape
    load = pltpu.make_async_copy(state_hbm, plane, load_sem)
    load.start()
    barrier = pltpu.get_barrier_semaphore()
    for d in range(1, ny):
        pl.semaphore_signal(
            barrier, inc=1, device_id=(i, lax.rem(j + d, ny)), device_id_type=MESH
        )
    for d in range(1, nx):
        pl.semaphore_signal(
            barrier, inc=1, device_id=(lax.rem(i + d, nx), j), device_id_type=MESH
        )

    recs = obs_ref.shape[0]
    slots = sb.shape[0]
    cap = slots // ny
    vert = vert_ref[...]
    var = iota((planes, lanes), 0) // 8
    basis = jnp.concatenate([jnp.where(var == v, vert, 0.0) for v in range(3)], axis=1)
    basis = jnp.concatenate([basis, jnp.zeros((lanes - planes, 3 * lanes), F32)], axis=0)
    payload = dot_t(obs_ref[...], basis, HIGHEST)
    eye = iota((recs, recs), 0) == iota((recs, recs), 1)
    x_col = jnp.sum(jnp.where(eye, x_ref[...].astype(F32), 0.0), axis=1, keepdims=True)
    y_col = jnp.sum(jnp.where(eye, y_ref[...].astype(F32), 0.0), axis=1, keepdims=True)
    lane = iota((recs, lanes), 1)
    payload = jnp.where(lane == 24, x_col, payload)
    payload = jnp.where(lane == 25, y_col, payload)
    payload = jnp.where(lane == 26, 1.0, payload)
    owner = jnp.sum(jnp.where(eye, owner_ref[...], 0), axis=1, keepdims=True)
    onehot = jnp.where(owner == lane, 1.0, 0.0)
    earlier = jnp.where(iota((recs, recs), 0) > iota((recs, recs), 1), 1.0, 0.0)
    rank = jnp.sum(dot(earlier, onehot) * onehot, axis=1, keepdims=True)
    slot = owner.astype(F32) * cap + rank
    slot_row = jnp.sum(jnp.where(eye, slot, 0.0), axis=0, keepdims=True).astype(I32)
    place = jnp.where(iota((slots, recs), 0) == slot_row, 1.0, 0.0)
    sb[...] = dot(place, payload, HIGHEST)

    pl.semaphore_wait(barrier, nx + ny - 2)
    first = []
    for d in range(1, ny):
        c = lax.rem(j + d, ny)
        copy = pltpu.make_async_remote_copy(
            src_ref=sb.at[pl.ds(pl.multiple_of(c * cap, cap), cap)],
            dst_ref=rb.at[pl.ds(pl.multiple_of(j * cap, cap), cap)],
            send_sem=s1_send.at[d], recv_sem=s1_recv.at[d],
            device_id=(i, c), device_id_type=MESH,
        )
        copy.start()
        first.append(copy)
    own = pl.ds(pl.multiple_of(j * cap, cap), cap)
    rb[own, :] = sb[own, :]

    load.wait()
    for k in range(planes):
        xe[0, k : k + 1, :] = plane[k, tile_x - 1 : tile_x, :]
        xe[1, k : k + 1, :] = plane[k, 0:1, :]
    edge_lane = iota((tile_x, lanes), 1)

    def gather_edges(k, edges):
        turned = pltpu.roll(plane[k], 2 * k + 1, 1)
        return jnp.where(edge_lane // 2 == k, turned, edges)

    edges = lax.fori_loop(0, planes, gather_edges, jnp.zeros((tile_x, lanes), F32))
    ye[...] = edges.T[: 2 * planes]
    halo = []
    for n, (src, dst, to) in enumerate((
        (xe.at[0], xr.at[0], (lax.rem(i + 1, nx), j)),
        (xe.at[1], xr.at[1], (lax.rem(i + nx - 1, nx), j)),
        (ye, yr.at[0], (i, lax.rem(j + 1, ny))),
        (ye, yr.at[1], (i, lax.rem(j + ny - 1, ny))),
    )):
        copy = pltpu.make_async_remote_copy(
            src_ref=src, dst_ref=dst, send_sem=h_send.at[n], recv_sem=h_recv.at[n],
            device_id=to, device_id_type=MESH,
        )
        copy.start()
        halo.append(copy)

    for copy in first:
        copy.wait()
    got = rb[...]
    got_t = got.T[:FEATURES]
    valid = got[:, 26:27]
    before = jnp.where(iota((slots, slots), 0) > iota((slots, slots), 1), 1.0, 0.0)
    rank = dot(before, jnp.broadcast_to(valid, (slots, lanes)))[:, 0:1]
    place = jnp.where(
        (iota((slots, slots), 1) == rank.astype(I32)) & (valid > 0.5), 1.0, 0.0
    )
    mb[i] = dot(got_t, place, HIGHEST)
    second = []
    for d in range(1, nx):
        copy = pltpu.make_async_remote_copy(
            src_ref=mb.at[i], dst_ref=mb.at[i],
            send_sem=s2_send.at[d], recv_sem=s2_recv.at[d],
            device_id=(lax.rem(i + d, nx), j), device_id_type=MESH,
        )
        copy.start()
        second.append(copy)
    chunk = 32

    def group_chunk(n, carry):
        here = pl.ds(pl.multiple_of(n * chunk, chunk), chunk)
        for v in range(3):
            parts = to_groups([plane[v * 8 + z, here, :] for z in range(8)])
            for g in range(GROUPS):
                high, low = split(parts[g])
                st_hi[g, here, v * lanes : (v + 1) * lanes] = high
                st_lo[g, here, v * lanes : (v + 1) * lanes] = low
        return carry

    lax.fori_loop(0, tile_x // chunk, group_chunk, 0)
    stores = [
        pltpu.make_async_copy(st_hi, high_hbm, store_sem.at[0]),
        pltpu.make_async_copy(st_lo, low_hbm, store_sem.at[1]),
    ]
    for copy in stores:
        copy.start()

    for copy in halo:
        copy.wait()
    xh_ref[0] = jnp.where(i > 0, xr[0], 0.0)
    xh_ref[1] = jnp.where(i < nx - 1, xr[1], 0.0)
    even = iota((2 * planes, tile_x), 0) % 2 == 0
    south = jnp.where(j > 0, yr[0], 0.0)
    north = jnp.where(j < ny - 1, yr[1], 0.0)
    yh_ref[...] = jnp.where(even, south, north)
    for copy in second:
        copy.wait()

    for k in range(nx):
        for f in range(3):
            rows[f, k : k + 1, :] = mb[k, 24 + f : 25 + f, :]
    y_cells = rows[1].astype(I32)
    valid = rows[2] > 0.5
    group = jnp.where(valid, y_cells // (lanes // GROUPS), GROUPS)
    masks = jnp.concatenate(
        [jnp.where(group == g, 1.0, 0.0) for g in range(GROUPS)], axis=0
    )
    lines = GROUPS * nx
    after = jnp.where(iota((slots, slots), 0) < iota((slots, slots), 1), 1.0, 0.0)
    rank = dot(masks, after)
    total = jnp.broadcast_to(jnp.sum(masks, axis=1, keepdims=True), (lines, lanes))
    line, other = iota((lines, lines), 0), iota((lines, lines), 1)
    same = line // nx == other // nx
    offset = dot(jnp.where(same & (other < line), 1.0, 0.0), total, HIGHEST)
    whole = dot(jnp.where(same, 1.0, 0.0), total, HIGHEST)
    count = (whole.astype(I32) + (BLOCK - 1)) // BLOCK
    base = dot(
        jnp.where((other // nx < line // nx) & (other % nx == 0), 1.0, 0.0),
        count.astype(F32),
        HIGHEST,
    )
    placed = masks * (base[:, 0:1] * BLOCK + offset[:, 0:1] + rank)
    pos = placed[0:nx]
    for g in range(1, GROUPS):
        pos = pos + placed[g * nx : (g + 1) * nx]
    dump = (slots * nx // BLOCK + GROUPS) * BLOCK
    info_ref[0:nx, :] = jnp.where(valid, pos.astype(I32), dump) + rows[0].astype(I32) * CELLS
    info_ref[nx : 2 * nx, :] = jnp.broadcast_to(
        jnp.sum(rows[2], axis=1, keepdims=True), (nx, slots)
    ).astype(I32)
    base = base.astype(I32)
    for g in range(GROUPS):
        info_ref[2 * nx + g : 2 * nx + g + 1, 0:lanes] = base[g * nx : g * nx + 1, :]
        info_ref[2 * nx + g : 2 * nx + g + 1, lanes : 2 * lanes] = count[g * nx : g * nx + 1, :]
    meta_ref[...] = mb[...]
    for copy in stores:
        copy.wait()


def block_tools(nx, lanes, info):
    def base(g):
        return info[2 * nx + g, 0]

    def count(g):
        return info[2 * nx + g, lanes]

    def group(b):
        found = 0
        for g in range(1, GROUPS):
            found = found + jnp.where(b >= base(g), 1, 0)
        return found

    return base, count, group, base(GROUPS - 1) + count(GROUPS - 1)


def gather_kernel(
    nx, info, meta_ref, cress_hbm, high_hbm, low_hbm, part_ref, values_ref, wt_hi_hbm, wt_lo_hbm,
    cress, st_hi, st_lo, sorted_w, wt_hi, wt_lo, by_slot, fold, sem,
):
    slots = info.shape[1]
    lanes = cress.shape[2]
    tile_x = cress_hbm.shape[1]
    pieces = tile_x // lanes
    base, count, group, blocks = block_tools(nx, lanes, info)
    loads = [
        pltpu.make_async_copy(
            cress_hbm.at[:, c * lanes : (c + 1) * lanes], cress.at[:, c, :], sem.at[c]
        )
        for c in range(pieces)
    ]
    state_loads = [
        pltpu.make_async_copy(high_hbm, st_hi, sem.at[3]),
        pltpu.make_async_copy(low_hbm, st_lo, sem.at[4]),
    ]
    for copy in loads + state_loads:
        copy.start()
    own_line = iota((8, lanes), 0) == pieces
    y_lane = FEATURES + 25
    blank = jnp.where(own_line & (iota((8, lanes), 1) == y_lane), -1.0, 0.0)

    def clear(b):
        where = pl.ds(pl.multiple_of(b * BLOCK, BLOCK), BLOCK)
        sorted_w[where] = jnp.broadcast_to(blank[None], (BLOCK, 8, lanes))

    for g in range(GROUPS):
        pl.when(count(g) > 0)(functools.partial(clear, base(g) + count(g) - 1))
    clear(blocks)
    part_ref[...] = jnp.zeros(part_ref.shape, F32)
    values_ref[...] = jnp.zeros(values_ref.shape, F32)
    wide = 3 * lanes
    for g in range(GROUPS):
        fold[g] = jnp.where(
            group_of(iota((wide, lanes), 0), g) == iota((wide, lanes), 1), 1.0, 0.0
        ).astype(BF16)
    above = jnp.zeros((FEATURES, slots), F32)
    below = jnp.zeros((lanes - 2 * FEATURES, slots), F32)
    y_row = iota((FEATURES, slots), 0) == 25
    for k in range(nx):
        own = meta_ref[k]
        cell = own - jnp.floor(own * (1.0 / 16.0)) * 16.0
        by_slot[k * slots : (k + 1) * slots, :] = jnp.concatenate(
            [above, jnp.where(y_row, cell, own), below], axis=0
        ).T

    for copy in loads:
        copy.wait()
    for k in range(nx):

        def bring(n, carry):
            start = pl.multiple_of(k * slots + n * STEP, STEP)
            entries = [info[k, n * STEP + m] for m in range(STEP)]
            for m, e in enumerate(entries):
                sorted_w[e & (CELLS - 1)] = jnp.where(
                    own_line,
                    by_slot[pl.ds(start + m, 1), :],
                    cress[lax.shift_right_logical(e, 12)],
                )
            return carry

        lax.fori_loop(0, (info[nx + k, 0] + STEP - 1) // STEP, bring, 0)

    for copy in state_loads:
        copy.wait()
    yy = (iota((BLOCK, wide), 1) % 16).astype(F32)
    lane = iota((BLOCK, lanes), 1)

    def block_sums(b):
        where = pl.ds(pl.multiple_of(b * BLOCK, BLOCK), BLOCK)
        g = group(b)
        parts = [sorted_w[where, c, :] for c in range(pieces)]
        own = sorted_w[where, pieces, :]
        high, low = split(jnp.concatenate(parts, axis=1))
        s_hi, s_lo = st_hi[g], st_lo[g]
        products = dot(
            jnp.concatenate([high, low, high], axis=1), jnp.concatenate([s_hi, s_hi, s_lo], axis=0)
        )
        chosen = split(jnp.where(yy == own[:, y_lane : y_lane + 1], products, 0.0))
        both = dot(jnp.concatenate(chosen, axis=0), fold[g])
        total = jnp.sum(parts[0] + parts[1] + parts[2], axis=1, keepdims=True)
        result = jnp.where(lane == 24, total, both[:BLOCK] + both[BLOCK:])
        result = jnp.where(lane < FEATURES, result, own).T
        return b, where, result, [
            (high[:, c * lanes : (c + 1) * lanes].T, low[:, c * lanes : (c + 1) * lanes].T)
            for c in range(pieces)
        ]

    per_device = part_ref.shape[2] // BLOCK

    def stores(n):
        here = pl.ds(pl.multiple_of(n * 4 * BLOCK, 4 * BLOCK), 4 * BLOCK)
        return [
            pltpu.make_async_copy(wt_hi.at[:, here], wt_hi_hbm.at[:, here], sem.at[5 + 2 * n]),
            pltpu.make_async_copy(wt_lo.at[:, here], wt_lo_hbm.at[:, here], sem.at[6 + 2 * n]),
        ]

    def four_blocks(n, carry):
        for b, where, result, turned in [
            block_sums(jnp.minimum(4 * n + m, blocks)) for m in range(4)
        ]:
            k = b // per_device
            here = pl.ds(pl.multiple_of((b - k * per_device) * BLOCK, BLOCK), BLOCK)
            part_ref[k, :, here] = result[:FEATURES]
            values_ref[k, :, here] = result[FEATURES : 2 * FEATURES]
            for c in range(pieces):
                wt_hi[c * lanes : (c + 1) * lanes, where] = turned[c][0]
                wt_lo[c * lanes : (c + 1) * lanes, where] = turned[c][1]
        for copy in stores(n):
            copy.start()
        return carry

    steps = jnp.maximum((blocks + 3) // 4, 1)
    lax.fori_loop(0, steps, four_blocks, 0)

    def done(n, carry):
        for copy in stores(n):
            copy.wait()
        return carry

    lax.fori_loop(0, steps, done, 0)


def reduce_kernel(
    nx, part_ref, vert_ref, xh_ref, yh_ref, values_hbm, state_hbm, out_ref, base_hbm,
    plane, moved, rs, ag, values, load_sem, own_sem, store_sem, send1, recv1, send2, recv2,
):
    i, j = lax.axis_index("gx"), lax.axis_index("gy")
    planes, padded_x, lanes = plane.shape
    tile_x = padded_x - 16
    load = pltpu.make_async_copy(state_hbm, plane.at[:, 8 : 8 + tile_x, :], load_sem)
    load.start()
    own = pltpu.make_async_copy(values_hbm.at[i], values, own_sem)
    own.start()
    barrier = pltpu.get_barrier_semaphore()
    for d in range(1, nx):
        pl.semaphore_signal(
            barrier, inc=1, device_id=(lax.rem(i + d, nx), j), device_id_type=MESH
        )
    for k in range(planes):
        plane[k, 7:8, :] = xh_ref[0, k : k + 1, :]
        plane[k, 8 + tile_x : 9 + tile_x, :] = xh_ref[1, k : k + 1, :]
    beside = jnp.concatenate(
        [yh_ref[...], jnp.zeros((lanes - 2 * planes, tile_x), F32)], axis=0
    ).T
    beside_high, beside_low = split(beside)
    beside = jnp.where(
        iota((tile_x, lanes), 1) < lanes // 2,
        beside_high.astype(F32),
        pltpu.roll(beside_low.astype(F32), lanes // 2, 1),
    ).astype(BF16)
    near = time_step * diffuse_h
    wind = time_step * 0.5 * advect_coef
    own_part = 1.0 - time_step * (4.0 * diffuse_h + 2.0 * diffuse_z)
    here = pl.ds(8, tile_x)
    source, target = iota((lanes, 2 * lanes), 0), iota((lanes, 2 * lanes), 1)
    turn = (source == target + 1) | ((target >= lanes) & (source == target - lanes - 1))
    turn = jnp.where(turn, 1.0, 0.0).astype(BF16)

    def move(k, carry):
        z = k % 8
        center = plane[k, here, :]
        high, low = split(center)
        fill = ((source % (lanes // 2) == 2 * k + 1) & (target == lanes - 1)) | (
            (source % (lanes // 2) == 2 * k) & (target == lanes)
        )
        fill = jnp.where(fill, 1.0, 0.0).astype(BF16)
        sides = dot(
            jnp.concatenate([high, low, beside], axis=1),
            jnp.concatenate([turn, turn, fill], axis=0),
        )
        wind_u = wind * plane[z, here, :]
        wind_v = wind * plane[8 + z, here, :]
        upper = plane[k + jnp.where(z < 7, 1, 0), here, :]
        lower = plane[k - jnp.where(z > 0, 1, 0), here, :]
        moved[k] = (
            own_part * center
            + (near - wind_u) * plane[k, 9 : 9 + tile_x, :]
            + (near + wind_u) * plane[k, 7 : 7 + tile_x, :]
            + (near - wind_v) * sides[:, :lanes]
            + (near + wind_v) * sides[:, lanes:]
            + (time_step * diffuse_z) * (upper + lower)
        )
        return carry

    vert = jnp.concatenate([vert_ref[...], jnp.zeros((8, lanes), F32)], axis=0)
    same = iota((FEATURES, FEATURES), 0) // 8 == iota((FEATURES, FEATURES), 1) // 8
    gram = jnp.where(same, dot_t(vert, vert, HIGHEST), 0.0)
    own.wait()
    at = values[...]
    row = iota(at.shape, 0)

    pl.semaphore_wait(barrier, nx - 1)
    copies = []
    for d in range(1, nx):
        k = lax.rem(i + d, nx)
        copy = pltpu.make_async_remote_copy(
            src_ref=part_ref.at[k], dst_ref=rs.at[i],
            send_sem=send1.at[d], recv_sem=recv1.at[d],
            device_id=(k, j), device_id_type=MESH,
        )
        copy.start()
        copies.append(copy)
    rs[i] = part_ref[i]
    load.wait()
    half = planes // 2
    lax.fori_loop(0, half, move, 0)
    stores = [pltpu.make_async_copy(moved.at[0:half], base_hbm.at[0:half], store_sem.at[0])]
    stores[0].start()
    for copy in copies:
        copy.wait()
    total = rs[0]
    for k in range(1, nx):
        total = total + rs[k]
    weight = total[24:25, :]
    mean = jnp.where(row < 24, total / jnp.where(weight > 0.0, weight, 1.0), 0.0)
    spread = spread_gain * (at - dot(gram, mean, HIGHEST))
    ag[i] = spread[: ag.shape[1]]
    copies = []
    for d in range(1, nx):
        copy = pltpu.make_async_remote_copy(
            src_ref=ag.at[i], dst_ref=ag.at[i],
            send_sem=send2.at[d], recv_sem=recv2.at[d],
            device_id=(lax.rem(i + d, nx), j), device_id_type=MESH,
        )
        copy.start()
        copies.append(copy)
    lax.fori_loop(half, planes, move, 0)
    stores.append(
        pltpu.make_async_copy(moved.at[half:planes], base_hbm.at[half:planes], store_sem.at[1])
    )
    stores[1].start()
    for copy in copies:
        copy.wait()
    out_ref[...] = ag[...]
    for copy in stores:
        copy.wait()


def update_kernel(
    nx, info, spread_ref, values_ref, wt_hi_hbm, wt_lo_hbm, base_hbm,
    out_hbm, moved, wt_hi, wt_lo, right, num, weights, widen, sem,
):
    planes, tile_x, lanes = moved.shape
    base, count, group, blocks = block_tools(nx, lanes, info)
    load_h = pltpu.make_async_copy(wt_hi_hbm, wt_hi, sem.at[1])
    load_l = pltpu.make_async_copy(wt_lo_hbm, wt_lo, sem.at[2])
    load_s = pltpu.make_async_copy(base_hbm, moved, sem.at[0])
    load_h.start()
    load_l.start()
    load_s.start()

    wide = 3 * lanes
    for g in range(GROUPS):
        widen[g] = jnp.where(
            group_of(iota((lanes, wide), 1), g) == iota((lanes, wide), 0), 1.0, 0.0
        ).astype(BF16)
    num[...] = jnp.zeros(num.shape, F32)
    weights[...] = jnp.zeros(weights.shape, F32)

    yy = (iota((BLOCK, wide), 1) % 16).astype(F32)
    load_h.wait()
    load_l.wait()

    right[...] = jnp.zeros(right.shape, BF16)
    per_device = spread_ref.shape[2] // BLOCK
    pad = jnp.zeros((lanes - FEATURES, BLOCK), F32)

    def widened(b):
        b = jnp.minimum(b, blocks)
        k = b // per_device
        here = pl.ds(pl.multiple_of((b - k * per_device) * BLOCK, BLOCK), BLOCK)
        value = jnp.concatenate(
            [spread_ref[k, :, here], values_ref[k, planes:, here], pad], axis=0
        ).T
        match = yy == value[:, 25:26]
        both = dot(jnp.concatenate(split(value), axis=0), widen[group(b)])
        s_hi = jnp.where(match, both[:BLOCK], 0.0).astype(BF16)
        s_lo = jnp.where(match, both[BLOCK:], 0.0).astype(BF16)
        ones = jnp.where(match[:, :lanes], 1.0, 0.0).astype(BF16)
        return s_hi, s_lo, ones

    def block_update(b, m):
        where = pl.ds(pl.multiple_of(jnp.maximum(b, 0) * BLOCK, BLOCK), BLOCK)
        w_hi, w_lo = wt_hi[:, where], wt_lo[:, where]
        return group(b), dot(jnp.concatenate([w_hi, w_hi, w_lo], axis=1), right[m])

    def two_blocks(n, carry):
        results = [block_update(2 * n - 2 + m, m) for m in range(2)]
        for m, (s_hi, s_lo, ones) in enumerate([widened(2 * n), widened(2 * n + 1)]):
            right[m, 0:BLOCK, :wide] = s_hi
            right[m, BLOCK : 2 * BLOCK, :wide] = s_lo
            right[m, 2 * BLOCK : 3 * BLOCK, :wide] = s_hi
            right[m, 0:BLOCK, wide:] = ones
            right[m, 2 * BLOCK : 3 * BLOCK, wide:] = ones
        for g, added in results:
            num[g] += added[:, :wide]
            weights[g] += added[:, wide:]
        return carry

    lax.fori_loop(0, (blocks + 1) // 2 + 1, two_blocks, 0)

    load_s.wait()
    chunk, parts = 96, 4
    length = tile_x // parts
    stores = []
    for part in range(parts):

        def finish(n, carry):
            here = pl.ds(pl.multiple_of(part * length + n * chunk, chunk), chunk)
            scale = [
                (time_step * nudge_gain) / jnp.maximum(weights[g, here, :], 1.0)
                for g in range(GROUPS)
            ]
            for v in range(3):
                gains = to_levels(
                    [num[g, here, v * lanes : (v + 1) * lanes] * scale[g] for g in range(GROUPS)]
                )
                for z in range(8):
                    moved[v * 8 + z, here, :] += gains[z]
            return carry

        lax.fori_loop(0, length // chunk, finish, 0)
        rows = pl.ds(part * length, length)
        stores.append(
            pltpu.make_async_copy(moved.at[:, rows, :], out_hbm.at[:, rows, :], sem.at[3 + part])
        )
        stores[-1].start()
    for copy in stores:
        copy.wait()


VM = pltpu.MemorySpace.VMEM


def vmem():
    return pl.BlockSpec(memory_space=VM)


def smem():
    return pl.BlockSpec(memory_space=pltpu.MemorySpace.SMEM)


def hbm():
    return pl.BlockSpec(memory_space=pl.ANY)


def gather_scratch(nx, slots, rows, cress_shape, grouped, lanes):
    across, tile_x = cress_shape
    return [
        pltpu.VMEM((across, 8, lanes), F32),
        pltpu.VMEM(grouped, BF16),
        pltpu.VMEM(grouped, BF16),
        pltpu.VMEM((rows + 8, 8, lanes), F32),
        pltpu.VMEM((tile_x, rows), BF16),
        pltpu.VMEM((tile_x, rows), BF16),
        pltpu.VMEM((nx * slots, lanes), F32),
        pltpu.VMEM((GROUPS, 3 * lanes, lanes), BF16),
        pltpu.SemaphoreType.DMA((5 + 2 * (rows // (4 * BLOCK)),)),
    ]


def update_scratch(nx, slots, rows, grouped, planes, lanes):
    tile_x = grouped[1]
    return [
        pltpu.VMEM((planes, tile_x, lanes), F32),
        pltpu.VMEM((tile_x, rows), BF16),
        pltpu.VMEM((tile_x, rows), BF16),
        pltpu.VMEM((2, 3 * BLOCK, 4 * lanes), BF16),
        pltpu.VMEM(grouped, F32),
        pltpu.VMEM((GROUPS, tile_x, lanes), F32),
        pltpu.VMEM((GROUPS, lanes, 3 * lanes), BF16),
        pltpu.SemaphoreType.DMA((7,)),
    ]


def local(nx, ny, model_state, obs_val, obs_owner, obs_x, obs_y, cressman, vertical):
    fields, levels, tile_x, lanes = model_state.shape
    planes = fields * levels
    recs = obs_val.shape[0]
    cap = max(2, 2 * recs // ny)
    slots = ny * cap
    rows = (slots * nx // BLOCK + GROUPS) * BLOCK
    chunk = rows // nx
    state = model_state.reshape(planes, tile_x, lanes)
    vert = vertical.reshape(planes, vertical.shape[2])
    shape = jax.ShapeDtypeStruct
    dma = pltpu.SemaphoreType.DMA
    limit = 56 * 1024 * 1024

    grouped = (GROUPS, tile_x, fields * lanes)
    info, meta, xh, yh, st_hi, st_lo = pl.pallas_call(
        functools.partial(dispatch_kernel, nx, ny),
        out_shape=(
            shape((2 * nx + GROUPS, slots), I32),
            shape((nx, FEATURES, slots), F32),
            shape((2, planes, lanes), F32),
            shape((2 * planes, tile_x), F32),
            shape(grouped, BF16),
            shape(grouped, BF16),
        ),
        in_specs=[vmem()] * 5 + [hbm()],
        out_specs=[vmem()] * 4 + [hbm()] * 2,
        scratch_shapes=[
            pltpu.VMEM((planes, tile_x, lanes), F32),
            pltpu.VMEM(grouped, BF16),
            pltpu.VMEM(grouped, BF16),
            pltpu.VMEM((slots, lanes), F32),
            pltpu.VMEM((slots, lanes), F32),
            pltpu.VMEM((nx, FEATURES, slots), F32),
            pltpu.VMEM((3, nx, slots), F32),
            pltpu.VMEM((2, planes, lanes), F32),
            pltpu.VMEM((2 * planes, tile_x), F32),
            pltpu.VMEM((2, planes, lanes), F32),
            pltpu.VMEM((2, 2 * planes, tile_x), F32),
            dma,
            dma((2,)),
            dma((ny,)),
            dma((ny,)),
            dma((nx,)),
            dma((nx,)),
            dma((4,)),
            dma((4,)),
        ],
        compiler_params=pltpu.CompilerParams(
            collective_id=0, has_side_effects=True, vmem_limit_bytes=limit
        ),
        name="dispatch",
    )(
        obs_val, obs_owner.reshape(1, recs), obs_x.reshape(1, recs), obs_y.reshape(1, recs),
        vert, state,
    )

    part, values, wt_hi, wt_lo = pl.pallas_call(
        functools.partial(gather_kernel, nx),
        out_shape=(
            shape((nx, FEATURES, chunk), F32),
            shape((nx, FEATURES, chunk), F32),
            shape((tile_x, rows), BF16),
            shape((tile_x, rows), BF16),
        ),
        in_specs=[smem(), vmem()] + [hbm()] * 3,
        out_specs=[vmem()] * 2 + [hbm()] * 2,
        scratch_shapes=gather_scratch(nx, slots, rows, cressman.shape, grouped, lanes),
        compiler_params=pltpu.CompilerParams(vmem_limit_bytes=limit),
        name="column_sums",
    )(info, meta, cressman, st_hi, st_lo)

    spread, base = pl.pallas_call(
        functools.partial(reduce_kernel, nx),
        out_shape=(shape((nx, planes, chunk), F32), shape((planes, tile_x, lanes), F32)),
        in_specs=[vmem()] * 4 + [hbm()] * 2,
        out_specs=[vmem(), hbm()],
        scratch_shapes=[
            pltpu.VMEM((planes, tile_x + 16, lanes), F32),
            pltpu.VMEM((planes, tile_x, lanes), F32),
            pltpu.VMEM((nx, FEATURES, chunk), F32),
            pltpu.VMEM((nx, planes, chunk), F32),
            pltpu.VMEM((FEATURES, chunk), F32),
            dma,
            dma,
            dma((2,)),
            dma((nx,)),
            dma((nx,)),
            dma((nx,)),
            dma((nx,)),
        ],
        compiler_params=pltpu.CompilerParams(
            collective_id=1, has_side_effects=True, vmem_limit_bytes=limit
        ),
        name="innovations",
    )(part, vert, xh, yh, values, state)

    out = pl.pallas_call(
        functools.partial(update_kernel, nx),
        out_shape=shape((planes, tile_x, lanes), F32),
        in_specs=[smem()] + [vmem()] * 2 + [hbm()] * 3,
        out_specs=hbm(),
        scratch_shapes=update_scratch(nx, slots, rows, grouped, planes, lanes),
        compiler_params=pltpu.CompilerParams(vmem_limit_bytes=limit),
        name="update",
    )(info, spread, values, wt_hi, wt_lo, base)
    return out.reshape(model_state.shape)


def solution(mesh):
    in_specs = (
        P(None, None, "gx", "gy"),
        P(("gx", "gy"), None),
        P(("gx", "gy"), None),
        P(("gx", "gy")),
        P(("gx", "gy")),
        P(None, "gx"),
        P(),
    )
    out_specs = P(None, None, "gx", "gy")
    return jax.shard_map(
        functools.partial(local, mesh.shape["gx"], mesh.shape["gy"]),
        mesh=mesh, in_specs=in_specs, out_specs=out_specs, check_vma=False,
    )
```

```python
import functools

import jax
import jax.numpy as jnp
from jax import lax
from jax.experimental import pallas as pl
from jax.experimental.pallas import tpu as pltpu
from jax.sharding import PartitionSpec as P

F32 = jnp.float32
BF16 = jnp.bfloat16
I32 = jnp.int32
HIGHEST = lax.Precision.HIGHEST
MESH = pl.DeviceIdType.MESH

advect_coef = 0.5
diffuse_h = 0.2
diffuse_z = 0.1
time_step = 0.5
nudge_gain = 1.0
spread_gain = 0.125

FEATURES = 32
GROUPS = 8
BLOCK = 128
CELLS = 4096
STEP = 32


def iota(shape, dim):
    return lax.broadcasted_iota(I32, shape, dim)


def dot(a, b, precision=None):
    return lax.dot_general(
        a, b, (((1,), (0,)), ((), ())), precision=precision, preferred_element_type=F32
    )


def dot_t(a, b, precision=None):
    return lax.dot_general(
        a, b, (((1,), (1,)), ((), ())), precision=precision, preferred_element_type=F32
    )


def split(value):
    high = value.astype(BF16)
    return high, (value - high.astype(F32)).astype(BF16)


def barrel(parts):
    block = iota(parts[0].shape, 1) // 16
    for bit in (1, 2, 4):
        upper = (block & bit) != 0
        parts = [jnp.where(upper, parts[(c + bit) % 8], parts[c]) for c in range(8)]
    return parts


def to_groups(parts):
    parts = barrel([pltpu.roll(p, 16 * z, 1) if z else p for z, p in enumerate(parts)])
    return [parts[-g % 8] for g in range(8)]


def to_levels(parts):
    parts = barrel(parts)
    return [
        pltpu.roll(parts[-z % 8], 128 - 16 * z, 1) if z else parts[0] for z in range(8)
    ]


def group_of(lane, g):
    return lane // 128 * 8 + (lane // 16 + 8 - g) % 8


def dispatch_kernel(
    nx, ny, obs_ref, owner_ref, x_ref, y_ref, vert_ref, state_hbm,
    info_ref, meta_ref, xh_ref, yh_ref, high_hbm, low_hbm,
    plane, st_hi, st_lo, sb, rb, mb, rows, xe, ye, xr, yr,
    load_sem, store_sem, s1_send, s1_recv, s2_send, s2_recv, h_send, h_recv,
):
    i, j = lax.axis_index("gx"), lax.axis_index("gy")
    planes, tile_x, lanes = plane.shape
    load = pltpu.make_async_copy(state_hbm, plane, load_sem)
    load.start()
    barrier = pltpu.get_barrier_semaphore()
    for d in range(1, ny):
        pl.semaphore_signal(
            barrier, inc=1, device_id=(i, lax.rem(j + d, ny)), device_id_type=MESH
        )
    for d in range(1, nx):
        pl.semaphore_signal(
            barrier, inc=1, device_id=(lax.rem(i + d, nx), j), device_id_type=MESH
        )

    recs = obs_ref.shape[0]
    slots = sb.shape[0]
    cap = slots // ny
    vert = vert_ref[...]
    var = iota((planes, lanes), 0) // 8
    basis = jnp.concatenate([jnp.where(var == v, vert, 0.0) for v in range(3)], axis=1)
    basis = jnp.concatenate([basis, jnp.zeros((lanes - planes, 3 * lanes), F32)], axis=0)
    payload = dot_t(obs_ref[...], basis, HIGHEST)
    eye = iota((recs, recs), 0) == iota((recs, recs), 1)
    x_col = jnp.sum(jnp.where(eye, x_ref[...].astype(F32), 0.0), axis=1, keepdims=True)
    y_col = jnp.sum(jnp.where(eye, y_ref[...].astype(F32), 0.0), axis=1, keepdims=True)
    lane = iota((recs, lanes), 1)
    payload = jnp.where(lane == 24, x_col, payload)
    payload = jnp.where(lane == 25, y_col, payload)
    payload = jnp.where(lane == 26, 1.0, payload)
    owner = jnp.sum(jnp.where(eye, owner_ref[...], 0), axis=1, keepdims=True)
    onehot = jnp.where(owner == lane, 1.0, 0.0)
    earlier = jnp.where(iota((recs, recs), 0) > iota((recs, recs), 1), 1.0, 0.0)
    rank = jnp.sum(dot(earlier, onehot) * onehot, axis=1, keepdims=True)
    slot = owner.astype(F32) * cap + rank
    slot_row = jnp.sum(jnp.where(eye, slot, 0.0), axis=0, keepdims=True).astype(I32)
    place = jnp.where(iota((slots, recs), 0) == slot_row, 1.0, 0.0)
    sb[...] = dot(place, payload, HIGHEST)

    pl.semaphore_wait(barrier, nx + ny - 2)
    first = []
    for d in range(1, ny):
        c = lax.rem(j + d, ny)
        copy = pltpu.make_async_remote_copy(
            src_ref=sb.at[pl.ds(pl.multiple_of(c * cap, cap), cap)],
            dst_ref=rb.at[pl.ds(pl.multiple_of(j * cap, cap), cap)],
            send_sem=s1_send.at[d], recv_sem=s1_recv.at[d],
            device_id=(i, c), device_id_type=MESH,
        )
        copy.start()
        first.append(copy)
    own = pl.ds(pl.multiple_of(j * cap, cap), cap)
    rb[own, :] = sb[own, :]

    load.wait()
    for k in range(planes):
        xe[0, k : k + 1, :] = plane[k, tile_x - 1 : tile_x, :]
        xe[1, k : k + 1, :] = plane[k, 0:1, :]
    edge_lane = iota((tile_x, lanes), 1)

    def gather_edges(k, edges):
        turned = pltpu.roll(plane[k], 2 * k + 1, 1)
        return jnp.where(edge_lane // 2 == k, turned, edges)

    edges = lax.fori_loop(0, planes, gather_edges, jnp.zeros((tile_x, lanes), F32))
    ye[...] = edges.T[: 2 * planes]
    halo = []
    for n, (src, dst, to) in enumerate((
        (xe.at[0], xr.at[0], (lax.rem(i + 1, nx), j)),
        (xe.at[1], xr.at[1], (lax.rem(i + nx - 1, nx), j)),
        (ye, yr.at[0], (i, lax.rem(j + 1, ny))),
        (ye, yr.at[1], (i, lax.rem(j + ny - 1, ny))),
    )):
        copy = pltpu.make_async_remote_copy(
            src_ref=src, dst_ref=dst, send_sem=h_send.at[n], recv_sem=h_recv.at[n],
            device_id=to, device_id_type=MESH,
        )
        copy.start()
        halo.append(copy)

    for copy in first:
        copy.wait()
    got = rb[...]
    got_t = got.T[:FEATURES]
    valid = got[:, 26:27]
    before = jnp.where(iota((slots, slots), 0) > iota((slots, slots), 1), 1.0, 0.0)
    rank = dot(before, jnp.broadcast_to(valid, (slots, lanes)))[:, 0:1]
    place = jnp.where(
        (iota((slots, slots), 1) == rank.astype(I32)) & (valid > 0.5), 1.0, 0.0
    )
    mb[i] = dot(got_t, place, HIGHEST)
    second = []
    for d in range(1, nx):
        copy = pltpu.make_async_remote_copy(
            src_ref=mb.at[i], dst_ref=mb.at[i],
            send_sem=s2_send.at[d], recv_sem=s2_recv.at[d],
            device_id=(lax.rem(i + d, nx), j), device_id_type=MESH,
        )
        copy.start()
        second.append(copy)
    chunk = 96

    def group_chunk(n, carry):
        here = pl.ds(pl.multiple_of(n * chunk, chunk), chunk)
        for v in range(3):
            parts = to_groups([plane[v * 8 + z, here, :] for z in range(8)])
            for g in range(GROUPS):
                high, low = split(parts[g])
                st_hi[g, here, v * lanes : (v + 1) * lanes] = high
                st_lo[g, here, v * lanes : (v + 1) * lanes] = low
        return carry

    lax.fori_loop(0, tile_x // chunk, group_chunk, 0)
    stores = [
        pltpu.make_async_copy(st_hi, high_hbm, store_sem.at[0]),
        pltpu.make_async_copy(st_lo, low_hbm, store_sem.at[1]),
    ]
    for copy in stores:
        copy.start()

    for copy in halo:
        copy.wait()
    xh_ref[0] = jnp.where(i > 0, xr[0], 0.0)
    xh_ref[1] = jnp.where(i < nx - 1, xr[1], 0.0)
    even = iota((2 * planes, tile_x), 0) % 2 == 0
    south = jnp.where(j > 0, yr[0], 0.0)
    north = jnp.where(j < ny - 1, yr[1], 0.0)
    yh_ref[...] = jnp.where(even, south, north)
    for copy in second:
        copy.wait()

    for k in range(nx):
        for f in range(3):
            rows[f, k : k + 1, :] = mb[k, 24 + f : 25 + f, :]
    y_cells = rows[1].astype(I32)
    valid = rows[2] > 0.5
    group = jnp.where(valid, y_cells // (lanes // GROUPS), GROUPS)
    masks = jnp.concatenate(
        [jnp.where(group == g, 1.0, 0.0) for g in range(GROUPS)], axis=0
    )
    lines = GROUPS * nx
    after = jnp.where(iota((slots, slots), 0) < iota((slots, slots), 1), 1.0, 0.0)
    rank = dot(masks, after)
    total = jnp.broadcast_to(jnp.sum(masks, axis=1, keepdims=True), (lines, lanes))
    line, other = iota((lines, lines), 0), iota((lines, lines), 1)
    same = line // nx == other // nx
    offset = dot(jnp.where(same & (other < line), 1.0, 0.0), total, HIGHEST)
    whole = dot(jnp.where(same, 1.0, 0.0), total, HIGHEST)
    count = (whole.astype(I32) + (BLOCK - 1)) // BLOCK
    base = dot(
        jnp.where((other // nx < line // nx) & (other % nx == 0), 1.0, 0.0),
        count.astype(F32),
        HIGHEST,
    )
    placed = masks * (base[:, 0:1] * BLOCK + offset[:, 0:1] + rank)
    pos = placed[0:nx]
    for g in range(1, GROUPS):
        pos = pos + placed[g * nx : (g + 1) * nx]
    dump = (slots * nx // BLOCK + GROUPS) * BLOCK
    info_ref[0:nx, :] = jnp.where(valid, pos.astype(I32), dump) + rows[0].astype(I32) * CELLS
    info_ref[nx : 2 * nx, :] = jnp.broadcast_to(
        jnp.sum(rows[2], axis=1, keepdims=True), (nx, slots)
    ).astype(I32)
    base = base.astype(I32)
    for g in range(GROUPS):
        info_ref[2 * nx + g : 2 * nx + g + 1, 0:lanes] = base[g * nx : g * nx + 1, :]
        info_ref[2 * nx + g : 2 * nx + g + 1, lanes : 2 * lanes] = count[g * nx : g * nx + 1, :]
    meta_ref[...] = mb[...]
    for copy in stores:
        copy.wait()


def block_tools(nx, lanes, info):
    def base(g):
        return info[2 * nx + g, 0]

    def count(g):
        return info[2 * nx + g, lanes]

    def group(b):
        found = 0
        for g in range(1, GROUPS):
            found = found + jnp.where(b >= base(g), 1, 0)
        return found

    return base, count, group, base(GROUPS - 1) + count(GROUPS - 1)


def gather_kernel(
    nx, info, meta_ref, cress_hbm, high_hbm, low_hbm, part_ref, values_ref, wt_hi_hbm, wt_lo_hbm,
    cress, st_hi, st_lo, sorted_w, wt_hi, wt_lo, by_slot, fold, sem,
):
    slots = info.shape[1]
    lanes = cress.shape[2]
    tile_x = cress_hbm.shape[1]
    pieces = tile_x // lanes
    base, count, group, blocks = block_tools(nx, lanes, info)
    loads = [
        pltpu.make_async_copy(
            cress_hbm.at[:, c * lanes : (c + 1) * lanes], cress.at[:, c, :], sem.at[c]
        )
        for c in range(pieces)
    ]
    state_loads = [
        pltpu.make_async_copy(high_hbm, st_hi, sem.at[3]),
        pltpu.make_async_copy(low_hbm, st_lo, sem.at[4]),
    ]
    for copy in loads + state_loads:
        copy.start()
    own_line = iota((8, lanes), 0) == pieces
    y_lane = FEATURES + 25
    blank = jnp.where(own_line & (iota((8, lanes), 1) == y_lane), -1.0, 0.0)

    def clear(b):
        where = pl.ds(pl.multiple_of(b * BLOCK, BLOCK), BLOCK)
        sorted_w[where] = jnp.broadcast_to(blank[None], (BLOCK, 8, lanes))

    for g in range(GROUPS):
        pl.when(count(g) > 0)(functools.partial(clear, base(g) + count(g) - 1))
    clear(blocks)
    part_ref[...] = jnp.zeros(part_ref.shape, F32)
    values_ref[...] = jnp.zeros(values_ref.shape, F32)
    wide = 3 * lanes
    for g in range(GROUPS):
        fold[g] = jnp.where(
            group_of(iota((wide, lanes), 0), g) == iota((wide, lanes), 1), 1.0, 0.0
        ).astype(BF16)
    above = jnp.zeros((FEATURES, slots), F32)
    below = jnp.zeros((lanes - 2 * FEATURES, slots), F32)
    y_row = iota((FEATURES, slots), 0) == 25
    for k in range(nx):
        own = meta_ref[k]
        cell = own - jnp.floor(own * (1.0 / 16.0)) * 16.0
        by_slot[k * slots : (k + 1) * slots, :] = jnp.concatenate(
            [above, jnp.where(y_row, cell, own), below], axis=0
        ).T

    for copy in loads:
        copy.wait()
    for k in range(nx):

        def bring(n, carry):
            start = pl.multiple_of(k * slots + n * STEP, STEP)
            entries = [info[k, n * STEP + m] for m in range(STEP)]
            for m, e in enumerate(entries):
                sorted_w[e & (CELLS - 1)] = jnp.where(
                    own_line,
                    by_slot[pl.ds(start + m, 1), :],
                    cress[lax.shift_right_logical(e, 12)],
                )
            return carry

        lax.fori_loop(0, (info[nx + k, 0] + STEP - 1) // STEP, bring, 0)

    for copy in state_loads:
        copy.wait()
    yy = (iota((BLOCK, wide), 1) % 16).astype(F32)
    lane = iota((BLOCK, lanes), 1)

    def block_sums(b):
        where = pl.ds(pl.multiple_of(b * BLOCK, BLOCK), BLOCK)
        g = group(b)
        parts = [sorted_w[where, c, :] for c in range(pieces)]
        own = sorted_w[where, pieces, :]
        high, low = split(jnp.concatenate(parts, axis=1))
        s_hi, s_lo = st_hi[g], st_lo[g]
        products = dot(
            jnp.concatenate([high, low, high], axis=1), jnp.concatenate([s_hi, s_hi, s_lo], axis=0)
        )
        chosen = split(jnp.where(yy == own[:, y_lane : y_lane + 1], products, 0.0))
        both = dot(jnp.concatenate(chosen, axis=0), fold[g])
        total = jnp.sum(parts[0] + parts[1] + parts[2], axis=1, keepdims=True)
        result = jnp.where(lane == 24, total, both[:BLOCK] + both[BLOCK:])
        result = jnp.where(lane < FEATURES, result, own).T
        return b, where, result, [
            (high[:, c * lanes : (c + 1) * lanes].T, low[:, c * lanes : (c + 1) * lanes].T)
            for c in range(pieces)
        ]

    per_device = part_ref.shape[2] // BLOCK

    def stores(n):
        here = pl.ds(pl.multiple_of(n * 4 * BLOCK, 4 * BLOCK), 4 * BLOCK)
        return [
            pltpu.make_async_copy(wt_hi.at[:, here], wt_hi_hbm.at[:, here], sem.at[5 + 2 * n]),
            pltpu.make_async_copy(wt_lo.at[:, here], wt_lo_hbm.at[:, here], sem.at[6 + 2 * n]),
        ]

    def four_blocks(n, carry):
        for b, where, result, turned in [
            block_sums(jnp.minimum(4 * n + m, blocks)) for m in range(4)
        ]:
            k = b // per_device
            here = pl.ds(pl.multiple_of((b - k * per_device) * BLOCK, BLOCK), BLOCK)
            part_ref[k, :, here] = result[:FEATURES]
            values_ref[k, :, here] = result[FEATURES : 2 * FEATURES]
            for c in range(pieces):
                wt_hi[c * lanes : (c + 1) * lanes, where] = turned[c][0]
                wt_lo[c * lanes : (c + 1) * lanes, where] = turned[c][1]
        for copy in stores(n):
            copy.start()
        return carry

    steps = jnp.maximum((blocks + 3) // 4, 1)
    lax.fori_loop(0, steps, four_blocks, 0)

    def done(n, carry):
        for copy in stores(n):
            copy.wait()
        return carry

    lax.fori_loop(0, steps, done, 0)


def reduce_kernel(
    nx, part_ref, vert_ref, xh_ref, yh_ref, values_hbm, state_hbm, out_ref, base_hbm,
    plane, moved, rs, ag, values, load_sem, own_sem, store_sem, send1, recv1, send2, recv2,
):
    i, j = lax.axis_index("gx"), lax.axis_index("gy")
    planes, padded_x, lanes = plane.shape
    tile_x = padded_x - 16
    load = pltpu.make_async_copy(state_hbm, plane.at[:, 8 : 8 + tile_x, :], load_sem)
    load.start()
    own = pltpu.make_async_copy(values_hbm.at[i], values, own_sem)
    own.start()
    barrier = pltpu.get_barrier_semaphore()
    for d in range(1, nx):
        pl.semaphore_signal(
            barrier, inc=1, device_id=(lax.rem(i + d, nx), j), device_id_type=MESH
        )
    for k in range(planes):
        plane[k, 7:8, :] = xh_ref[0, k : k + 1, :]
        plane[k, 8 + tile_x : 9 + tile_x, :] = xh_ref[1, k : k + 1, :]
    beside = jnp.concatenate(
        [yh_ref[...], jnp.zeros((lanes - 2 * planes, tile_x), F32)], axis=0
    ).T
    beside_high, beside_low = split(beside)
    beside = jnp.where(
        iota((tile_x, lanes), 1) < lanes // 2,
        beside_high.astype(F32),
        pltpu.roll(beside_low.astype(F32), lanes // 2, 1),
    ).astype(BF16)
    near = time_step * diffuse_h
    wind = time_step * 0.5 * advect_coef
    own_part = 1.0 - time_step * (4.0 * diffuse_h + 2.0 * diffuse_z)
    here = pl.ds(8, tile_x)
    source, target = iota((lanes, 2 * lanes), 0), iota((lanes, 2 * lanes), 1)
    turn = (source == target + 1) | ((target >= lanes) & (source == target - lanes - 1))
    turn = jnp.where(turn, 1.0, 0.0).astype(BF16)

    def move(k, carry):
        z = k % 8
        center = plane[k, here, :]
        high, low = split(center)
        fill = ((source % (lanes // 2) == 2 * k + 1) & (target == lanes - 1)) | (
            (source % (lanes // 2) == 2 * k) & (target == lanes)
        )
        fill = jnp.where(fill, 1.0, 0.0).astype(BF16)
        sides = dot(
            jnp.concatenate([high, low, beside], axis=1),
            jnp.concatenate([turn, turn, fill], axis=0),
        )
        wind_u = wind * plane[z, here, :]
        wind_v = wind * plane[8 + z, here, :]
        upper = plane[k + jnp.where(z < 7, 1, 0), here, :]
        lower = plane[k - jnp.where(z > 0, 1, 0), here, :]
        moved[k] = (
            own_part * center
            + (near - wind_u) * plane[k, 9 : 9 + tile_x, :]
            + (near + wind_u) * plane[k, 7 : 7 + tile_x, :]
            + (near - wind_v) * sides[:, :lanes]
            + (near + wind_v) * sides[:, lanes:]
            + (time_step * diffuse_z) * (upper + lower)
        )
        return carry

    vert = jnp.concatenate([vert_ref[...], jnp.zeros((8, lanes), F32)], axis=0)
    same = iota((FEATURES, FEATURES), 0) // 8 == iota((FEATURES, FEATURES), 1) // 8
    gram = jnp.where(same, dot_t(vert, vert, HIGHEST), 0.0)
    own.wait()
    at = values[...]
    row = iota(at.shape, 0)

    pl.semaphore_wait(barrier, nx - 1)
    copies = []
    for d in range(1, nx):
        k = lax.rem(i + d, nx)
        copy = pltpu.make_async_remote_copy(
            src_ref=part_ref.at[k], dst_ref=rs.at[i],
            send_sem=send1.at[d], recv_sem=recv1.at[d],
            device_id=(k, j), device_id_type=MESH,
        )
        copy.start()
        copies.append(copy)
    rs[i] = part_ref[i]
    load.wait()
    half = planes // 2
    lax.fori_loop(0, half, move, 0)
    stores = [pltpu.make_async_copy(moved.at[0:half], base_hbm.at[0:half], store_sem.at[0])]
    stores[0].start()
    for copy in copies:
        copy.wait()
    total = rs[0]
    for k in range(1, nx):
        total = total + rs[k]
    weight = total[24:25, :]
    mean = jnp.where(row < 24, total / jnp.where(weight > 0.0, weight, 1.0), 0.0)
    spread = spread_gain * (at - dot(gram, mean, HIGHEST))
    ag[i] = spread[: ag.shape[1]]
    copies = []
    for d in range(1, nx):
        copy = pltpu.make_async_remote_copy(
            src_ref=ag.at[i], dst_ref=ag.at[i],
            send_sem=send2.at[d], recv_sem=recv2.at[d],
            device_id=(lax.rem(i + d, nx), j), device_id_type=MESH,
        )
        copy.start()
        copies.append(copy)
    lax.fori_loop(half, planes, move, 0)
    stores.append(
        pltpu.make_async_copy(moved.at[half:planes], base_hbm.at[half:planes], store_sem.at[1])
    )
    stores[1].start()
    for copy in copies:
        copy.wait()
    out_ref[...] = ag[...]
    for copy in stores:
        copy.wait()


def update_kernel(
    nx, info, spread_ref, values_ref, wt_hi_hbm, wt_lo_hbm, base_hbm,
    out_hbm, moved, wt_hi, wt_lo, right, num, weights, widen, sem,
):
    planes, tile_x, lanes = moved.shape
    base, count, group, blocks = block_tools(nx, lanes, info)
    load_h = pltpu.make_async_copy(wt_hi_hbm, wt_hi, sem.at[1])
    load_l = pltpu.make_async_copy(wt_lo_hbm, wt_lo, sem.at[2])
    load_s = pltpu.make_async_copy(base_hbm, moved, sem.at[0])
    load_h.start()
    load_l.start()
    load_s.start()

    wide = 3 * lanes
    for g in range(GROUPS):
        widen[g] = jnp.where(
            group_of(iota((lanes, wide), 1), g) == iota((lanes, wide), 0), 1.0, 0.0
        ).astype(BF16)
    num[...] = jnp.zeros(num.shape, F32)
    weights[...] = jnp.zeros(weights.shape, F32)

    yy = (iota((BLOCK, wide), 1) % 16).astype(F32)
    load_h.wait()
    load_l.wait()

    right[...] = jnp.zeros(right.shape, BF16)
    per_device = spread_ref.shape[2] // BLOCK
    pad = jnp.zeros((lanes - FEATURES, BLOCK), F32)

    def widened(b):
        b = jnp.minimum(b, blocks)
        k = b // per_device
        here = pl.ds(pl.multiple_of((b - k * per_device) * BLOCK, BLOCK), BLOCK)
        value = jnp.concatenate(
            [spread_ref[k, :, here], values_ref[k, planes:, here], pad], axis=0
        ).T
        match = yy == value[:, 25:26]
        both = dot(jnp.concatenate(split(value), axis=0), widen[group(b)])
        s_hi = jnp.where(match, both[:BLOCK], 0.0).astype(BF16)
        s_lo = jnp.where(match, both[BLOCK:], 0.0).astype(BF16)
        ones = jnp.where(match[:, :lanes], 1.0, 0.0).astype(BF16)
        return s_hi, s_lo, ones

    def block_update(b, m):
        where = pl.ds(pl.multiple_of(jnp.maximum(b, 0) * BLOCK, BLOCK), BLOCK)
        w_hi, w_lo = wt_hi[:, where], wt_lo[:, where]
        return group(b), dot(jnp.concatenate([w_hi, w_hi, w_lo], axis=1), right[m])

    def two_blocks(n, carry):
        results = [block_update(2 * n - 2 + m, m) for m in range(2)]
        for m, (s_hi, s_lo, ones) in enumerate([widened(2 * n), widened(2 * n + 1)]):
            right[m, 0:BLOCK, :wide] = s_hi
            right[m, BLOCK : 2 * BLOCK, :wide] = s_lo
            right[m, 2 * BLOCK : 3 * BLOCK, :wide] = s_hi
            right[m, 0:BLOCK, wide:] = ones
            right[m, 2 * BLOCK : 3 * BLOCK, wide:] = ones
        for g, added in results:
            num[g] += added[:, :wide]
            weights[g] += added[:, wide:]
        return carry

    lax.fori_loop(0, (blocks + 1) // 2 + 1, two_blocks, 0)

    load_s.wait()
    chunk, parts = 96, 4
    length = tile_x // parts
    stores = []
    for part in range(parts):

        def finish(n, carry):
            here = pl.ds(pl.multiple_of(part * length + n * chunk, chunk), chunk)
            scale = [
                (time_step * nudge_gain) / jnp.maximum(weights[g, here, :], 1.0)
                for g in range(GROUPS)
            ]
            for v in range(3):
                gains = to_levels(
                    [num[g, here, v * lanes : (v + 1) * lanes] * scale[g] for g in range(GROUPS)]
                )
                for z in range(8):
                    moved[v * 8 + z, here, :] += gains[z]
            return carry

        lax.fori_loop(0, length // chunk, finish, 0)
        rows = pl.ds(part * length, length)
        stores.append(
            pltpu.make_async_copy(moved.at[:, rows, :], out_hbm.at[:, rows, :], sem.at[3 + part])
        )
        stores[-1].start()
    for copy in stores:
        copy.wait()


VM = pltpu.MemorySpace.VMEM


def vmem():
    return pl.BlockSpec(memory_space=VM)


def smem():
    return pl.BlockSpec(memory_space=pltpu.MemorySpace.SMEM)


def hbm():
    return pl.BlockSpec(memory_space=pl.ANY)


def gather_scratch(nx, slots, rows, cress_shape, grouped, lanes):
    across, tile_x = cress_shape
    return [
        pltpu.VMEM((across, 8, lanes), F32),
        pltpu.VMEM(grouped, BF16),
        pltpu.VMEM(grouped, BF16),
        pltpu.VMEM((rows + 8, 8, lanes), F32),
        pltpu.VMEM((tile_x, rows), BF16),
        pltpu.VMEM((tile_x, rows), BF16),
        pltpu.VMEM((nx * slots, lanes), F32),
        pltpu.VMEM((GROUPS, 3 * lanes, lanes), BF16),
        pltpu.SemaphoreType.DMA((5 + 2 * (rows // (4 * BLOCK)),)),
    ]


def update_scratch(nx, slots, rows, grouped, planes, lanes):
    tile_x = grouped[1]
    return [
        pltpu.VMEM((planes, tile_x, lanes), F32),
        pltpu.VMEM((tile_x, rows), BF16),
        pltpu.VMEM((tile_x, rows), BF16),
        pltpu.VMEM((2, 3 * BLOCK, 4 * lanes), BF16),
        pltpu.VMEM(grouped, F32),
        pltpu.VMEM((GROUPS, tile_x, lanes), F32),
        pltpu.VMEM((GROUPS, lanes, 3 * lanes), BF16),
        pltpu.SemaphoreType.DMA((7,)),
    ]


def local(nx, ny, model_state, obs_val, obs_owner, obs_x, obs_y, cressman, vertical):
    fields, levels, tile_x, lanes = model_state.shape
    planes = fields * levels
    recs = obs_val.shape[0]
    cap = max(2, 2 * recs // ny)
    slots = ny * cap
    rows = (slots * nx // BLOCK + GROUPS) * BLOCK
    chunk = rows // nx
    state = model_state.reshape(planes, tile_x, lanes)
    vert = vertical.reshape(planes, vertical.shape[2])
    shape = jax.ShapeDtypeStruct
    dma = pltpu.SemaphoreType.DMA
    limit = 56 * 1024 * 1024

    grouped = (GROUPS, tile_x, fields * lanes)
    info, meta, xh, yh, st_hi, st_lo = pl.pallas_call(
        functools.partial(dispatch_kernel, nx, ny),
        out_shape=(
            shape((2 * nx + GROUPS, slots), I32),
            shape((nx, FEATURES, slots), F32),
            shape((2, planes, lanes), F32),
            shape((2 * planes, tile_x), F32),
            shape(grouped, BF16),
            shape(grouped, BF16),
        ),
        in_specs=[vmem()] * 5 + [hbm()],
        out_specs=[vmem()] * 4 + [hbm()] * 2,
        scratch_shapes=[
            pltpu.VMEM((planes, tile_x, lanes), F32),
            pltpu.VMEM(grouped, BF16),
            pltpu.VMEM(grouped, BF16),
            pltpu.VMEM((slots, lanes), F32),
            pltpu.VMEM((slots, lanes), F32),
            pltpu.VMEM((nx, FEATURES, slots), F32),
            pltpu.VMEM((3, nx, slots), F32),
            pltpu.VMEM((2, planes, lanes), F32),
            pltpu.VMEM((2 * planes, tile_x), F32),
            pltpu.VMEM((2, planes, lanes), F32),
            pltpu.VMEM((2, 2 * planes, tile_x), F32),
            dma,
            dma((2,)),
            dma((ny,)),
            dma((ny,)),
            dma((nx,)),
            dma((nx,)),
            dma((4,)),
            dma((4,)),
        ],
        compiler_params=pltpu.CompilerParams(
            collective_id=0, has_side_effects=True, vmem_limit_bytes=limit
        ),
        name="dispatch",
    )(
        obs_val, obs_owner.reshape(1, recs), obs_x.reshape(1, recs), obs_y.reshape(1, recs),
        vert, state,
    )

    part, values, wt_hi, wt_lo = pl.pallas_call(
        functools.partial(gather_kernel, nx),
        out_shape=(
            shape((nx, FEATURES, chunk), F32),
            shape((nx, FEATURES, chunk), F32),
            shape((tile_x, rows), BF16),
            shape((tile_x, rows), BF16),
        ),
        in_specs=[smem(), vmem()] + [hbm()] * 3,
        out_specs=[vmem()] * 2 + [hbm()] * 2,
        scratch_shapes=gather_scratch(nx, slots, rows, cressman.shape, grouped, lanes),
        compiler_params=pltpu.CompilerParams(vmem_limit_bytes=limit),
        name="column_sums",
    )(info, meta, cressman, st_hi, st_lo)

    spread, base = pl.pallas_call(
        functools.partial(reduce_kernel, nx),
        out_shape=(shape((nx, planes, chunk), F32), shape((planes, tile_x, lanes), F32)),
        in_specs=[vmem()] * 4 + [hbm()] * 2,
        out_specs=[vmem(), hbm()],
        scratch_shapes=[
            pltpu.VMEM((planes, tile_x + 16, lanes), F32),
            pltpu.VMEM((planes, tile_x, lanes), F32),
            pltpu.VMEM((nx, FEATURES, chunk), F32),
            pltpu.VMEM((nx, planes, chunk), F32),
            pltpu.VMEM((FEATURES, chunk), F32),
            dma,
            dma,
            dma((2,)),
            dma((nx,)),
            dma((nx,)),
            dma((nx,)),
            dma((nx,)),
        ],
        compiler_params=pltpu.CompilerParams(
            collective_id=1, has_side_effects=True, vmem_limit_bytes=limit
        ),
        name="innovations",
    )(part, vert, xh, yh, values, state)

    out = pl.pallas_call(
        functools.partial(update_kernel, nx),
        out_shape=shape((planes, tile_x, lanes), F32),
        in_specs=[smem()] + [vmem()] * 2 + [hbm()] * 3,
        out_specs=hbm(),
        scratch_shapes=update_scratch(nx, slots, rows, grouped, planes, lanes),
        compiler_params=pltpu.CompilerParams(vmem_limit_bytes=limit),
        name="update",
    )(info, spread, values, wt_hi, wt_lo, base)
    return out.reshape(model_state.shape)


def solution(mesh):
    in_specs = (
        P(None, None, "gx", "gy"),
        P(("gx", "gy"), None),
        P(("gx", "gy"), None),
        P(("gx", "gy")),
        P(("gx", "gy")),
        P(None, "gx"),
        P(),
    )
    out_specs = P(None, None, "gx", "gy")
    return jax.shard_map(
        functools.partial(local, mesh.shape["gx"], mesh.shape["gy"]),
        mesh=mesh, in_specs=in_specs, out_specs=out_specs, check_vma=False,
    )
```
